32 devices in a mesh: dp: 4 (over z), row: 4 (over y, x), col: 2 (over core).
Axes of the slice: x: 2, y: 2, z: 4, core: 2. Of those that a mesh axis runs over, the one named last changes fastest.
Arguments:
- tokens: bfloat16 [16, 2048, 768], P(('dp', 'row'), 'col'), may hold values from -6 to 6
- timesteps: int32 [16], P(('dp', 'row')), may hold values from 0 to 999
- block_ids: int32 [16, 2048], P(('dp', 'row')), may hold values from 0 to 11, never falling along the last dimension, each value on 1 to 256 neighbouring positions
- table: float32 [1000, 768], replicated, may hold values from -3 to 3
- gain_one: float32 [768], replicated, may hold values from 0.5 to 1.5
- bias_one: float32 [768], replicated, may hold values from -1.75 to 1.75
- w_query: float32 [768, 768], P('row', 'col'), may hold values from -0.21875 to 0.21875
- w_key: float32 [768, 768], P('row', 'col'), may hold values from -0.21875 to 0.21875
- w_value: float32 [768, 768], P('row', 'col'), may hold values from -0.21875 to 0.21875
- b_query: float32 [768], P('col'), may hold values from -1.75 to 1.75
- b_value: float32 [768], P('col'), may hold values from -1.75 to 1.75
- w_out: float32 [768, 768], P('col', 'row'), may hold values from -3.5 to 3.5
- b_out: float32 [768], replicated, may hold values from -1.75 to 1.75
- gain_two: float32 [768], replicated, may hold values from 0.5 to 1.5
- bias_two: float32 [768], replicated, may hold values from -1.75 to 1.75
- w_up: float32 [768, 3072], P('row', 'col'), may hold values from -0.21875 to 0.21875
- b_up: float32 [3072], P('col'), may hold values from -1.75 to 1.75
- w_down: float32 [3072, 768], P('col', 'row'), may hold values from -0.109375 to 0.109375
- b_down: float32 [768], replicated, may hold values from -1.75 to 1.75
- cotangent: bfloat16 [16, 2048, 768], P(('dp', 'row'), 'col'), may hold values from -6 to 6
Outputs:
- layer_out: bfloat16 [16, 2048, 768], P(('dp', 'row'), 'col')
- grad_tokens: float32 [16, 2048, 768], P(('dp', 'row'), 'col')
- grad_table: float32 [1000, 768], replicated
- grad_gain_one: float32 [768], replicated
- grad_bias_one: float32 [768], replicated
- grad_w_query: float32 [768, 768], P('row', 'col')
- grad_w_key: float32 [768, 768], P('row', 'col')
- grad_w_value: float32 [768, 768], P('row', 'col')
- grad_b_query: float32 [768], P('col')
- grad_b_value: float32 [768], P('col')
- grad_w_out: float32 [768, 768], P('col', 'row')
- grad_b_out: float32 [768], replicated
- grad_gain_two: float32 [768], replicated
- grad_bias_two: float32 [768], replicated
- grad_w_up: float32 [768, 3072], P('row', 'col')
- grad_b_up: float32 [3072], P('col')
- grad_w_down: float32 [3072, 768], P('col', 'row')
- grad_b_down: float32 [768], replicated
The draws below stay inside these ranges and needn't reach their ends.
Inputs may be any that keep to these rules, and one draw needn't show every extreme that they name: `block_ids`: block numbers never fall along a sequence; every block number of a sequence is used, each block holds 1 to 256 positions, and some block holds exactly 256.
All inputs are finite; a program needn't handle non-finite values.
Results may differ from the reference program's by a relative error of at most 0.012.
The reference program's roundings to bfloat16 on the way count: a program that leaves them out, or rounds other values in their place, can miss the bound.
Values may be sent and summed in bfloat16 or wider, within the bound.
No kernel may reach another device: no remote copies, remote signals or barrier semaphores. Data moves between devices by JAX's collectives and lax.ppermute only.
A program may use at most 256 MiB of HBM per device.

```python
import math
import jax
import jax.numpy as jnp
import numpy as np
from jax import lax

D = 768
HEADS = 12
HEAD_DIM = 64
FF = 3072
STEPS = 1000
LEN = 2048
BLOCK = 256
NSEQ = 16
NBLK = 12


def place_ends(entries, key, smallest, top_value):
    longest = entries.shape.index(max(entries.shape))
    spots = []
    for shift in (0, 1):
        where = [jax.random.randint(jax.random.fold_in(key, axis), (), 0, length) for axis, length in enumerate(entries.shape)]
        where[longest] = (where[longest] + shift) % entries.shape[longest]
        spots.append(tuple(where))
    return entries.at[spots[0]].set(smallest).at[spots[1]].set(top_value)


def levels(rng, dims, shards, smallest, largest):
    def one(dim, blocks):
        draws = jax.random.uniform(jax.random.fold_in(jax.random.fold_in(rng, 6), dim), (blocks,), jnp.float32, smallest / len(shards), largest / len(shards))
        return jnp.repeat(jnp.exp(draws), dims[dim] // blocks).reshape((-1,) + (1,) * (len(dims) - dim - 1))

    factor_of = one(*shards[0])
    for cut in shards[1:]:
        factor_of = factor_of * one(*cut)
    return factor_of


def split_up(count, total, reach, skew):
    loads = [(1 << 20) // math.isqrt(rank ** skew) + 1 for rank in range(2, count + 1)]
    surplus, holding = total - reach - (count - 1), [1] * (count - 1)
    while surplus > 0:
        free = [i for i in range(count - 1) if holding[i] < reach]
        pool, left = sum([loads[i] for i in free]), surplus
        for i in free:
            more = min(reach - holding[i], max(1, left * loads[i] // pool), surplus)
            holding[i] = holding[i] + more
            surplus = surplus - more
    return np.array([reach] + holding)


def ragged_sizes(key, number_of, total, reach, skew):
    if number_of == 2:
        one = jax.random.randint(key, (), max(1, total - reach), min(reach, total - 1) + 1)
        return jnp.stack([one, total - one])
    lengths = jnp.asarray(split_up(number_of, total, reach, skew), jnp.int32)
    couples = (number_of - 1) // 2
    source_of, taker = lengths[1:1 + 2 * couples:2], lengths[2:2 + 2 * couples:2]
    slack = jnp.minimum(source_of - 1, reach - taker)
    moved = jax.random.randint(jax.random.fold_in(key, 1), (couples,), 0, 1 << 20) % (slack + 1)
    lengths = lengths.at[1:1 + 2 * couples:2].set(source_of - moved).at[2:2 + 2 * couples:2].set(taker + moved)
    return lengths[jax.random.permutation(jax.random.fold_in(key, 2), number_of)]


def gaussian(rng, shape, deviation, most, cuts=(), held_as=jnp.bfloat16):
    level = levels(rng, shape, cuts, -0.22, 0.18) if cuts else 1.0
    array = jax.random.normal(rng, shape, jnp.float32) * deviation * level
    return jnp.minimum(jnp.maximum(array, -most), most).astype(held_as)


def setup_inputs(seed: int = 0) -> dict:
    arg_keys = jax.random.split(jax.random.key(seed), 21)
    return {
        "tokens": gaussian(arg_keys[0], (NSEQ, LEN, D), 1.0, 6.0, ((0, 16), (1, 2))),
        "timesteps": place_ends(jax.random.randint(arg_keys[1], (NSEQ,), 0, STEPS), jax.random.fold_in(arg_keys[1], 1), 0, STEPS - 1).astype(jnp.int32),
        "block_ids": jax.vmap(lambda own: jnp.searchsorted(jnp.cumsum(ragged_sizes(own, NBLK, LEN, BLOCK, 0)), jnp.arange(LEN), side="right"))(jax.random.split(arg_keys[2], NSEQ)).reshape((NSEQ, LEN)).astype(jnp.int32),
        "table": gaussian(arg_keys[3], (STEPS, D), 0.5, 3.0, (), jnp.float32),
        "gain_one": jnp.clip(1.0 + 0.1 * jax.random.normal(arg_keys[4], (D,), jnp.float32), 0.5, 1.5),
        "bias_one": gaussian(arg_keys[5], (D,), 0.3, 1.75, (), jnp.float32),
        "w_query": gaussian(arg_keys[6], (D, D), D ** -0.5, 0.21875, ((0, 4), (1, 2)), jnp.float32),
        "w_key": gaussian(arg_keys[7], (D, D), D ** -0.5, 0.21875, ((0, 4), (1, 2)), jnp.float32),
        "w_value": gaussian(arg_keys[8], (D, D), D ** -0.5, 0.21875, ((0, 4), (1, 2)), jnp.float32),
        "b_query": gaussian(arg_keys[9], (D,), 0.3, 1.75, ((0, 2),), jnp.float32),
        "b_value": gaussian(arg_keys[10], (D,), 0.3, 1.75, ((0, 2),), jnp.float32),
        "w_out": gaussian(arg_keys[11], (D, D), (max(D // 256, 1)) ** -0.5, 3.5, ((0, 2), (1, 4)), jnp.float32),
        "b_out": gaussian(arg_keys[12], (D,), 0.3, 1.75, (), jnp.float32),
        "gain_two": jnp.clip(1.0 + 0.1 * jax.random.normal(arg_keys[13], (D,), jnp.float32), 0.5, 1.5),
        "bias_two": gaussian(arg_keys[14], (D,), 0.3, 1.75, (), jnp.float32),
        "w_up": gaussian(arg_keys[15], (D, FF), D ** -0.5, 0.21875, ((0, 4), (1, 2)), jnp.float32),
        "b_up": gaussian(arg_keys[16], (FF,), 0.3, 1.75, ((0, 2),), jnp.float32),
        "w_down": gaussian(arg_keys[17], (FF, D), FF ** -0.5, 0.109375, ((0, 2), (1, 4)), jnp.float32),
        "b_down": gaussian(arg_keys[18], (D,), 0.3, 1.75, (), jnp.float32),
        "cotangent": gaussian(arg_keys[19], (NSEQ, LEN, D), 1.0, 6.0, ((0, 16), (1, 2))),
    }


@jax.custom_vjp
def low(v):
    return lax.optimization_barrier(v.astype(jnp.bfloat16)).astype(jnp.float32)

@jax.custom_vjp
def low_back(v):
    return v

def low_keep(v):
    return (low(v), None)

def low_pass(kept, grad):
    return (grad,)

def back_keep(v):
    return (v, None)

def back_low(kept, grad):
    return (low(grad),)
low.defvjp(low_keep, low_pass)
low_back.defvjp(back_keep, back_low)

def layer_norm(values, gain, bias):
    mean = lax.optimization_barrier(jnp.mean(values, axis=-1, keepdims=True))
    centred = values - mean
    spread = lax.optimization_barrier(jnp.mean(centred * centred, axis=-1, keepdims=True))
    return centred * lax.rsqrt(spread + 1e-05) * gain + bias

def matmul(left, right):
    return jnp.dot(left, right, precision=lax.Precision.HIGHEST, preferred_element_type=jnp.float32)

def sequence_forward(params, tokens, timestep, blocks):
    table, gain_one, bias_one, w_query, w_key, w_value, b_query, b_value, w_out, b_out, gain_two, bias_two, w_up, b_up, w_down, b_down = params
    start = tokens + lax.dynamic_index_in_dim(table, timestep, 0, keepdims=False)
    normed_one = low(layer_norm(start, gain_one, bias_one))
    query = low(low_back(matmul(normed_one, low(w_query)) + b_query))
    key = low(low_back(matmul(normed_one, low(w_key))))
    value = low(low_back(matmul(normed_one, low(w_value)) + b_value))
    row_block = min(512, LEN)
    block_count = LEN // row_block
    key_heads = key.reshape(LEN, HEADS, HEAD_DIM)
    value_heads = value.reshape(LEN, HEADS, HEAD_DIM)

    def attend(pieces):
        query_part, query_ids = pieces
        scores = jnp.einsum('qhd,khd->hqk', query_part, key_heads, precision=lax.Precision.HIGHEST) * HEAD_DIM ** (-0.5)
        allowed = blocks[None, None, :] <= query_ids[None, :, None]
        scores = low_back(jnp.where(allowed, scores, -1000000000.0))
        probs = jax.nn.softmax(scores, axis=-1)
        return jnp.einsum('hqk,khd->qhd', low(probs), value_heads, precision=lax.Precision.HIGHEST)
    attended = lax.map(jax.checkpoint(attend), (query.reshape(block_count, row_block, HEADS, HEAD_DIM), blocks.reshape(block_count, row_block)))
    attended = low(low_back(attended.reshape(LEN, D)))
    branch = low_back(matmul(attended, low(w_out)) + b_out)
    middle = start + branch
    normed_two = low(layer_norm(middle, gain_two, bias_two))
    hidden_pre = low_back(matmul(normed_two, low(w_up)) + b_up)
    hidden = low(jax.nn.gelu(hidden_pre, approximate=False))
    mixer = low_back(matmul(hidden, low(w_down)) + b_down)
    return middle + mixer

def reference(tokens, timesteps, block_ids, table, gain_one, bias_one, w_query, w_key, w_value, b_query, b_value, w_out, b_out, gain_two, bias_two, w_up, b_up, w_down, b_down, cotangent):
    params = (table, gain_one, bias_one, w_query, w_key, w_value, b_query, b_value, w_out, b_out, gain_two, bias_two, w_up, b_up, w_down, b_down)

    def one_sequence(totals, pieces):
        seq_tokens, step_now, blocks, seq_cot = pieces

        def forward(param_set, inputs):
            return sequence_forward(param_set, inputs, step_now, blocks)
        output, pullback = jax.vjp(forward, params, seq_tokens.astype(jnp.float32))
        param_grads, token_grad = pullback(seq_cot.astype(jnp.float32))
        totals = jax.tree.map(jnp.add, totals, param_grads)
        return (totals, (output.astype(jnp.bfloat16), token_grad))
    zeros = jax.tree.map(jnp.zeros_like, params)
    totals, (outputs, token_grads) = lax.scan(one_sequence, zeros, (tokens, timesteps, block_ids, cotangent))
    return (outputs, token_grads, totals[0], totals[1], totals[2], totals[3], totals[4], totals[5], totals[6], totals[7], totals[8], totals[9], totals[10], totals[11], totals[12], totals[13], totals[14], totals[15])
```

```python
import functools

import jax
import jax.numpy as jnp
from jax import lax
from jax.experimental import pallas as pl
from jax.experimental.pallas import tpu as pltpu
from jax.sharding import PartitionSpec as P

HEAD_DIM = 64
norm_eps = 1e-05
masked_score = -1000000000.0
low = jnp.bfloat16
wide = jnp.float32
tile_rows = 256


def dot_nn(left, right):
    return lax.dot_general(left, right, (((1,), (0,)), ((), ())), preferred_element_type=wide)


def dot_nt(left, right):
    return lax.dot_general(left, right, (((1,), (1,)), ((), ())), preferred_element_type=wide)


def dot_tn(left, right):
    return lax.dot_general(left, right, (((0,), (0,)), ((), ())), preferred_element_type=wide)


def fold_lanes(values, op):
    folded = values[:, :128]
    for start in range(128, values.shape[1], 128):
        folded = op(folded, values[:, start : start + 128])
    return folded


def column_of(ids_row):
    parts = []
    for start in range(0, ids_row.shape[1], 128):
        piece = ids_row[:, start : start + 128].astype(wide)
        parts.append(jnp.transpose(jnp.broadcast_to(piece, (128, 128))))
    return jnp.concatenate(parts, axis=0)


def allowed_mask(ids_ref, ids_column, start, size):
    parts = []
    for lane in range(start, start + size, 128):
        parts.append(ids_ref[:, lane : lane + 128].astype(wide) <= ids_column)
    return jnp.concatenate(parts, axis=1)


def attend_forward_body(count, half, col_ref, q_ref, k_ref, v_ref, ids_ref, o_ref, lse_ref, s_ref):
    step = pl.program_id(1)
    side = col_ref[0]
    size = tile_rows
    lane = lax.broadcasted_iota(jnp.int32, (size, 128), 1)

    def key_tile(ref, j):
        return ref[(j // half) ^ side, (j % half) * size : (j % half + 1) * size, :]

    def variant(c):
        keys = min(c + 2, count)
        query = q_ref[...]
        ids_column = column_of(ids_ref[:, c * size : (c + 1) * size])
        out = None
        for head in range(2):
            mine = (lane < HEAD_DIM) if head == 0 else (lane >= HEAD_DIM)
            part = jnp.where(mine, query, jnp.zeros_like(query)) * jnp.asarray(0.125, low)
            top = None
            for j in range(keys):
                scores = dot_nt(part, key_tile(k_ref, j))
                if j >= c:
                    mask = allowed_mask(ids_ref, ids_column, j * size, size)
                    scores = jnp.where(mask, scores, masked_score)
                s_ref[head, :, j * size : (j + 1) * size] = scores
                peak = fold_lanes(scores, jnp.maximum)
                top = peak if top is None else jnp.maximum(top, peak)
            top = jnp.max(top, axis=1, keepdims=True)
            total = None
            acc = None
            for j in range(keys):
                expo = jnp.exp(s_ref[head, :, j * size : (j + 1) * size] - top)
                part_sum = fold_lanes(expo, jnp.add)
                total = part_sum if total is None else total + part_sum
                mixed = dot_nn(expo.astype(low), key_tile(v_ref, j))
                acc = mixed if acc is None else acc + mixed
            total = jnp.sum(total, axis=1, keepdims=True)
            mixed = acc / total
            out = mixed if head == 0 else jnp.where(mine, mixed, out)
            lse_ref[:, head : head + 1] = top + jnp.log(total)
        o_ref[...] = out.astype(low)

    for c in range(count):
        pl.when(step == c)(functools.partial(variant, c))


def attend_forward(side, qkv, ids, head_cols):
    sides, rows, _ = qkv.shape
    length = sides * rows
    count = length // tile_rows
    half = rows // tile_rows
    pairs = head_cols // 128

    def row_map(h, i, c):
        return ((i // half) ^ c[0], i % half, h)

    return pl.pallas_call(
        functools.partial(attend_forward_body, count, half),
        grid_spec=pltpu.PrefetchScalarGridSpec(
            num_scalar_prefetch=1,
            grid=(pairs, count),
            in_specs=[
                pl.BlockSpec((None, tile_rows, 128), row_map),
                pl.BlockSpec((sides, rows, 128), lambda h, i, c: (0, 0, pairs + h)),
                pl.BlockSpec((sides, rows, 128), lambda h, i, c: (0, 0, 2 * pairs + h)),
                pl.BlockSpec((1, length), lambda h, i, c: (0, 0)),
            ],
            out_specs=[
                pl.BlockSpec((None, tile_rows, 128), row_map),
                pl.BlockSpec((None, tile_rows, 2), lambda h, i, c: (h, i, 0)),
            ],
            scratch_shapes=[pltpu.VMEM((2, tile_rows, length), wide)],
        ),
        out_shape=[
            jax.ShapeDtypeStruct((sides, rows, head_cols), low),
            jax.ShapeDtypeStruct((pairs, length, 2), wide),
        ],
        name="attend_forward",
    )(side, qkv, qkv, qkv, ids)


def attend_backward_body(
    count, half, col_ref, q_ref, k_ref, v_ref, g_ref, ids_ref, lse_ref,
    gq_ref, gk_ref, gv_ref, p_ref, gp_ref, gk_acc, gv_acc,
):
    step = pl.program_id(1)
    side = col_ref[0]
    size = tile_rows
    lane = lax.broadcasted_iota(jnp.int32, (size, 128), 1)

    def key_tile(ref, j):
        return ref[(j // half) ^ side, (j % half) * size : (j % half + 1) * size, :]

    @pl.when(step == 0)
    def _():
        gk_acc[...] = jnp.zeros_like(gk_acc)
        gv_acc[...] = jnp.zeros_like(gv_acc)

    def variant(c):
        keys = min(c + 2, count)
        query = q_ref[...]
        grad = g_ref[...]
        query_turned = jnp.transpose(query.astype(wide)).astype(low)
        grad_turned = jnp.transpose(grad.astype(wide)).astype(low)
        ids_column = column_of(ids_ref[:, c * size : (c + 1) * size])
        out = None
        for head in range(2):
            mine = (lane < HEAD_DIM) if head == 0 else (lane >= HEAD_DIM)
            spot = slice(head * HEAD_DIM, (head + 1) * HEAD_DIM)
            part = jnp.where(mine, query, jnp.zeros_like(query)) * jnp.asarray(0.125, low)
            grad_part = jnp.where(mine, grad, jnp.zeros_like(grad))
            log_sum = lse_ref[:, head : head + 1]
            inner = None
            for j in range(keys):
                here = slice(j * size, (j + 1) * size)
                scores = dot_nt(part, key_tile(k_ref, j))
                grad_probs = dot_nt(grad_part, key_tile(v_ref, j))
                probs = jnp.exp(scores - log_sum)
                if j >= c:
                    mask = allowed_mask(ids_ref, ids_column, j * size, size)
                    probs = jnp.where(mask, probs, 0.0)
                p_ref[head, :, here] = probs
                gp_ref[head, :, here] = grad_probs
                piece = fold_lanes(probs * grad_probs, jnp.add)
                inner = piece if inner is None else inner + piece
                gv_acc[spot, here] += dot_nn(grad_turned[spot, :], probs.astype(low))
            inner = jnp.sum(inner, axis=1, keepdims=True)
            grad_query = None
            for j in range(keys):
                here = slice(j * size, (j + 1) * size)
                grad_scores = (p_ref[head, :, here] * (gp_ref[head, :, here] - inner)).astype(low)
                piece = dot_nn(grad_scores, key_tile(k_ref, j))
                grad_query = piece if grad_query is None else grad_query + piece
                gk_acc[spot, here] += dot_nn(query_turned[spot, :], grad_scores)
            out = grad_query if head == 0 else jnp.where(mine, grad_query, out)
        gq_ref[...] = (out * 0.125).astype(low)

    for c in range(count):
        pl.when(step == c)(functools.partial(variant, c))

    @pl.when(step == count - 1)
    def _():
        for j in range(count):
            here = slice(j * size, (j + 1) * size)
            rows = slice((j % half) * size, (j % half + 1) * size)
            gk_ref[(j // half) ^ side, rows, :] = jnp.transpose(gk_acc[:, here] * 0.125).astype(low)
            gv_ref[(j // half) ^ side, rows, :] = jnp.transpose(gv_acc[:, here]).astype(low)


def attend_backward(side, qkv, grad, ids, log_sums, head_cols):
    sides, rows, _ = qkv.shape
    length = sides * rows
    count = length // tile_rows
    half = rows // tile_rows
    pairs = head_cols // 128

    def row_map(h, i, c):
        return ((i // half) ^ c[0], i % half, h)

    row_spec = pl.BlockSpec((None, tile_rows, 128), row_map)
    whole = pl.BlockSpec((sides, rows, 128), lambda h, i, c: (0, 0, h))
    return pl.pallas_call(
        functools.partial(attend_backward_body, count, half),
        grid_spec=pltpu.PrefetchScalarGridSpec(
            num_scalar_prefetch=1,
            grid=(pairs, count),
            in_specs=[
                row_spec,
                pl.BlockSpec((sides, rows, 128), lambda h, i, c: (0, 0, pairs + h)),
                pl.BlockSpec((sides, rows, 128), lambda h, i, c: (0, 0, 2 * pairs + h)),
                row_spec,
                pl.BlockSpec((1, length), lambda h, i, c: (0, 0)),
                pl.BlockSpec((None, tile_rows, 2), lambda h, i, c: (h, i, 0)),
            ],
            out_specs=[row_spec, whole, whole],
            scratch_shapes=[
                pltpu.VMEM((2, tile_rows, length), wide),
                pltpu.VMEM((2, tile_rows, length), wide),
                pltpu.VMEM((128, length), wide),
                pltpu.VMEM((128, length), wide),
            ],
        ),
        out_shape=[jax.ShapeDtypeStruct((sides, rows, head_cols), low)] * 3,
        name="attend_backward",
    )(side, qkv, qkv, qkv, grad, ids, log_sums)


def layer_norm_parts(values, gain, bias):
    mean = jnp.mean(values, axis=-1, keepdims=True)
    centred = values - mean
    inverse = lax.rsqrt(jnp.mean(centred * centred, axis=-1, keepdims=True) + norm_eps)
    unit = centred * inverse
    return (unit * gain + bias, unit, inverse)


def norm_back(grad_normed, unit, inverse, gain):
    grad_unit = grad_normed * gain
    first_mean = jnp.mean(grad_unit, axis=-1, keepdims=True)
    second_mean = jnp.mean(grad_unit * unit, axis=-1, keepdims=True)
    return inverse * (grad_unit - first_mean - unit * second_mean)


def gelu_exact(values):
    return jax.nn.gelu(values, approximate=False)


def swap(values, axis, distance):
    size = lax.axis_size(axis)
    return lax.ppermute(values, axis, [(i, i ^ distance) for i in range(size)])


def gather_row(shard):
    size = lax.axis_size("row")
    if size != 4:
        return lax.all_gather(shard, "row", axis=0, tiled=True)
    me = lax.axis_index("row")
    rows = shard.shape[0]
    cut = rows // 2
    first, second = shard[:cut], shard[cut:]
    first_x, second_x = swap(first, "row", 1), swap(second, "row", 1)
    second_y, first_y = swap(second, "row", 2), swap(first, "row", 2)
    first_xy, second_xy = swap(first_x, "row", 2), swap(second_y, "row", 1)
    whole = jnp.zeros((size * rows, shard.shape[1]), shard.dtype)
    pieces = ((0, first, second), (1, first_x, second_x), (2, first_y, second_y), (3, first_xy, second_xy))
    for distance, upper, lower in pieces:
        base = (me ^ distance) * rows
        whole = lax.dynamic_update_slice(whole, upper, (base, 0))
        whole = lax.dynamic_update_slice(whole, lower, (base + cut, 0))
    return whole


def sum_line(values):
    size = lax.axis_size("dp")
    if size != 4:
        return lax.psum(values, "dp")
    me = lax.axis_index("dp")
    inner = (me == 1) | (me == 2)
    kept = values.astype(wide)
    kept = kept + lax.ppermute(values, "dp", [(0, 1), (3, 2)]).astype(wide)
    sent = kept.astype(values.dtype)
    total = (kept + lax.ppermute(sent, "dp", [(1, 2), (2, 1)]).astype(wide)).astype(values.dtype)
    outer = lax.ppermute(total, "dp", [(1, 0), (2, 3)])
    return jnp.where(inner, total, outer)


def reduce_weight(partial):
    width = partial.shape[1] // 2
    arrived = swap(partial[:, width:].astype(low), "col", 1)
    merged = partial[:, :width] + arrived.astype(wide)
    return reduce_rows(merged)


def reduce_rows(merged):
    size = lax.axis_size("row")
    if size != 4:
        share = lax.psum_scatter(merged.astype(low), "row", scatter_dimension=0, tiled=True)
        return sum_line(share).astype(wide)
    me = lax.axis_index("row")
    rows = merged.shape[0] // size
    cut = rows // 2

    def piece(distance, start, count):
        return lax.dynamic_slice_in_dim(merged, (me ^ distance) * rows + start, count, 0)

    from_y = swap(piece(3, 0, cut).astype(low), "row", 2)
    from_x = swap(piece(3, cut, cut).astype(low), "row", 1)
    to_x = piece(1, 0, rows) + jnp.pad(from_y.astype(wide), ((0, cut), (0, 0)))
    to_y = piece(2, 0, rows) + jnp.pad(from_x.astype(wide), ((cut, 0), (0, 0)))
    got_x = swap(to_x.astype(low), "row", 1)
    got_y = swap(to_y.astype(low), "row", 2)
    share = piece(0, 0, rows) + got_x.astype(wide) + got_y.astype(wide)
    return sum_line(share.astype(low)).astype(wide)


def sum_row_dp(values):
    if lax.axis_size("row") != 4:
        return lax.psum(values, ("dp", "row"))
    values = values + swap(values, "row", 1)
    values = values + swap(values, "row", 2)
    return sum_line(values)


def shards(
    tokens, timesteps, block_ids, table, gain_one, bias_one, w_query, w_key, w_value, b_query,
    b_value, w_out, b_out, gain_two, bias_two, w_up, b_up, w_down, b_down, cotangent,
):
    seq_count, local_len, model_width = tokens.shape
    assert seq_count == 1 and lax.axis_size("col") == 2
    head_cols = w_query.shape[1]
    hidden_cols = w_up.shape[1]
    col_index = lax.axis_index("col")
    row_index = lax.axis_index("row")
    row_size, dp_size = lax.axis_size("row"), lax.axis_size("dp")
    seq_index = lax.axis_index("dp") * row_size + row_index
    seq_total = dp_size * row_size
    side = jnp.reshape(col_index, (1,)).astype(jnp.int32)

    group_one = jnp.concatenate([w_query, w_key, w_value], axis=1).astype(low)
    group_two = jnp.concatenate([w_out.T, w_up], axis=1).astype(low)
    group_three = w_down.T.astype(low)
    in_proj = gather_row(group_one)
    out_up = gather_row(group_two)
    down_mine = gather_row(group_three)
    in_proj_other = swap(in_proj, "col", 1)
    out_up_other = swap(out_up, "col", 1)
    down_other = swap(down_mine, "col", 1)

    table_row = lax.dynamic_slice_in_dim(table, timesteps[0], 1, 0)
    start = tokens[0].astype(wide) + table_row
    normed_one, unit_one, inverse_one = layer_norm_parts(start, gain_one, bias_one)
    rows_mine = normed_one.astype(low)
    rows_both = jnp.stack([rows_mine, swap(rows_mine, "col", 1)])
    in_bias = jnp.concatenate([b_query, jnp.zeros_like(b_query), b_value])
    qkv = (
        jnp.einsum("ard,dh->arh", rows_both, in_proj, preferred_element_type=wide) + in_bias
    ).astype(low)
    mixed, log_sums = attend_forward(side, qkv, block_ids, head_cols)
    attended = jnp.concatenate([mixed[0], swap(mixed[1], "col", 1)], axis=1)

    out_turned = jnp.concatenate([out_up[:, :head_cols], out_up_other[:, :head_cols]], axis=1)
    up_full = jnp.concatenate([out_up[:, head_cols:], out_up_other[:, head_cols:]], axis=1)
    down_turned = jnp.concatenate([down_mine, down_other], axis=1)
    up_bias = jnp.concatenate([b_up, swap(b_up, "col", 1)])

    middle = start + (dot_nt(attended, out_turned) + b_out)
    normed_two, unit_two, inverse_two = layer_norm_parts(middle, gain_two, bias_two)
    rows_two = normed_two.astype(low)
    hidden_pre = dot_nn(rows_two, up_full) + up_bias
    hidden, gelu_back = jax.vjp(gelu_exact, hidden_pre)
    hidden = hidden.astype(low)
    layer_out = (middle + (dot_nt(hidden, down_turned) + b_down)).astype(low)

    cot = cotangent[0]
    grad_b_down = jnp.sum(cot, axis=0, dtype=wide)
    grad_pre = gelu_back(dot_nn(cot, down_turned))[0].astype(low)
    grad_b_up_wide = jnp.sum(grad_pre, axis=0, dtype=wide)
    own_down = reduce_weight(dot_tn(cot, hidden))
    own_up = reduce_weight(dot_tn(rows_two, grad_pre))
    grad_normed_two = dot_nt(grad_pre, up_full)
    grad_gain_two = jnp.sum(grad_normed_two * unit_two, axis=0)
    grad_bias_two = jnp.sum(grad_normed_two, axis=0)
    grad_middle = cot.astype(wide) + norm_back(grad_normed_two, unit_two, inverse_two, gain_two)
    grad_branch = grad_middle.astype(low)
    grad_b_out = jnp.sum(grad_branch, axis=0, dtype=wide)
    own_out = reduce_weight(dot_tn(grad_branch, attended))
    grad_attended = dot_nn(grad_branch, out_turned).astype(low)
    grad_heads = jnp.stack([grad_attended[:, :head_cols], swap(grad_attended[:, head_cols:], "col", 1)])

    grad_query, grad_key, grad_value = attend_backward(
        side, qkv, grad_heads, block_ids, log_sums, head_cols
    )
    grad_qkv = jnp.concatenate([grad_query, grad_key, grad_value], axis=2)
    own_in = reduce_rows(
        jnp.einsum("ard,arh->dh", rows_both, grad_qkv, preferred_element_type=wide)
    )
    grad_in_bias = jnp.sum(grad_qkv, axis=(0, 1), dtype=wide)
    grad_normed_one = dot_nt(grad_qkv[0], in_proj) + dot_nt(swap(grad_qkv[1], "col", 1), in_proj_other)
    grad_gain_one = jnp.sum(grad_normed_one * unit_one, axis=0)
    grad_bias_one = jnp.sum(grad_normed_one, axis=0)
    grad_tokens = grad_middle + norm_back(grad_normed_one, unit_one, inverse_one, gain_one)
    token_sum = jnp.sum(grad_tokens, axis=0)

    vectors = jnp.stack(
        [grad_gain_one, grad_bias_one, grad_b_out, grad_gain_two, grad_bias_two, grad_b_down, token_sum]
    )
    vectors = vectors + swap(vectors, "col", 1)
    grad_b_up = grad_b_up_wide[:hidden_cols] + swap(grad_b_up_wide[hidden_cols:], "col", 1)
    slot = lax.broadcasted_iota(jnp.int32, (seq_total, 1), 0) == seq_index
    sums_by_seq = jnp.where(slot, vectors[6:7], 0.0)
    steps_by_seq = jnp.where(slot, timesteps[0].astype(wide), 0.0)
    packed = jnp.concatenate(
        [
            vectors[:6].reshape(-1),
            grad_in_bias,
            grad_b_up,
            sums_by_seq.reshape(-1),
            steps_by_seq.reshape(-1),
        ]
    )
    pad = -packed.shape[0] % 1024
    packed = sum_row_dp(jnp.pad(packed, (0, pad)).reshape(-1, 128)).reshape(-1)
    place = 0
    taken = []
    for size in (6 * model_width, 3 * head_cols, hidden_cols, seq_total * model_width, seq_total):
        taken.append(packed[place : place + size])
        place += size
    six = taken[0].reshape(6, model_width)
    in_bias_sum = taken[1]
    step_onehot = (
        lax.broadcasted_iota(jnp.int32, (seq_total, table.shape[0]), 1)
        == taken[4][:, None].astype(jnp.int32)
    ).astype(wide)
    grad_table = jnp.einsum(
        "sv,sd->vd",
        step_onehot,
        taken[3].reshape(seq_total, model_width),
        precision=lax.Precision.HIGHEST,
        preferred_element_type=wide,
    )
    return (
        layer_out[None],
        grad_tokens[None],
        grad_table,
        six[0],
        six[1],
        own_in[:, :head_cols],
        own_in[:, head_cols : 2 * head_cols],
        own_in[:, 2 * head_cols :],
        in_bias_sum[:head_cols],
        in_bias_sum[2 * head_cols :],
        own_out.T,
        six[2],
        six[3],
        six[4],
        own_up,
        taken[2],
        own_down.T,
        six[5],
    )


def solution(mesh):
    return jax.shard_map(
        shards,
        mesh=mesh,
        in_specs=(
            P(("dp", "row"), "col", None),
            P(("dp", "row")),
            P(("dp", "row"), None),
            P(),
            P(),
            P(),
            P("row", "col"),
            P("row", "col"),
            P("row", "col"),
            P("col"),
            P("col"),
            P("col", "row"),
            P(),
            P(),
            P(),
            P("row", "col"),
            P("col"),
            P("col", "row"),
            P(),
            P(("dp", "row"), "col", None),
        ),
        out_specs=(
            P(("dp", "row"), "col", None),
            P(("dp", "row"), "col", None),
            P(),
            P(),
            P(),
            P("row", "col"),
            P("row", "col"),
            P("row", "col"),
            P("col"),
            P("col"),
            P("col", "row"),
            P(),
            P(),
            P(),
            P("row", "col"),
            P("col"),
            P("col", "row"),
            P(),
        ),
        check_vma=False,
    )
```

```python
import functools

import jax
import jax.numpy as jnp
from jax import lax
from jax.experimental import pallas as pl
from jax.experimental.pallas import tpu as pltpu
from jax.sharding import PartitionSpec as P

HEAD_DIM = 64
norm_eps = 1e-05
masked_score = -1000000000.0
low = jnp.bfloat16
wide = jnp.float32
tile_rows = 256


def cost(micros):
    return pl.CostEstimate(flops=int(micros * 1.1e9), transcendentals=0, bytes_accessed=1 << 20)


def dot_nn(left, right):
    return lax.dot_general(left, right, (((1,), (0,)), ((), ())), preferred_element_type=wide)


def dot_nt(left, right):
    return lax.dot_general(left, right, (((1,), (1,)), ((), ())), preferred_element_type=wide)


def dot_tn(left, right):
    return lax.dot_general(left, right, (((0,), (0,)), ((), ())), preferred_element_type=wide)


def column_of(ids_row):
    parts = []
    for start in range(0, ids_row.shape[1], 128):
        piece = ids_row[:, start : start + 128].astype(wide)
        parts.append(jnp.transpose(jnp.broadcast_to(piece, (128, 128))))
    return jnp.concatenate(parts, axis=0)


def lanes(values):
    return [values[:, first : first + 128] for first in range(0, values.shape[1], 128)]


def variants(count):
    return [(2 * n, min(2 * n + 3, count)) for n in range(count // 2)]


def key_tile(ref, tile, half, side):
    rows = slice((tile % half) * tile_rows, (tile % half + 1) * tile_rows)
    return ref[(tile // half) ^ side, rows, :]


def allowed_part(ids_ref, ids_column, first):
    return ids_ref[:, first : first + 128].astype(wide) <= ids_column


def row_tile(half, shift):
    return lambda i, c: jnp.clip(i - half * (c[0] ^ shift), 0, half - 1)


def attend_forward_body(
    count, half, col_ref, q_ref, k_ref, v_ref, ids_ref, own_ref, other_ref, lse_ref, s_ref
):
    step, head = pl.program_id(1), pl.program_id(2)
    side = col_ref[0]
    lane = lax.broadcasted_iota(jnp.int32, (tile_rows, 128), 1)
    mine = lane // HEAD_DIM == head
    own_ids = ids_ref[:, pl.ds(pl.multiple_of(step * tile_rows, tile_rows), tile_rows)]

    def variant(open_tiles, keys):
        query = q_ref[...]
        part = jnp.where(mine, query, jnp.zeros_like(query)) * jnp.asarray(0.125, low)
        ids_column = column_of(own_ids)
        top = None
        for tile in range(keys):
            first = tile * tile_rows
            scores = lanes(dot_nt(part, key_tile(k_ref, tile, half, side)))
            for n, values in enumerate(scores):
                at = first + 128 * n
                if tile >= open_tiles:
                    values = jnp.where(
                        allowed_part(ids_ref, ids_column, at), values, masked_score
                    )
                s_ref[:, at : at + 128] = values
                top = values if top is None else jnp.maximum(top, values)
        top = jnp.max(top, axis=1, keepdims=True)
        total = None
        acc = None
        for tile in range(keys):
            first = tile * tile_rows
            expo = [jnp.exp(s - top) for s in lanes(s_ref[:, first : first + tile_rows])]
            for values in expo:
                total = values if total is None else total + values
            low_expo = jnp.concatenate([e.astype(low) for e in expo], axis=1)
            mixed = dot_nn(low_expo, key_tile(v_ref, tile, half, side))
            acc = mixed if acc is None else acc + mixed
        total = jnp.sum(total, axis=1, keepdims=True)
        out = (acc / total).astype(low)
        lse_ref[...] = jnp.where(
            lax.broadcasted_iota(jnp.int32, lse_ref.shape, 1) == head,
            top + jnp.log(total),
            lse_ref[...],
        )
        owned = (step // half) ^ side == 0

        @pl.when(owned)
        def _():
            own_ref[...] = jnp.where(mine, out, own_ref[...])

        @pl.when(jnp.logical_not(owned))
        def _():
            other_ref[...] = jnp.where(mine, out, other_ref[...])

    for n, bounds in enumerate(variants(count)):
        pl.when(step // 2 == n)(functools.partial(variant, *bounds))


def attend_forward(meta, qkv, ids, first, pairs):
    sides, rows, _ = qkv.shape
    length = sides * rows
    count = length // tile_rows
    half = rows // tile_rows
    head_cols = 128 * pairs
    own, other = row_tile(half, 0), row_tile(half, 1)
    return pl.pallas_call(
        functools.partial(attend_forward_body, count, half),
        grid_spec=pltpu.PrefetchScalarGridSpec(
            num_scalar_prefetch=1,
            grid=(pairs, count, 2),
            in_specs=[
                pl.BlockSpec(
                    (None, tile_rows, 128),
                    lambda h, i, e, c: ((i // half) ^ c[0], i % half, 3 * (h + first)),
                ),
                pl.BlockSpec((sides, rows, 128), lambda h, i, e, c: (0, 0, 3 * (h + first) + 1)),
                pl.BlockSpec((sides, rows, 128), lambda h, i, e, c: (0, 0, 3 * (h + first) + 2)),
                pl.BlockSpec((1, length), lambda h, i, e, c: (0, 0)),
            ],
            out_specs=[
                pl.BlockSpec((tile_rows, 128), lambda h, i, e, c: (own(i, c), h)),
                pl.BlockSpec((tile_rows, 128), lambda h, i, e, c: (other(i, c), h)),
                pl.BlockSpec((None, tile_rows, 2), lambda h, i, e, c: (h, i, 0)),
            ],
            scratch_shapes=[pltpu.VMEM((tile_rows, length), wide)],
        ),
        out_shape=[
            jax.ShapeDtypeStruct((rows, head_cols), low),
            jax.ShapeDtypeStruct((rows, head_cols), low),
            jax.ShapeDtypeStruct((pairs, length, 2), wide),
        ],
        cost_estimate=cost(14 * pairs),
        name="attend_forward",
    )(meta, qkv, qkv, qkv, ids)


def attend_backward_body(
    count, half, col_ref, q_ref, k_ref, v_ref, g_ref, g_other_ref, ids_ref, lse_ref,
    own_ref, other_ref, sum_ref, p_ref, gp_ref, low_ref, gq_ref, gk_acc, gv_acc,
):
    step, head = pl.program_id(1), pl.program_id(2)
    side = col_ref[0]
    lane = lax.broadcasted_iota(jnp.int32, (tile_rows, 128), 1)
    mine = lane // HEAD_DIM == head
    own_ids = ids_ref[:, pl.ds(pl.multiple_of(step * tile_rows, tile_rows), tile_rows)]

    def store(tile, place, values):
        start = pl.multiple_of((tile % half) * tile_rows, tile_rows)
        here = (pl.ds(start, tile_rows), slice(place * 128, (place + 1) * 128))
        owned = (tile // half) ^ side == 0

        @pl.when(owned)
        def _():
            own_ref[here] = values

        @pl.when(jnp.logical_not(owned))
        def _():
            other_ref[here] = values

    @pl.when((step == 0) & (head == 0))
    def _():
        gk_acc[...] = jnp.zeros_like(gk_acc)
        gv_acc[...] = jnp.zeros_like(gv_acc)
        sum_ref[...] = jnp.zeros_like(sum_ref)

    def variant(open_tiles, keys):
        query = q_ref[...]
        grad = jnp.where((step // half) ^ side == 0, g_ref[...], g_other_ref[...])
        part = jnp.where(mine, query, jnp.zeros_like(query)) * jnp.asarray(0.125, low)
        grad_part = jnp.where(mine, grad, jnp.zeros_like(grad))
        start = pl.multiple_of(head * HEAD_DIM, HEAD_DIM)
        spot = pl.ds(start, HEAD_DIM)

        def turned(values):
            flat = jnp.transpose(values)
            return jnp.where(head == 0, flat[:HEAD_DIM], flat[HEAD_DIM:])

        query_turned, grad_turned = turned(query), turned(grad)
        ids_column = column_of(own_ids)
        log_sum = jnp.where(head == 0, lse_ref[:, :1], lse_ref[:, 1:])
        inner = None
        for tile in range(keys):
            first = tile * tile_rows
            here = slice(first, first + tile_rows)
            scores = lanes(dot_nt(part, key_tile(k_ref, tile, half, side)))
            grad_probs = dot_nt(grad_part, key_tile(v_ref, tile, half, side))
            gp_ref[:, here] = grad_probs
            lows = []
            for n, (values, slope) in enumerate(zip(scores, lanes(grad_probs))):
                at = first + 128 * n
                values = jnp.exp(values - log_sum)
                if tile >= open_tiles:
                    values = jnp.where(allowed_part(ids_ref, ids_column, at), values, 0.0)
                p_ref[:, at : at + 128] = values
                lows.append(values.astype(low))
                values = values * slope
                inner = values if inner is None else inner + values
            lows = jnp.concatenate(lows, axis=1)
            gv_acc[spot, here] += dot_nn(grad_turned, lows)
        inner = jnp.sum(inner, axis=1, keepdims=True)
        grad_query = None
        for tile in range(keys):
            here = slice(tile * tile_rows, (tile + 1) * tile_rows)
            slopes = (p_ref[:, here] * (gp_ref[:, here] - inner)).astype(low)
            piece = dot_nn(slopes, key_tile(k_ref, tile, half, side))
            grad_query = piece if grad_query is None else grad_query + piece
            gk_acc[spot, here] += dot_nn(query_turned, slopes)
        gq_ref[...] = jnp.where(mine, grad_query, gq_ref[...])

    for n, bounds in enumerate(variants(count)):
        pl.when(step // 2 == n)(functools.partial(variant, *bounds))

    @pl.when(head == 1)
    def _():
        out = (gq_ref[...] * 0.125).astype(low)
        store(step, 0, out)
        sum_ref[0:1, :] += jnp.sum(out.astype(wide), axis=0, keepdims=True)

    @pl.when((step == count - 1) & (head == 1))
    def _():
        def finish(tile, _):
            here = pl.ds(pl.multiple_of(tile * tile_rows, tile_rows), tile_rows)
            grad_key = jnp.transpose(gk_acc[:, here] * 0.125).astype(low)
            grad_value = jnp.transpose(gv_acc[:, here]).astype(low)
            store(tile, 1, grad_key)
            store(tile, 2, grad_value)
            sum_ref[1:2, :] += jnp.sum(grad_value.astype(wide), axis=0, keepdims=True)

        lax.fori_loop(0, count, finish, None)


def attend_backward(meta, qkv, grad, grad_other, ids, log_sums, first, pairs, lse_first):
    sides, rows, _ = qkv.shape
    length = sides * rows
    count = length // tile_rows
    half = rows // tile_rows
    own, other = row_tile(half, 0), row_tile(half, 1)
    whole = pl.BlockSpec((rows, 384), lambda h, i, e, c: (0, h))
    return pl.pallas_call(
        functools.partial(attend_backward_body, count, half),
        grid_spec=pltpu.PrefetchScalarGridSpec(
            num_scalar_prefetch=1,
            grid=(pairs, count, 2),
            in_specs=[
                pl.BlockSpec(
                    (None, tile_rows, 128),
                    lambda h, i, e, c: ((i // half) ^ c[0], i % half, 3 * (h + first)),
                ),
                pl.BlockSpec((sides, rows, 128), lambda h, i, e, c: (0, 0, 3 * (h + first) + 1)),
                pl.BlockSpec((sides, rows, 128), lambda h, i, e, c: (0, 0, 3 * (h + first) + 2)),
                pl.BlockSpec((tile_rows, 128), lambda h, i, e, c: (own(i, c), h + first)),
                pl.BlockSpec((tile_rows, 128), lambda h, i, e, c: (other(i, c), h + first)),
                pl.BlockSpec((1, length), lambda h, i, e, c: (0, 0)),
                pl.BlockSpec((None, tile_rows, 2), lambda h, i, e, c: (h + lse_first, i, 0)),
            ],
            out_specs=[whole, whole, pl.BlockSpec((8, 128), lambda h, i, e, c: (0, h))],
            scratch_shapes=[
                pltpu.VMEM((tile_rows, length), wide),
                pltpu.VMEM((tile_rows, length), wide),
                pltpu.VMEM((8, 128), low),
                pltpu.VMEM((tile_rows, 128), wide),
                pltpu.VMEM((128, length), wide),
                pltpu.VMEM((128, length), wide),
            ],
        ),
        out_shape=[jax.ShapeDtypeStruct((rows, 384 * pairs), low)] * 2
        + [jax.ShapeDtypeStruct((8, 128 * pairs), wide)],
        cost_estimate=cost(25 * pairs),
        name="attend_backward",
    )(meta, qkv, qkv, qkv, grad, grad_other, ids, log_sums)


def norm_parts(values):
    mean = jnp.mean(values, axis=-1, keepdims=True)
    centred = values - mean
    inverse = lax.rsqrt(jnp.mean(centred * centred, axis=-1, keepdims=True) + norm_eps)
    return centred * inverse, inverse


def norm_back(grad_normed, unit, inverse, gain):
    grad_unit = grad_normed * gain
    first_mean = jnp.mean(grad_unit, axis=-1, keepdims=True)
    second_mean = jnp.mean(grad_unit * unit, axis=-1, keepdims=True)
    return inverse * (grad_unit - first_mean - unit * second_mean)


erfc_terms = (
    -0.12664913241116757, 0.4719797697046255, -0.4849989149703286, 0.5173882238837517,
    -0.0742751946996765, 0.20647784419749105, 0.15044607588806108, 0.17042678586105697,
    0.16920458065681523,
)


def gelu_with_slope(values):
    turned = 1.0 / (1.0 + (0.3 * 0.5**0.5) * jnp.abs(values))
    bell = jnp.exp(-0.5 * (values * values))
    series = jnp.full_like(values, 0.5 * erfc_terms[0])
    for term in erfc_terms[1:]:
        series = series * turned + 0.5 * term
    tail = series * turned * bell
    below = jnp.where(values < 0.0, tail, 1.0 - tail)
    return values * below, below + values * (bell * (0.5 / jnp.pi) ** 0.5)


def swap(values, axis, distance):
    size = lax.axis_size(axis)
    return lax.ppermute(values, axis, [(i, i ^ distance) for i in range(size)])


def gather_near(shard):
    return swap(shard, "row", 1), swap(shard, "row", 2)


def gather_far(shard, from_x, from_y):
    cut = shard.shape[0] // 2
    first_xy = swap(from_x[:cut], "row", 2)
    second_xy = swap(from_y[cut:], "row", 1)
    return [(0, 0, shard), (1, 0, from_x), (2, 0, from_y), (3, 0, first_xy), (3, cut, second_xy)]


def piece_copies(layout, refs, target, row_index, shard_rows, sems):
    copies = []
    for n, ((distance, first, rows), ref) in enumerate(zip(layout, refs)):
        base = pl.multiple_of((row_index ^ distance) * shard_rows + first, 16)
        copies.append(pltpu.make_async_copy(ref, target.at[pl.ds(base, rows), :], sems.at[n]))
    return copies


def layout_of(pieces):
    return [(distance, first, piece.shape[0]) for distance, first, piece in pieces]


hbm = pl.BlockSpec(memory_space=pl.ANY)


def project_in_body(layout, tiles, meta_ref, mine_ref, other_ref, bias_ref, *rest):
    pieces = rest[: len(layout)]
    out_ref, turned_ref, weight_out, weight, sems, out_sem = rest[len(layout) :]
    step = pl.program_id(0)
    keep = pltpu.make_async_copy(weight, weight_out, out_sem)

    @pl.when(step == 0)
    def _():
        copies = piece_copies(layout, pieces, weight, meta_ref[1], weight.shape[0] // 4, sems)
        for copy in copies:
            copy.start()
        for copy in copies:
            copy.wait()
        keep.start()

    @pl.when(step < tiles)
    def _():
        rows = mine_ref[...]
        out_ref[...] = (dot_nn(rows, weight[...]) + bias_ref[...]).astype(low)
        turned_ref[...] = jnp.transpose(rows)

    @pl.when(step >= tiles)
    def _():
        rows = other_ref[...]
        out_ref[...] = (dot_nn(rows, weight[...]) + bias_ref[...]).astype(low)
        turned_ref[...] = jnp.transpose(rows)

    @pl.when(step == 2 * tiles - 1)
    def _():
        keep.wait()


def project_in(meta, mine, other, bias, pieces):
    rows, model = mine.shape
    size = 2 * tile_rows
    tiles = rows // size
    width = pieces[0][2].shape[1]
    return pl.pallas_call(
        functools.partial(project_in_body, layout_of(pieces), tiles),
        grid_spec=pltpu.PrefetchScalarGridSpec(
            num_scalar_prefetch=1,
            grid=(2 * tiles,),
            in_specs=[
                pl.BlockSpec((size, model), lambda i, m: (jnp.minimum(i, tiles - 1), 0)),
                pl.BlockSpec((size, model), lambda i, m: (jnp.maximum(i - tiles, 0), 0)),
                pl.BlockSpec((1, width), lambda i, m: (0, 0)),
            ]
            + [hbm] * len(pieces),
            out_specs=[
                pl.BlockSpec((None, size, width), lambda i, m: (i // tiles, i % tiles, 0)),
                pl.BlockSpec((model, size), lambda i, m: (0, i)),
                hbm,
            ],
            scratch_shapes=[
                pltpu.VMEM((model, width), low),
                pltpu.SemaphoreType.DMA((len(pieces),)),
                pltpu.SemaphoreType.DMA(()),
            ],
        ),
        out_shape=[
            jax.ShapeDtypeStruct((2, rows, width), low),
            jax.ShapeDtypeStruct((model, 2 * rows), low),
            jax.ShapeDtypeStruct((model, width), low),
        ],
        cost_estimate=cost(7),
        name="project_in",
    )(meta, mine, other, bias, *[piece for _, _, piece in pieces])


def load_weights(layout, pieces, weight, meta_ref, sems):
    copies = []
    for side in range(2):
        copies += piece_copies(
            layout, pieces[side], weight.at[side], meta_ref[1], weight.shape[1] // 4, sems.at[side]
        )
    for copy in copies:
        copy.start()
    for copy in copies:
        copy.wait()


hidden_chunk = 512


def feed_body(
    layout, head_cols, hidden_cols, meta_ref, tok_ref, row_ref, mixed_ref, mixed_last_ref,
    got_ref, got_last_ref, cot_ref, vec_ref, up_bias_ref, *rest,
):
    count = len(layout)
    pieces = (rest[:count], rest[count : 2 * count])
    (
        out_ref, keep_ref, send_ref, gkeep_ref, gsend_ref, two_ref, cot_turned_ref, branch_ref,
        middle_ref, own_ref, other_ref, sum_ref, bias_ref, weight, sems,
    ) = rest[2 * count :]

    @pl.when(pl.program_id(0) == 0)
    def _():
        load_weights(layout, pieces, weight, meta_ref, sems)
        sum_ref[...] = jnp.zeros_like(sum_ref)
        bias_ref[...] = jnp.zeros_like(bias_ref)

    bias_out, gain, bias, bias_down = (vec_ref[n : n + 1, :] for n in range(4))
    cot = cot_ref[...]
    cot_turned_ref[...] = jnp.transpose(cot)
    start = tok_ref[...].astype(wide) + row_ref[...]
    cut = mixed_ref.shape[1]
    branch = dot_nt(mixed_ref[...], weight[0, :, :cut])
    branch = branch + dot_nt(mixed_last_ref[...], weight[0, :, cut:head_cols])
    branch = branch + dot_nt(got_ref[...], weight[1, :, :cut])
    branch = branch + dot_nt(got_last_ref[...], weight[1, :, cut:head_cols])
    middle = start + (branch + bias_out)
    unit, inverse = norm_parts(middle)
    two = (unit * gain + bias).astype(low)
    two_ref[...] = jnp.transpose(two)
    mixer = None
    grad_two = None
    for side in range(2):
        for first in range(0, hidden_cols, hidden_chunk):
            here = slice(first, first + hidden_chunk)
            there = slice(side * hidden_cols + first, side * hidden_cols + first + hidden_chunk)
            up = weight[side, :, head_cols + first : head_cols + first + hidden_chunk]
            at = head_cols + hidden_cols + first
            down = weight[side, :, at : at + hidden_chunk]
            hidden, slope = gelu_with_slope(dot_nn(two, up) + up_bias_ref[:, there])
            hidden = hidden.astype(low)
            (send_ref if side else keep_ref)[:, here] = hidden
            part = dot_nt(hidden, down)
            mixer = part if mixer is None else mixer + part
            grad_pre = (dot_nn(cot, down) * slope).astype(low)
            (gsend_ref if side else gkeep_ref)[:, here] = grad_pre
            bias_ref[:, there] += jnp.sum(grad_pre.astype(wide), axis=0, keepdims=True)
            part = dot_nt(grad_pre, up)
            grad_two = part if grad_two is None else grad_two + part
    out_ref[...] = (middle + (mixer + bias_down)).astype(low)
    cot = cot.astype(wide)
    grad_middle = cot + norm_back(grad_two, unit, inverse, gain)
    grad_branch = grad_middle.astype(low)
    middle_ref[...] = grad_middle
    branch_ref[...] = jnp.transpose(grad_branch)
    own_ref[...] = dot_nn(grad_branch, weight[0, :, :head_cols]).astype(low)
    other_ref[...] = dot_nn(grad_branch, weight[1, :, :head_cols]).astype(low)
    for n, values in enumerate((grad_branch.astype(wide), grad_two * unit, grad_two, cot)):
        sum_ref[n : n + 1, :] += jnp.sum(values, axis=0, keepdims=True)


def feed(meta, tokens, table_row, mixed, got, cot, vectors, up_bias, mine, other):
    rows, model = tokens.shape
    size = tile_rows
    head_cols = sum(part.shape[1] for part in mixed)
    hidden_cols = up_bias.shape[1] // 2
    width = mine[0][2].shape[1]

    def tile(columns):
        return pl.BlockSpec((size, columns), lambda i, m: (i, 0))

    def fixed(*shape):
        return pl.BlockSpec(shape, lambda i, m: (0,) * len(shape))

    def turned(depth):
        return pl.BlockSpec((depth, size), lambda i, m: (0, i))

    def array(columns, dtype):
        return jax.ShapeDtypeStruct((rows, columns), dtype)

    flipped = jax.ShapeDtypeStruct((model, rows), low)
    return pl.pallas_call(
        functools.partial(feed_body, layout_of(mine), head_cols, hidden_cols),
        grid_spec=pltpu.PrefetchScalarGridSpec(
            num_scalar_prefetch=1,
            grid=(rows // size,),
            in_specs=[tile(model), fixed(1, model)]
            + [tile(part.shape[1]) for part in (*mixed, *got)]
            + [tile(model), fixed(8, model), fixed(1, 2 * hidden_cols)]
            + [hbm] * (2 * len(mine)),
            out_specs=[tile(model)]
            + [tile(hidden_cols)] * 4
            + [turned(model)] * 3
            + [tile(model), tile(head_cols), tile(head_cols), fixed(8, model)]
            + [fixed(1, 2 * hidden_cols)],
            scratch_shapes=[
                pltpu.VMEM((2, model, width), low),
                pltpu.SemaphoreType.DMA((2, len(mine))),
            ],
        ),
        out_shape=[array(model, low)]
        + [array(hidden_cols, low)] * 4
        + [flipped] * 3
        + [array(model, wide), array(head_cols, low), array(head_cols, low)]
        + [jax.ShapeDtypeStruct((8, model), wide)]
        + [jax.ShapeDtypeStruct((1, 2 * hidden_cols), wide)],
        cost_estimate=cost(45),
        name="feed",
    )(
        meta, tokens, table_row, *mixed, *got, cot, vectors, up_bias,
        *[piece for _, _, piece in mine], *[piece for _, _, piece in other],
    )


def weight_parts_body(products, near, meta_ref, *refs):
    send_ref, keep_ref = refs[-2:]
    shard = send_ref.shape[0] // 2
    order = [pl.multiple_of((meta_ref[1] ^ d) * shard, 64) for d in (3, near, 3 - near, 0)]

    def in_order(ref):
        return jnp.concatenate([ref[pl.ds(start, shard), :] for start in order], axis=0)

    at = 0
    for lefts, arrived, first, tiles in products:
        inputs = refs[at : at + 2 * lefts + arrived]
        at += 2 * lefts + arrived

        @pl.when((pl.program_id(0) >= first) & (pl.program_id(0) < first + tiles))
        def _(inputs=inputs, lefts=lefts, arrived=arrived):
            total = None
            for n in range(lefts):
                part = dot_nn(in_order(inputs[2 * n]), inputs[2 * n + 1][...])
                total = part if total is None else total + part
            if arrived:
                total = total + in_order(inputs[-1]).astype(wide)
            total = total.astype(low)
            send_ref[...] = total[: 2 * shard]
            keep_ref[...] = total[2 * shard :]


def weight_parts(meta, products, near, micros):
    model = products[0][0][0][0].shape[0]
    operands, specs, shapes = [], [], []
    step = 384
    first = 0
    for pairs, arrived in products:
        tiles = pairs[0][2].shape[1] // step

        def tile(i, m, first=first, tiles=tiles):
            return (0, jnp.clip(i - first, 0, tiles - 1))

        for left, place, right in pairs:
            depth = right.shape[0]
            specs.append(pl.BlockSpec((model, depth), lambda i, m, p=place: (0, p)))
            specs.append(pl.BlockSpec((depth, step), tile))
            operands += [left, right]
        if arrived is not None:
            specs.append(pl.BlockSpec((model, step), tile))
            operands.append(arrived)
        shapes.append((len(pairs), int(arrived is not None), first, tiles))
        first += tiles
    half = jax.ShapeDtypeStruct((model // 2, first * step), low)
    return pl.pallas_call(
        functools.partial(weight_parts_body, shapes, near),
        grid_spec=pltpu.PrefetchScalarGridSpec(
            num_scalar_prefetch=1,
            grid=(first,),
            in_specs=specs,
            out_specs=[pl.BlockSpec((model // 2, step), lambda i, m: (0, i))] * 2,
        ),
        out_shape=[half, half],
        cost_estimate=cost(micros),
        name="weight_parts",
    )(meta, *operands)


def product_body(left_ref, right_ref, out_ref):
    out_ref[...] = dot_nn(left_ref[...], right_ref[...]).astype(low)


def product(left, right, micros):
    rows, depth = left.shape
    columns = right.shape[1]
    step = 384
    return pl.pallas_call(
        product_body,
        grid=(columns // step,),
        in_specs=[
            pl.BlockSpec((rows, depth), lambda i: (0, 0)),
            pl.BlockSpec((depth, step), lambda i: (0, i)),
        ],
        out_specs=pl.BlockSpec((rows, step), lambda i: (0, i)),
        out_shape=jax.ShapeDtypeStruct((rows, columns), low),
        cost_estimate=cost(micros),
        name="product",
    )(left, right)


def pack_body(*refs):
    out_ref = refs[-1]
    for n in range(out_ref.shape[1] // 128):
        kind, pair = n % 3, n // 3
        out_ref[:, 128 * n : 128 * (n + 1)] = refs[kind][:, 128 * pair : 128 * (pair + 1)].astype(low)


def pack(*weights):
    rows, columns = weights[0].shape
    return pl.pallas_call(
        pack_body,
        out_shape=jax.ShapeDtypeStruct((rows, 3 * columns), low),
        cost_estimate=cost(1),
        name="pack",
    )(*weights)


def grad_in_body(cuts, tok_ref, row_ref, gain_ref, own_ref, other_ref, middle_ref, *rest):
    grads = rest[: 2 * len(cuts)]
    out_ref, sum_ref = rest[2 * len(cuts) :]

    @pl.when(pl.program_id(0) == 0)
    def _():
        sum_ref[...] = jnp.zeros_like(sum_ref)

    grad = None
    for n, (first, last) in enumerate(cuts):
        for values, weight in ((grads[2 * n], own_ref), (grads[2 * n + 1], other_ref)):
            part = dot_nt(values[...], weight[:, first:last])
            grad = part if grad is None else grad + part
    unit, inverse = norm_parts(tok_ref[...].astype(wide) + row_ref[...])
    tokens = middle_ref[...] + norm_back(grad, unit, inverse, gain_ref[...])
    out_ref[...] = tokens
    for n, values in enumerate((grad * unit, grad, tokens)):
        sum_ref[n : n + 1, :] += jnp.sum(values, axis=0, keepdims=True)


def grad_in(tokens, table_row, gain, own, other, grad_middle, grads):
    rows, model = tokens.shape
    size = tile_rows
    width = own.shape[1]
    cuts = []
    for mine, _ in grads:
        first = cuts[-1][1] if cuts else 0
        cuts.append((first, first + mine.shape[1]))

    def tile(columns):
        return pl.BlockSpec((size, columns), lambda i: (i, 0))

    def fixed(*shape):
        return pl.BlockSpec(shape, lambda i: (0, 0))

    flat = [values for pair in grads for values in pair]
    return pl.pallas_call(
        functools.partial(grad_in_body, cuts),
        grid=(rows // size,),
        in_specs=[
            tile(model), fixed(1, model), fixed(1, model), fixed(model, width),
            fixed(model, width), tile(model),
        ]
        + [tile(values.shape[1]) for values in flat],
        out_specs=[tile(model), fixed(8, model)],
        out_shape=[
            jax.ShapeDtypeStruct((rows, model), wide),
            jax.ShapeDtypeStruct((8, model), wide),
        ],
        cost_estimate=cost(9),
        name="grad_in",
    )(tokens, table_row, gain, own, other, grad_middle, *flat)


def after(values, *needed):
    needed = [value for value in needed if value is not None]
    return lax.optimization_barrier((values, *needed))[0] if needed else values


def line_steps(values):
    if lax.axis_size("dp") != 4:
        return lax.psum(values, "dp")
    for distance in (1, 2):
        arrived = swap(values, "dp", distance)
        token = yield values
        arrived = after(arrived, token)
        values = (values.astype(wide) + arrived.astype(wide)).astype(values.dtype)
    return values


def weight_steps(parts, near):
    send, keep = parts
    shard = send.shape[0] // 2
    arrived = swap(send, "row", near)
    token = yield send
    arrived = after(arrived, token)
    passed = (keep[:shard].astype(wide) + arrived[:shard].astype(wide)).astype(low)
    last = swap(passed, "row", 3 - near)
    token = yield passed
    last = after(last, token)
    share = keep[shard:].astype(wide) + arrived[shard:].astype(wide) + last.astype(wide)
    total = yield from line_steps(share.astype(low))
    return total.astype(wide)


def vector_steps(values):
    for axis, distance in (("row", 1), ("row", 2)):
        arrived = swap(values, axis, distance)
        token = yield values
        values = values + after(arrived, token)
    total = yield from line_steps(values)
    return total


class Chains:
    def __init__(self):
        self.steps, self.done = [], {}

    def add(self, steps):
        self.steps.append(steps)
        return [next(steps)]

    def advance(self, token=None, chosen=None):
        sent = []
        for n, steps in enumerate(self.steps):
            if n not in self.done and (chosen is None or n in chosen):
                try:
                    sent.append(steps.send(token))
                except StopIteration as stop:
                    self.done[n] = stop.value
        return sent


def shards(
    tokens, timesteps, block_ids, table, gain_one, bias_one, w_query, w_key, w_value, b_query,
    b_value, w_out, b_out, gain_two, bias_two, w_up, b_up, w_down, b_down, cotangent,
):
    seq_count, local_len, model_width = tokens.shape
    row_size, dp_size = lax.axis_size("row"), lax.axis_size("dp")
    assert seq_count == 1 and lax.axis_size("col") == 2 and row_size == 4
    head_cols = w_query.shape[1]
    hidden_cols = w_up.shape[1]
    col_index = lax.axis_index("col")
    row_index = lax.axis_index("row")
    seq_index = lax.axis_index("dp") * row_size + row_index
    seq_total = dp_size * row_size
    meta = jnp.stack([col_index, row_index]).astype(jnp.int32)

    cuts = [slice(first, first + 128) for first in range(0, head_cols, 128)]
    group_one = pack(w_query, w_key, w_value)
    in_bias = jnp.concatenate(
        [part for cut in cuts for part in (b_query[cut], jnp.zeros_like(b_query[cut]), b_value[cut])]
    )[None]
    in_pieces = gather_far(group_one, *gather_near(group_one))
    group_two = jnp.concatenate([w_out.T, w_up, w_down.T], axis=1).astype(low)
    group_two = after(group_two, in_pieces[3][2], in_pieces[4][2])
    near_x, near_y = gather_near(group_two)

    table_row = lax.dynamic_slice_in_dim(table, timesteps[0], 1, 0)
    unit_one, _ = norm_parts(tokens[0].astype(wide) + table_row)
    rows_mine = (unit_one * gain_one + bias_one).astype(low)
    rows_other = swap(rows_mine, "col", 1)
    up_bias = jnp.concatenate([b_up, swap(b_up, "col", 1)])[None]
    qkv, rows_turned, in_own = project_in(
        meta, rows_mine, after(rows_other, up_bias), in_bias, in_pieces
    )
    in_other = swap(in_own, "col", 1)
    shard_other = swap(group_two, "col", 1)
    pairs = head_cols // 128
    mixed, mixed_other, log_sums = attend_forward(
        meta, after(qkv, in_other, shard_other), block_ids, 0, pairs - 1
    )
    got = swap(mixed_other, "col", 1)
    near_x, near_y = after(near_x, mixed), after(near_y, mixed)
    near_x_other, near_y_other = swap(near_x, "col", 1), swap(near_y, "col", 1)
    mine = gather_far(group_two, near_x, near_y)
    mixed_last, mixed_last_other, log_sums_last = attend_forward(
        meta, after(qkv, got, near_x_other, near_y_other), block_ids, pairs - 1, 1
    )
    got_last = swap(mixed_last_other, "col", 1)
    far = [after(piece, mixed_last) for _, _, piece in mine[3:]]
    others = [shard_other, near_x_other, near_y_other] + [swap(piece, "col", 1) for piece in far]
    other = [(distance, first, piece) for (distance, first, _), piece in zip(mine, others)]

    spare = jnp.zeros_like(b_out)
    vectors = jnp.stack([b_out, gain_two, bias_two, b_down, spare, spare, spare, spare])
    cot = cotangent[0]
    (
        layer_out, keep, send, grad_keep, grad_send, two_turned, cot_turned, branch_turned,
        grad_middle, grad_own, grad_other, sums, grad_up_bias,
    ) = feed(
        meta, tokens[0], table_row, (mixed, mixed_last), (got, got_last), cot, vectors, up_bias,
        mine, other,
    )
    up_arrived = swap(product(two_turned, grad_send, 4), "col", 1)
    out_arrived = swap(
        product(branch_turned, jnp.concatenate([got, got_last], axis=1), 1), "col", 1
    )
    down_arrived = swap(product(cot_turned, send, 4), "col", 1)
    grad_got = swap(grad_other, "col", 1)
    up_parts = weight_parts(
        meta,
        [
            ([(two_turned, 0, grad_keep)], up_arrived),
            ([(branch_turned, 0, jnp.concatenate([mixed, mixed_last], axis=1))], out_arrived),
        ],
        1,
        8,
    )
    chains = Chains()
    chains.add(weight_steps(up_parts, 1))
    down_parts = weight_parts(
        meta, [([(cot_turned, 0, after(keep, *up_parts))], down_arrived)], 2, 7
    )
    chains.add(weight_steps(down_parts, 2))
    grad_b_up = grad_up_bias[0, :hidden_cols] + swap(grad_up_bias[0, hidden_cols:], "col", 1)
    before = [*up_parts, *down_parts, grad_b_up]

    own_grads, gots, bias_sums = [], [], []
    for pair in range(pairs):
        last = pair == pairs - 1
        own, away, bias_sum = attend_backward(
            meta, after(qkv, *before), grad_own, grad_got, block_ids,
            log_sums_last if last else log_sums, pair, 1, 0 if last else pair,
        )
        own_grads.append(own)
        gots.append(swap(away, "col", 1))
        bias_sums.append(bias_sum)
        before = [*chains.advance(own), gots[-1]]
        if last or pair == pairs - 2:
            products = [(own, away)] if last else list(zip(own_grads, aways + [away]))
            near = 1 if last else 2
            parts = weight_parts(
                meta,
                [([(rows_turned, 0, a), (rows_turned, 1, b)], None) for a, b in products],
                near,
                3 * len(products),
            )
            before += parts
            chains.add(weight_steps(parts, near))
        else:
            aways = [away] if pair == 0 else aways + [away]
    grad_tokens, late_sums = grad_in(
        after(tokens[0], *before), table_row, gain_one[None], in_own, in_other, grad_middle,
        list(zip(own_grads, gots)),
    )
    chains.advance(grad_tokens, (2, 3))

    shared = jnp.concatenate([late_sums[:3], sums[:4]])
    shared = shared + swap(shared, "col", 1)
    slot = lax.broadcasted_iota(jnp.int32, (seq_total, 1), 0) == seq_index
    packed = jnp.concatenate(
        [
            jnp.concatenate([shared[:2], shared[3:]]).reshape(-1),
            jnp.concatenate([part[:1] for part in bias_sums], axis=1).reshape(-1),
            jnp.concatenate([part[1:2] for part in bias_sums], axis=1).reshape(-1),
            grad_b_up,
            jnp.where(slot, shared[2:3], 0.0).reshape(-1),
            jnp.where(slot, timesteps[0].astype(wide), 0.0).reshape(-1),
        ]
    )
    pad = -packed.shape[0] % 1024
    chains.add(vector_steps(jnp.pad(packed, (0, pad)).reshape(-1, 128)))
    while not {2, 3, 4} <= set(chains.done):
        chains.advance(None, (2, 3, 4))
    chains.advance(chains.done[4])
    done = chains.done
    own_up_out, own_down = done[0], done[1]
    own_in = jnp.concatenate([done[2], done[3]], axis=1)
    own_in = [
        jnp.concatenate([own_in[:, 128 * n : 128 * (n + 1)] for n in range(kind, 3 * pairs, 3)], axis=1)
        for kind in range(3)
    ]
    packed = done[4].reshape(-1)
    place = 0
    taken = []
    for size in (6 * model_width, 2 * head_cols, hidden_cols, seq_total * model_width, seq_total):
        taken.append(packed[place : place + size])
        place += size
    six = taken[0].reshape(6, model_width)
    step_onehot = (
        lax.broadcasted_iota(jnp.int32, (seq_total, table.shape[0]), 1)
        == taken[4][:, None].astype(jnp.int32)
    ).astype(wide)
    grad_table = jnp.einsum(
        "sv,sd->vd",
        step_onehot,
        taken[3].reshape(seq_total, model_width),
        precision=lax.Precision.HIGHEST,
        preferred_element_type=wide,
    )
    return (
        layer_out[None],
        grad_tokens[None],
        grad_table,
        six[0],
        six[1],
        own_in[0],
        own_in[1],
        own_in[2],
        taken[1][:head_cols],
        taken[1][head_cols:],
        own_up_out[:, hidden_cols:].T,
        six[2],
        six[3],
        six[4],
        own_up_out[:, :hidden_cols],
        taken[2],
        own_down.T,
        six[5],
    )


def solution(mesh):
    return jax.shard_map(
        shards,
        mesh=mesh,
        in_specs=(
            P(("dp", "row"), "col", None),
            P(("dp", "row")),
            P(("dp", "row"), None),
            P(),
            P(),
            P(),
            P("row", "col"),
            P("row", "col"),
            P("row", "col"),
            P("col"),
            P("col"),
            P("col", "row"),
            P(),
            P(),
            P(),
            P("row", "col"),
            P("col"),
            P("col", "row"),
            P(),
            P(("dp", "row"), "col", None),
        ),
        out_specs=(
            P(("dp", "row"), "col", None),
            P(("dp", "row"), "col", None),
            P(),
            P(),
            P(),
            P("row", "col"),
            P("row", "col"),
            P("row", "col"),
            P("col"),
            P("col"),
            P("col", "row"),
            P(),
            P(),
            P(),
            P("row", "col"),
            P("col"),
            P("col", "row"),
            P(),
        ),
        check_vma=False,
    )
```

```python
import functools

import jax
import jax.numpy as jnp
from jax import lax
from jax.experimental import pallas as pl
from jax.experimental.pallas import tpu as pltpu
from jax.sharding import PartitionSpec as P

HEAD_DIM = 64
norm_eps = 1e-05
masked_score = -1000000000.0
low = jnp.bfloat16
wide = jnp.float32
tile_rows = 256


def cost(micros):
    return pl.CostEstimate(flops=int(micros * 1.1e9), transcendentals=0, bytes_accessed=1 << 20)


def dot_nn(left, right):
    return lax.dot_general(left, right, (((1,), (0,)), ((), ())), preferred_element_type=wide)


def dot_nt(left, right):
    return lax.dot_general(left, right, (((1,), (1,)), ((), ())), preferred_element_type=wide)


def dot_tn(left, right):
    return lax.dot_general(left, right, (((0,), (0,)), ((), ())), preferred_element_type=wide)


def column_of(ids_row):
    parts = []
    for start in range(0, ids_row.shape[1], 128):
        piece = ids_row[:, start : start + 128].astype(wide)
        parts.append(jnp.transpose(jnp.broadcast_to(piece, (128, 128))))
    return jnp.concatenate(parts, axis=0)


def lanes(values):
    return [values[:, first : first + 128] for first in range(0, values.shape[1], 128)]


def variants(count):
    return [(2 * n, min(2 * n + 3, count)) for n in range(count // 2)]


def key_tile(ref, tile, half, side):
    rows = slice((tile % half) * tile_rows, (tile % half + 1) * tile_rows)
    return ref[(tile // half) ^ side, rows, :]


def allowed_part(ids_ref, ids_column, first):
    return ids_ref[:, first : first + 128].astype(wide) <= ids_column


def row_tile(half, shift):
    return lambda i, c: jnp.clip(i - half * (c[0] ^ shift), 0, half - 1)


def attend_forward_body(
    count, half, col_ref, q_ref, k_ref, v_ref, ids_ref, own_ref, other_ref, lse_ref, s_ref
):
    step = pl.program_id(1)
    side = col_ref[0]
    lane = lax.broadcasted_iota(jnp.int32, (tile_rows, 128), 1)
    own_ids = ids_ref[:, pl.ds(pl.multiple_of(step * tile_rows, tile_rows), tile_rows)]

    def groups(values):
        return values.reshape(tile_rows // 8, 8, tile_rows)

    def variant(open_tiles, keys):
        query = q_ref[...]
        query_ids = own_ids.astype(wide)
        masks = {}
        for tile in range(open_tiles, keys):
            column = column_of(ids_ref[:, tile * tile_rows : (tile + 1) * tile_rows])
            masks[tile] = jnp.concatenate([column, column], axis=1) <= query_ids
        mixed = []
        for head in range(2):
            mine = lane // HEAD_DIM == head
            part = jnp.where(mine, query, jnp.zeros_like(query)) * jnp.asarray(0.125, low)
            top = None
            for tile in range(keys):
                scores = dot_nt(key_tile(k_ref, tile, half, side), part)
                if tile >= open_tiles:
                    scores = jnp.where(masks[tile], scores, masked_score)
                s_ref[head, tile * tile_rows : (tile + 1) * tile_rows, :] = scores
                peak = jnp.max(groups(scores), axis=0)
                top = peak if top is None else jnp.maximum(top, peak)
            top = jnp.max(top, axis=0, keepdims=True)
            total = None
            acc = None
            for tile in range(keys):
                expo = jnp.exp(s_ref[head, tile * tile_rows : (tile + 1) * tile_rows, :] - top)
                piece = jnp.sum(groups(expo), axis=0)
                total = piece if total is None else total + piece
                columns = slice((tile % half) * tile_rows, (tile % half + 1) * tile_rows)
                values = v_ref[
                    (tile // half) ^ side, head * HEAD_DIM : (head + 1) * HEAD_DIM, columns
                ]
                piece = dot_nn(values, expo.astype(low))
                acc = piece if acc is None else acc + piece
            total = jnp.sum(total, axis=0, keepdims=True)
            mixed.append(acc / total)
            lse_ref[head : head + 1, :] = top + jnp.log(total)
        out = jnp.transpose(jnp.concatenate(mixed, axis=0)).astype(low)
        owned = (step // half) ^ side == 0

        @pl.when(owned)
        def _():
            own_ref[...] = out

        @pl.when(jnp.logical_not(owned))
        def _():
            other_ref[...] = out

    for n, bounds in enumerate(variants(count)):
        pl.when(step // 2 == n)(functools.partial(variant, *bounds))


def attend_forward(meta, qkv, values_turned, ids, first, pairs):
    sides, rows, _ = qkv.shape
    length = sides * rows
    count = length // tile_rows
    half = rows // tile_rows
    head_cols = 128 * pairs
    own, other = row_tile(half, 0), row_tile(half, 1)
    return pl.pallas_call(
        functools.partial(attend_forward_body, count, half),
        grid_spec=pltpu.PrefetchScalarGridSpec(
            num_scalar_prefetch=1,
            grid=(pairs, count),
            in_specs=[
                pl.BlockSpec(
                    (None, tile_rows, 128),
                    lambda h, i, c: ((i // half) ^ c[0], i % half, 3 * (h + first)),
                ),
                pl.BlockSpec((sides, rows, 128), lambda h, i, c: (0, 0, 3 * (h + first) + 1)),
                pl.BlockSpec((sides, 128, rows), lambda h, i, c: (0, h + first, 0)),
                pl.BlockSpec((1, length), lambda h, i, c: (0, 0)),
            ],
            out_specs=[
                pl.BlockSpec((tile_rows, 128), lambda h, i, c: (own(i, c), h)),
                pl.BlockSpec((tile_rows, 128), lambda h, i, c: (other(i, c), h)),
                pl.BlockSpec((None, 2, tile_rows), lambda h, i, c: (h, 0, i)),
            ],
            scratch_shapes=[pltpu.VMEM((2, length, tile_rows), wide)],
        ),
        out_shape=[
            jax.ShapeDtypeStruct((rows, head_cols), low),
            jax.ShapeDtypeStruct((rows, head_cols), low),
            jax.ShapeDtypeStruct((pairs, 2, length), wide),
        ],
        cost_estimate=cost(14 * pairs),
        name="attend_forward",
    )(meta, qkv, qkv, values_turned, ids)


def attend_backward_body(
    count, half, col_ref, q_ref, k_ref, v_ref, g_ref, g_other_ref, ids_ref, lse_ref,
    own_ref, other_ref, sum_ref, p_ref, gp_ref, low_ref, gq_ref, gk_acc, gv_acc,
):
    step, head = pl.program_id(1), pl.program_id(2)
    side = col_ref[0]
    lane = lax.broadcasted_iota(jnp.int32, (tile_rows, 128), 1)
    mine = lane // HEAD_DIM == head
    own_ids = ids_ref[:, pl.ds(pl.multiple_of(step * tile_rows, tile_rows), tile_rows)]

    def store(tile, place, values):
        start = pl.multiple_of((tile % half) * tile_rows, tile_rows)
        here = (pl.ds(start, tile_rows), slice(place * 128, (place + 1) * 128))
        owned = (tile // half) ^ side == 0

        @pl.when(owned)
        def _():
            own_ref[here] = values

        @pl.when(jnp.logical_not(owned))
        def _():
            other_ref[here] = values

    @pl.when((step == 0) & (head == 0))
    def _():
        gk_acc[...] = jnp.zeros_like(gk_acc)
        gv_acc[...] = jnp.zeros_like(gv_acc)
        sum_ref[...] = jnp.zeros_like(sum_ref)

    def variant(open_tiles, keys):
        query = q_ref[...]
        grad = jnp.where((step // half) ^ side == 0, g_ref[...], g_other_ref[...])
        part = jnp.where(mine, query, jnp.zeros_like(query)) * jnp.asarray(0.125, low)
        grad_part = jnp.where(mine, grad, jnp.zeros_like(grad))
        start = pl.multiple_of(head * HEAD_DIM, HEAD_DIM)
        spot = pl.ds(start, HEAD_DIM)

        def turned(values):
            flat = jnp.transpose(values)
            return jnp.where(head == 0, flat[:HEAD_DIM], flat[HEAD_DIM:])

        query_turned, grad_turned = turned(query), turned(grad)
        ids_column = column_of(own_ids)
        log_sum = column_of(jnp.where(head == 0, lse_ref[:1, :], lse_ref[1:, :]))
        inner = None
        for tile in range(keys):
            first = tile * tile_rows
            here = slice(first, first + tile_rows)
            scores = lanes(dot_nt(part, key_tile(k_ref, tile, half, side)))
            grad_probs = dot_nt(grad_part, key_tile(v_ref, tile, half, side))
            gp_ref[:, here] = grad_probs
            lows = []
            for n, (values, slope) in enumerate(zip(scores, lanes(grad_probs))):
                at = first + 128 * n
                values = jnp.exp(values - log_sum)
                if tile >= open_tiles:
                    values = jnp.where(allowed_part(ids_ref, ids_column, at), values, 0.0)
                p_ref[:, at : at + 128] = values
                lows.append(values.astype(low))
                values = values * slope
                inner = values if inner is None else inner + values
            lows = jnp.concatenate(lows, axis=1)
            gv_acc[spot, here] += dot_nn(grad_turned, lows)
        inner = jnp.sum(inner, axis=1, keepdims=True)
        grad_query = None
        for tile in range(keys):
            here = slice(tile * tile_rows, (tile + 1) * tile_rows)
            slopes = (p_ref[:, here] * (gp_ref[:, here] - inner)).astype(low)
            piece = dot_nn(slopes, key_tile(k_ref, tile, half, side))
            grad_query = piece if grad_query is None else grad_query + piece
            gk_acc[spot, here] += dot_nn(query_turned, slopes)
        gq_ref[...] = jnp.where(mine, grad_query, gq_ref[...])

    for n, bounds in enumerate(variants(count)):
        pl.when(step // 2 == n)(functools.partial(variant, *bounds))

    @pl.when(head == 1)
    def _():
        out = (gq_ref[...] * 0.125).astype(low)
        store(step, 0, out)
        sum_ref[0:1, :] += jnp.sum(out.astype(wide), axis=0, keepdims=True)

    @pl.when((step == count - 1) & (head == 1))
    def _():
        def finish(tile, _):
            here = pl.ds(pl.multiple_of(tile * tile_rows, tile_rows), tile_rows)
            grad_key = jnp.transpose(gk_acc[:, here] * 0.125).astype(low)
            grad_value = jnp.transpose(gv_acc[:, here]).astype(low)
            store(tile, 1, grad_key)
            store(tile, 2, grad_value)
            sum_ref[1:2, :] += jnp.sum(grad_value.astype(wide), axis=0, keepdims=True)

        lax.fori_loop(0, count, finish, None)


def attend_backward(meta, qkv, grad, grad_other, ids, log_sums, first, pairs, lse_first):
    sides, rows, _ = qkv.shape
    length = sides * rows
    count = length // tile_rows
    half = rows // tile_rows
    own, other = row_tile(half, 0), row_tile(half, 1)
    whole = pl.BlockSpec((rows, 384), lambda h, i, e, c: (0, h))
    return pl.pallas_call(
        functools.partial(attend_backward_body, count, half),
        grid_spec=pltpu.PrefetchScalarGridSpec(
            num_scalar_prefetch=1,
            grid=(pairs, count, 2),
            in_specs=[
                pl.BlockSpec(
                    (None, tile_rows, 128),
                    lambda h, i, e, c: ((i // half) ^ c[0], i % half, 3 * (h + first)),
                ),
                pl.BlockSpec((sides, rows, 128), lambda h, i, e, c: (0, 0, 3 * (h + first) + 1)),
                pl.BlockSpec((sides, rows, 128), lambda h, i, e, c: (0, 0, 3 * (h + first) + 2)),
                pl.BlockSpec((tile_rows, 128), lambda h, i, e, c: (own(i, c), h + first)),
                pl.BlockSpec((tile_rows, 128), lambda h, i, e, c: (other(i, c), h + first)),
                pl.BlockSpec((1, length), lambda h, i, e, c: (0, 0)),
                pl.BlockSpec((None, 2, tile_rows), lambda h, i, e, c: (h + lse_first, 0, i)),
            ],
            out_specs=[whole, whole, pl.BlockSpec((8, 128), lambda h, i, e, c: (0, h))],
            scratch_shapes=[
                pltpu.VMEM((tile_rows, length), wide),
                pltpu.VMEM((tile_rows, length), wide),
                pltpu.VMEM((8, 128), low),
                pltpu.VMEM((tile_rows, 128), wide),
                pltpu.VMEM((128, length), wide),
                pltpu.VMEM((128, length), wide),
            ],
        ),
        out_shape=[jax.ShapeDtypeStruct((rows, 384 * pairs), low)] * 2
        + [jax.ShapeDtypeStruct((8, 128 * pairs), wide)],
        cost_estimate=cost(25 * pairs),
        name="attend_backward",
    )(meta, qkv, qkv, qkv, grad, grad_other, ids, log_sums)


def norm_parts(values):
    mean = jnp.mean(values, axis=-1, keepdims=True)
    centred = values - mean
    inverse = lax.rsqrt(jnp.mean(centred * centred, axis=-1, keepdims=True) + norm_eps)
    return centred * inverse, inverse


def norm_back(grad_normed, unit, inverse, gain):
    grad_unit = grad_normed * gain
    first_mean = jnp.mean(grad_unit, axis=-1, keepdims=True)
    second_mean = jnp.mean(grad_unit * unit, axis=-1, keepdims=True)
    return inverse * (grad_unit - first_mean - unit * second_mean)


erfc_terms = (
    -0.12664913241116757, 0.4719797697046255, -0.4849989149703286, 0.5173882238837517,
    -0.0742751946996765, 0.20647784419749105, 0.15044607588806108, 0.17042678586105697,
    0.16920458065681523,
)


def gelu_with_slope(values):
    turned = 1.0 / (1.0 + (0.3 * 0.5**0.5) * jnp.abs(values))
    bell = jnp.exp(-0.5 * (values * values))
    series = jnp.full_like(values, 0.5 * erfc_terms[0])
    for term in erfc_terms[1:]:
        series = series * turned + 0.5 * term
    tail = series * turned * bell
    below = jnp.where(values < 0.0, tail, 1.0 - tail)
    return values * below, below + values * (bell * (0.5 / jnp.pi) ** 0.5)


def swap(values, axis, distance):
    size = lax.axis_size(axis)
    return lax.ppermute(values, axis, [(i, i ^ distance) for i in range(size)])


def gather_near(shard):
    return swap(shard, "row", 1), swap(shard, "row", 2)


def gather_far(shard, from_x, from_y):
    cut = shard.shape[0] // 2
    first_xy = swap(from_x[:cut], "row", 2)
    second_xy = swap(from_y[cut:], "row", 1)
    return [(0, 0, shard), (1, 0, from_x), (2, 0, from_y), (3, 0, first_xy), (3, cut, second_xy)]


def piece_copies(layout, refs, target, row_index, shard_rows, sems):
    copies = []
    for n, ((distance, first, rows), ref) in enumerate(zip(layout, refs)):
        base = pl.multiple_of((row_index ^ distance) * shard_rows + first, 16)
        copies.append(pltpu.make_async_copy(ref, target.at[pl.ds(base, rows), :], sems.at[n]))
    return copies


def layout_of(pieces):
    return [(distance, first, piece.shape[0]) for distance, first, piece in pieces]


hbm = pl.BlockSpec(memory_space=pl.ANY)


def project_in_body(layout, tiles, meta_ref, mine_ref, other_ref, bias_ref, *rest):
    pieces = rest[: len(layout)]
    out_ref, turned_ref, values_ref, weight_out, weight, sems, out_sem = rest[len(layout) :]
    step = pl.program_id(0)
    keep = pltpu.make_async_copy(weight, weight_out, out_sem)

    def project(rows):
        out = (dot_nn(rows, weight[...]) + bias_ref[...]).astype(low)
        out_ref[...] = out
        turned_ref[...] = jnp.transpose(rows)
        for pair in range(out.shape[1] // 384):
            values = out[:, 384 * pair + 256 : 384 * (pair + 1)]
            values_ref[128 * pair : 128 * (pair + 1), :] = jnp.transpose(values)

    @pl.when(step == 0)
    def _():
        copies = piece_copies(layout, pieces, weight, meta_ref[1], weight.shape[0] // 4, sems)
        for copy in copies:
            copy.start()
        for copy in copies:
            copy.wait()
        keep.start()

    @pl.when(step < tiles)
    def _():
        project(mine_ref[...])

    @pl.when(step >= tiles)
    def _():
        project(other_ref[...])

    @pl.when(step == 2 * tiles - 1)
    def _():
        keep.wait()


def project_in(meta, mine, other, bias, pieces):
    rows, model = mine.shape
    size = 2 * tile_rows
    tiles = rows // size
    width = pieces[0][2].shape[1]
    return pl.pallas_call(
        functools.partial(project_in_body, layout_of(pieces), tiles),
        grid_spec=pltpu.PrefetchScalarGridSpec(
            num_scalar_prefetch=1,
            grid=(2 * tiles,),
            in_specs=[
                pl.BlockSpec((size, model), lambda i, m: (jnp.minimum(i, tiles - 1), 0)),
                pl.BlockSpec((size, model), lambda i, m: (jnp.maximum(i - tiles, 0), 0)),
                pl.BlockSpec((1, width), lambda i, m: (0, 0)),
            ]
            + [hbm] * len(pieces),
            out_specs=[
                pl.BlockSpec((None, size, width), lambda i, m: (i // tiles, i % tiles, 0)),
                pl.BlockSpec((model, size), lambda i, m: (0, i)),
                pl.BlockSpec((None, width // 3, size), lambda i, m: (i // tiles, 0, i % tiles)),
                hbm,
            ],
            scratch_shapes=[
                pltpu.VMEM((model, width), low),
                pltpu.SemaphoreType.DMA((len(pieces),)),
                pltpu.SemaphoreType.DMA(()),
            ],
        ),
        out_shape=[
            jax.ShapeDtypeStruct((2, rows, width), low),
            jax.ShapeDtypeStruct((model, 2 * rows), low),
            jax.ShapeDtypeStruct((2, width // 3, rows), low),
            jax.ShapeDtypeStruct((model, width), low),
        ],
        cost_estimate=cost(7),
        name="project_in",
    )(meta, mine, other, bias, *[piece for _, _, piece in pieces])


def load_weights(layout, pieces, weight, meta_ref, sems):
    copies = []
    for side in range(2):
        copies += piece_copies(
            layout, pieces[side], weight.at[side], meta_ref[1], weight.shape[1] // 4, sems.at[side]
        )
    for copy in copies:
        copy.start()
    for copy in copies:
        copy.wait()


hidden_chunk = 768


def feed_body(
    layout, head_cols, hidden_cols, meta_ref, tok_ref, row_ref, mixed_ref, mixed_last_ref,
    got_ref, got_last_ref, cot_ref, vec_ref, up_bias_ref, *rest,
):
    count = len(layout)
    pieces = (rest[:count], rest[count : 2 * count])
    (
        out_ref, hidden_ref, grad_ref, two_ref, cot_turned_ref, branch_ref, middle_ref, own_ref,
        other_ref, sum_ref, bias_ref, weight, sems, mixer_ref, grad_two_ref,
    ) = rest[2 * count :]

    @pl.when(pl.program_id(0) == 0)
    def _():
        load_weights(layout, pieces, weight, meta_ref, sems)
        sum_ref[...] = jnp.zeros_like(sum_ref)
        bias_ref[...] = jnp.zeros_like(bias_ref)

    bias_out, gain, bias, bias_down = (vec_ref[n : n + 1, :] for n in range(4))
    cot = cot_ref[...]
    cot_turned_ref[...] = jnp.transpose(cot)
    start = tok_ref[...].astype(wide) + row_ref[...]
    cut = mixed_ref.shape[1]
    branch = dot_nt(mixed_ref[...], weight[0, :, :cut])
    branch = branch + dot_nt(mixed_last_ref[...], weight[0, :, cut:head_cols])
    branch = branch + dot_nt(got_ref[...], weight[1, :, :cut])
    branch = branch + dot_nt(got_last_ref[...], weight[1, :, cut:head_cols])
    middle = start + (branch + bias_out)
    unit, inverse = norm_parts(middle)
    two = (unit * gain + bias).astype(low)
    two_ref[...] = jnp.transpose(two)
    mixer_ref[...] = jnp.zeros_like(mixer_ref)
    grad_two_ref[...] = jnp.zeros_like(grad_two_ref)

    def visit(side, _):
        mixer = None
        grad_two = None
        for first in range(0, hidden_cols, hidden_chunk):
            here = slice(first, first + hidden_chunk)
            up = weight[side, :, head_cols + first : head_cols + first + hidden_chunk]
            at = head_cols + hidden_cols + first
            down = weight[side, :, at : at + hidden_chunk]
            hidden, slope = gelu_with_slope(dot_nn(two, up) + up_bias_ref[side, :, here])
            hidden = hidden.astype(low)
            hidden_ref[side, :, here] = hidden
            part = dot_nt(hidden, down)
            mixer = part if mixer is None else mixer + part
            grad_pre = (dot_nn(cot, down) * slope).astype(low)
            grad_ref[side, :, here] = grad_pre
            bias_ref[side, :, here] += jnp.sum(grad_pre.astype(wide), axis=0, keepdims=True)
            part = dot_nt(grad_pre, up)
            grad_two = part if grad_two is None else grad_two + part
        mixer_ref[...] += mixer
        grad_two_ref[...] += grad_two

    lax.fori_loop(0, 2, visit, None)
    mixer, grad_two = mixer_ref[...], grad_two_ref[...]
    out_ref[...] = (middle + (mixer + bias_down)).astype(low)
    cot = cot.astype(wide)
    grad_middle = cot + norm_back(grad_two, unit, inverse, gain)
    grad_branch = grad_middle.astype(low)
    middle_ref[...] = grad_middle
    branch_ref[...] = jnp.transpose(grad_branch)
    own_ref[...] = dot_nn(grad_branch, weight[0, :, :head_cols]).astype(low)
    other_ref[...] = dot_nn(grad_branch, weight[1, :, :head_cols]).astype(low)
    for n, values in enumerate((grad_branch.astype(wide), grad_two * unit, grad_two, cot)):
        sum_ref[n : n + 1, :] += jnp.sum(values, axis=0, keepdims=True)


def feed(meta, tokens, table_row, mixed, got, cot, vectors, up_bias, mine, other):
    rows, model = tokens.shape
    size = tile_rows
    head_cols = sum(part.shape[1] for part in mixed)
    hidden_cols = up_bias.shape[2]
    width = mine[0][2].shape[1]

    def tile(columns):
        return pl.BlockSpec((size, columns), lambda i, m: (i, 0))

    def fixed(*shape):
        return pl.BlockSpec(shape, lambda i, m: (0,) * len(shape))

    def turned(depth):
        return pl.BlockSpec((depth, size), lambda i, m: (0, i))

    def array(columns, dtype):
        return jax.ShapeDtypeStruct((rows, columns), dtype)

    flipped = jax.ShapeDtypeStruct((model, rows), low)
    return pl.pallas_call(
        functools.partial(feed_body, layout_of(mine), head_cols, hidden_cols),
        grid_spec=pltpu.PrefetchScalarGridSpec(
            num_scalar_prefetch=1,
            grid=(rows // size,),
            in_specs=[tile(model), fixed(1, model)]
            + [tile(part.shape[1]) for part in (*mixed, *got)]
            + [tile(model), fixed(8, model), fixed(2, 1, hidden_cols)]
            + [hbm] * (2 * len(mine)),
            out_specs=[tile(model)]
            + [pl.BlockSpec((2, size, hidden_cols), lambda i, m: (0, i, 0))] * 2
            + [turned(model)] * 3
            + [tile(model), tile(head_cols), tile(head_cols), fixed(8, model)]
            + [fixed(2, 1, hidden_cols)],
            scratch_shapes=[
                pltpu.VMEM((2, model, width), low),
                pltpu.SemaphoreType.DMA((2, len(mine))),
                pltpu.VMEM((size, model), wide),
                pltpu.VMEM((size, model), wide),
            ],
        ),
        out_shape=[array(model, low)]
        + [jax.ShapeDtypeStruct((2, rows, hidden_cols), low)] * 2
        + [flipped] * 3
        + [array(model, wide), array(head_cols, low), array(head_cols, low)]
        + [jax.ShapeDtypeStruct((8, model), wide)]
        + [jax.ShapeDtypeStruct((2, 1, hidden_cols), wide)],
        cost_estimate=cost(45),
        name="feed",
    )(
        meta, tokens, table_row, *mixed, *got, cot, vectors, up_bias,
        *[piece for _, _, piece in mine], *[piece for _, _, piece in other],
    )


def weight_parts_body(products, near, meta_ref, *refs):
    send_ref, keep_ref = refs[-2:]
    shard = send_ref.shape[0] // 2
    order = [pl.multiple_of((meta_ref[1] ^ d) * shard, 64) for d in (3, near, 3 - near, 0)]

    def in_order(ref):
        return jnp.concatenate([ref[pl.ds(start, shard), :] for start in order], axis=0)

    at = 0
    for lefts, arrived, first, tiles in products:
        inputs = refs[at : at + 2 * lefts + arrived]
        at += 2 * lefts + arrived

        @pl.when((pl.program_id(0) >= first) & (pl.program_id(0) < first + tiles))
        def _(inputs=inputs, lefts=lefts, arrived=arrived):
            total = None
            for n in range(lefts):
                part = dot_nn(in_order(inputs[2 * n]), inputs[2 * n + 1][...])
                total = part if total is None else total + part
            if arrived:
                total = total + in_order(inputs[-1]).astype(wide)
            total = total.astype(low)
            send_ref[...] = total[: 2 * shard]
            keep_ref[...] = total[2 * shard :]


def weight_parts(meta, products, near, micros):
    model = products[0][0][0][0].shape[0]
    operands, specs, shapes = [], [], []
    step = 384 if any(pairs[0][2].shape[-1] % 512 for pairs, _ in products) else 512
    first = 0
    for pairs, arrived in products:
        tiles = pairs[0][2].shape[-1] // step

        def tile(i, m, first=first, tiles=tiles):
            return (0, jnp.clip(i - first, 0, tiles - 1))

        for left, place, right in pairs:
            depth = right.shape[-2]
            specs.append(pl.BlockSpec((model, depth), lambda i, m, p=place: (0, p)))
            if right.ndim == 3:
                specs.append(pl.BlockSpec((None, depth, step), lambda i, m, t=tile: (0, *t(i, m))))
            else:
                specs.append(pl.BlockSpec((depth, step), tile))
            operands += [left, right]
        if arrived is not None:
            specs.append(pl.BlockSpec((model, step), tile))
            operands.append(arrived)
        shapes.append((len(pairs), int(arrived is not None), first, tiles))
        first += tiles
    half = jax.ShapeDtypeStruct((model // 2, first * step), low)
    return pl.pallas_call(
        functools.partial(weight_parts_body, shapes, near),
        grid_spec=pltpu.PrefetchScalarGridSpec(
            num_scalar_prefetch=1,
            grid=(first,),
            in_specs=specs,
            out_specs=[pl.BlockSpec((model // 2, step), lambda i, m: (0, i))] * 2,
        ),
        out_shape=[half, half],
        cost_estimate=cost(micros),
        name="weight_parts",
    )(meta, *operands)


def product_body(left_ref, right_ref, out_ref):
    out_ref[...] = dot_nn(left_ref[...], right_ref[...]).astype(low)


def product(left, right, micros):
    rows, depth = left.shape
    columns = right.shape[-1]
    step = 512 if columns % 512 == 0 else 384
    right_spec = pl.BlockSpec((depth, step), lambda i: (0, i))
    if right.ndim == 3:
        right_spec = pl.BlockSpec((None, depth, step), lambda i: (1, 0, i))
    return pl.pallas_call(
        product_body,
        grid=(columns // step,),
        in_specs=[pl.BlockSpec((rows, depth), lambda i: (0, 0)), right_spec],
        out_specs=pl.BlockSpec((rows, step), lambda i: (0, i)),
        out_shape=jax.ShapeDtypeStruct((rows, columns), low),
        cost_estimate=cost(micros),
        name="product",
    )(left, right)


def pack_body(*refs):
    out_ref = refs[-1]
    for n in range(out_ref.shape[1] // 128):
        kind, pair = n % 3, n // 3
        out_ref[:, 128 * n : 128 * (n + 1)] = refs[kind][:, 128 * pair : 128 * (pair + 1)].astype(low)


def pack(*weights):
    rows, columns = weights[0].shape
    return pl.pallas_call(
        pack_body,
        out_shape=jax.ShapeDtypeStruct((rows, 3 * columns), low),
        cost_estimate=cost(1),
        name="pack",
    )(*weights)


def grad_in_body(cuts, tok_ref, row_ref, gain_ref, own_ref, other_ref, middle_ref, *rest):
    grads = rest[: 2 * len(cuts)]
    out_ref, sum_ref = rest[2 * len(cuts) :]

    @pl.when(pl.program_id(0) == 0)
    def _():
        sum_ref[...] = jnp.zeros_like(sum_ref)

    grad = None
    for n, (first, last) in enumerate(cuts):
        for values, weight in ((grads[2 * n], own_ref), (grads[2 * n + 1], other_ref)):
            part = dot_nt(values[...], weight[:, first:last])
            grad = part if grad is None else grad + part
    unit, inverse = norm_parts(tok_ref[...].astype(wide) + row_ref[...])
    tokens = middle_ref[...] + norm_back(grad, unit, inverse, gain_ref[...])
    out_ref[...] = tokens
    for n, values in enumerate((grad * unit, grad, tokens)):
        sum_ref[n : n + 1, :] += jnp.sum(values, axis=0, keepdims=True)


def grad_in(tokens, table_row, gain, own, other, grad_middle, grads):
    rows, model = tokens.shape
    size = tile_rows
    width = own.shape[1]
    cuts = []
    for mine, _ in grads:
        first = cuts[-1][1] if cuts else 0
        cuts.append((first, first + mine.shape[1]))

    def tile(columns):
        return pl.BlockSpec((size, columns), lambda i: (i, 0))

    def fixed(*shape):
        return pl.BlockSpec(shape, lambda i: (0, 0))

    flat = [values for pair in grads for values in pair]
    return pl.pallas_call(
        functools.partial(grad_in_body, cuts),
        grid=(rows // size,),
        in_specs=[
            tile(model), fixed(1, model), fixed(1, model), fixed(model, width),
            fixed(model, width), tile(model),
        ]
        + [tile(values.shape[1]) for values in flat],
        out_specs=[tile(model), fixed(8, model)],
        out_shape=[
            jax.ShapeDtypeStruct((rows, model), wide),
            jax.ShapeDtypeStruct((8, model), wide),
        ],
        cost_estimate=cost(9),
        name="grad_in",
    )(tokens, table_row, gain, own, other, grad_middle, *flat)


def after(values, *needed):
    needed = jax.tree.leaves(needed)
    return lax.optimization_barrier((values, *needed))[0] if needed else values


def line_steps(values):
    if lax.axis_size("dp") != 4:
        return lax.psum(values, "dp")
    for distance in (1, 2):
        arrived = swap(values, "dp", distance)
        token = yield values
        arrived = after(arrived, token)
        values = (values.astype(wide) + arrived.astype(wide)).astype(values.dtype)
    return values


def split_line_steps(values):
    if lax.axis_size("dp") != 4:
        return lax.psum(values, "dp")
    me = lax.axis_index("dp")
    first, second = me % 2, me // 2
    half = values.shape[0] // 2

    def take(array, place, count):
        return lax.dynamic_slice_in_dim(array, place * count, count, 0)

    def join(place, mine, other):
        swapped = jnp.concatenate([other, mine], axis=0)
        return jnp.where(place == 0, jnp.concatenate([mine, other], axis=0), swapped)

    for place, distance in ((first, 1), (second, 2)):
        sent = take(values, 1 - place, half)
        arrived = swap(sent, "dp", distance)
        token = yield sent
        arrived = after(arrived, token)
        values = (take(values, place, half).astype(wide) + arrived.astype(wide)).astype(low)
        half //= 2
    for place, distance in ((second, 2), (first, 1)):
        arrived = swap(values, "dp", distance)
        token = yield values
        values = join(place, values, after(arrived, token))
    return values


def weight_steps(parts, near, line=line_steps):
    send, keep = parts
    shard = send.shape[0] // 2
    arrived = swap(send, "row", near)
    token = yield send
    arrived = after(arrived, token)
    passed = (keep[:shard].astype(wide) + arrived[:shard].astype(wide)).astype(low)
    last = swap(passed, "row", 3 - near)
    token = yield passed
    last = after(last, token)
    share = keep[shard:].astype(wide) + arrived[shard:].astype(wide) + last.astype(wide)
    total = yield from line(share.astype(low))
    return total.astype(wide)


def vector_steps(values):
    for axis, distance in (("row", 1), ("row", 2)):
        arrived = swap(values, axis, distance)
        token = yield values
        values = values + after(arrived, token)
    total = yield from line_steps(values)
    return total


class Chains:
    def __init__(self):
        self.steps, self.done = [], {}

    def add(self, steps):
        self.steps.append(steps)
        return [next(steps)]

    def advance(self, token=None, chosen=None):
        sent = []
        for n, steps in enumerate(self.steps):
            if n not in self.done and (chosen is None or n in chosen):
                try:
                    sent.append(steps.send(token))
                except StopIteration as stop:
                    self.done[n] = stop.value
        return sent


def shards(
    tokens, timesteps, block_ids, table, gain_one, bias_one, w_query, w_key, w_value, b_query,
    b_value, w_out, b_out, gain_two, bias_two, w_up, b_up, w_down, b_down, cotangent,
):
    seq_count, local_len, model_width = tokens.shape
    row_size, dp_size = lax.axis_size("row"), lax.axis_size("dp")
    assert seq_count == 1 and lax.axis_size("col") == 2 and row_size == 4
    head_cols = w_query.shape[1]
    hidden_cols = w_up.shape[1]
    col_index = lax.axis_index("col")
    row_index = lax.axis_index("row")
    seq_index = lax.axis_index("dp") * row_size + row_index
    seq_total = dp_size * row_size
    meta = jnp.stack([col_index, row_index]).astype(jnp.int32)

    cuts = [slice(first, first + 128) for first in range(0, head_cols, 128)]
    group_one = pack(w_query, w_key, w_value)
    in_bias = jnp.concatenate(
        [part for cut in cuts for part in (b_query[cut], jnp.zeros_like(b_query[cut]), b_value[cut])]
    )[None]
    in_pieces = gather_far(group_one, *gather_near(group_one))
    group_two = jnp.concatenate([w_out.T, w_up, w_down.T], axis=1).astype(low)
    group_two = after(group_two, in_pieces[3][2], in_pieces[4][2])
    near_x, near_y = gather_near(group_two)

    table_row = lax.dynamic_slice_in_dim(table, timesteps[0], 1, 0)
    unit_one, _ = norm_parts(tokens[0].astype(wide) + table_row)
    rows_mine = (unit_one * gain_one + bias_one).astype(low)
    rows_other = swap(rows_mine, "col", 1)
    up_bias = jnp.stack([b_up, swap(b_up, "col", 1)])[:, None]
    qkv, rows_turned, values_turned, in_own = project_in(
        meta, rows_mine, after(rows_other, up_bias), in_bias, in_pieces
    )
    in_other = swap(in_own, "col", 1)
    shard_other = swap(group_two, "col", 1)
    pairs = head_cols // 128
    mixed, mixed_other, log_sums = attend_forward(
        meta, qkv, values_turned, block_ids, 0, pairs - 1
    )
    got = swap(mixed_other, "col", 1)
    near_x, near_y = after(near_x, mixed), after(near_y, mixed)
    near_x_other, near_y_other = swap(near_x, "col", 1), swap(near_y, "col", 1)
    mine = gather_far(group_two, near_x, near_y)
    mixed_last, mixed_last_other, log_sums_last = attend_forward(
        meta, after(qkv, in_other, shard_other, got, near_x_other, near_y_other), values_turned,
        block_ids, pairs - 1, 1,
    )
    got_last = swap(mixed_last_other, "col", 1)
    far = [after(piece, mixed_last) for _, _, piece in mine[3:]]
    others = [shard_other, near_x_other, near_y_other] + [swap(piece, "col", 1) for piece in far]
    other = [(distance, first, piece) for (distance, first, _), piece in zip(mine, others)]

    spare = jnp.zeros_like(b_out)
    vectors = jnp.stack([b_out, gain_two, bias_two, b_down, spare, spare, spare, spare])
    cot = cotangent[0]
    (
        layer_out, hidden, grad_hidden, two_turned, cot_turned, branch_turned,
        grad_middle, grad_own, grad_other, sums, grad_up_bias,
    ) = feed(
        meta, tokens[0], table_row, (mixed, mixed_last), (got, got_last), cot, vectors, up_bias,
        mine, other,
    )
    up_arrived = swap(product(two_turned, grad_hidden, 4), "col", 1)
    down_arrived = swap(product(cot_turned, hidden, 4), "col", 1)
    grad_got = swap(grad_other, "col", 1)
    up_parts = weight_parts(meta, [([(two_turned, 0, grad_hidden)], up_arrived)], 1, 6)
    chains = Chains()
    chains.add(weight_steps(up_parts, 1, split_line_steps))
    down_parts = weight_parts(
        meta, [([(cot_turned, 0, hidden)], after(down_arrived, *up_parts))], 2, 6
    )
    chains.add(weight_steps(down_parts, 2, split_line_steps))
    grad_b_up = grad_up_bias[0, 0] + swap(grad_up_bias[1, 0], "col", 1)
    before = [*up_parts, *down_parts, grad_b_up]

    own_grads, aways, gots, bias_sums = [], [], [], []
    for pair in range(pairs):
        last = pair == pairs - 1
        own, away, bias_sum = attend_backward(
            meta, after(qkv, *before), grad_own, grad_got, block_ids,
            log_sums_last if last else log_sums, pair, 1, 0 if last else pair,
        )
        own_grads.append(own)
        gots.append(swap(away, "col", 1))
        bias_sums.append(bias_sum)
        before = [*chains.advance(own), gots[-1]]
        aways.append(away)
        if pair == 0:
            out_sent = product(
                branch_turned, after(jnp.concatenate([got, got_last], axis=1), *before), 2
            )
            out_arrived = swap(out_sent, "col", 1)
            before.append(out_sent)
            continue
        if pair == pairs - 2:
            out_keep = jnp.concatenate([mixed, mixed_last], axis=1)
            products = [([(branch_turned, 0, out_keep)], out_arrived)]
            ours, theirs = own_grads, aways
        else:
            products, ours, theirs = [], [own], [away]
        near = 1 if last else 2
        products += [([(rows_turned, 0, a), (rows_turned, 1, b)], None) for a, b in zip(ours, theirs)]
        parts = weight_parts(meta, products, near, 3 * len(products))
        before += parts
        chains.add(weight_steps(parts, near))
    grad_tokens, late_sums = grad_in(
        after(tokens[0], *before), table_row, gain_one[None], in_own, in_other, grad_middle,
        list(zip(own_grads, gots)),
    )
    sent = chains.advance(grad_tokens)

    shared = jnp.concatenate([late_sums[:3], sums[:4]])
    shared = shared + swap(shared, "col", 1)
    slot = lax.broadcasted_iota(jnp.int32, (seq_total, 1), 0) == seq_index
    packed = jnp.concatenate(
        [
            jnp.concatenate([shared[:2], shared[3:]]).reshape(-1),
            jnp.concatenate([part[:1] for part in bias_sums], axis=1).reshape(-1),
            jnp.concatenate([part[1:2] for part in bias_sums], axis=1).reshape(-1),
            grad_b_up,
            jnp.where(slot, shared[2:3], 0.0).reshape(-1),
            jnp.where(slot, timesteps[0].astype(wide), 0.0).reshape(-1),
        ]
    )
    pad = -packed.shape[0] % 1024
    chains.add(vector_steps(jnp.pad(packed, (0, pad)).reshape(-1, 128)))
    sent = chains.advance(sent, (2, 3, 4))
    sent = chains.advance(sent, (2, 3, 4))
    sent += chains.advance(sent, (0, 1))
    while not {2, 3, 4} <= set(chains.done):
        sent = chains.advance(sent, (2, 3, 4))
    chains.advance(chains.done[4])
    done = chains.done
    own_up, own_down = done[0], done[1]
    own_out, done[2] = done[2][:, :head_cols], done[2][:, head_cols:]
    own_in = jnp.concatenate([done[2], done[3]], axis=1)
    own_in = [
        jnp.concatenate([own_in[:, 128 * n : 128 * (n + 1)] for n in range(kind, 3 * pairs, 3)], axis=1)
        for kind in range(3)
    ]
    packed = done[4].reshape(-1)
    place = 0
    taken = []
    for size in (6 * model_width, 2 * head_cols, hidden_cols, seq_total * model_width, seq_total):
        taken.append(packed[place : place + size])
        place += size
    six = taken[0].reshape(6, model_width)
    step_onehot = (
        lax.broadcasted_iota(jnp.int32, (seq_total, table.shape[0]), 1)
        == taken[4][:, None].astype(jnp.int32)
    ).astype(wide)
    grad_table = jnp.einsum(
        "sv,sd->vd",
        step_onehot,
        taken[3].reshape(seq_total, model_width),
        precision=lax.Precision.HIGHEST,
        preferred_element_type=wide,
    )
    return (
        layer_out[None],
        grad_tokens[None],
        grad_table,
        six[0],
        six[1],
        own_in[0],
        own_in[1],
        own_in[2],
        taken[1][:head_cols],
        taken[1][head_cols:],
        own_out.T,
        six[2],
        six[3],
        six[4],
        own_up,
        taken[2],
        own_down.T,
        six[5],
    )


def solution(mesh):
    return jax.shard_map(
        shards,
        mesh=mesh,
        in_specs=(
            P(("dp", "row"), "col", None),
            P(("dp", "row")),
            P(("dp", "row"), None),
            P(),
            P(),
            P(),
            P("row", "col"),
            P("row", "col"),
            P("row", "col"),
            P("col"),
            P("col"),
            P("col", "row"),
            P(),
            P(),
            P(),
            P("row", "col"),
            P("col"),
            P("col", "row"),
            P(),
            P(("dp", "row"), "col", None),
        ),
        out_specs=(
            P(("dp", "row"), "col", None),
            P(("dp", "row"), "col", None),
            P(),
            P(),
            P(),
            P("row", "col"),
            P("row", "col"),
            P("row", "col"),
            P("col"),
            P("col"),
            P("col", "row"),
            P(),
            P(),
            P(),
            P("row", "col"),
            P("col"),
            P("col", "row"),
            P(),
        ),
        check_vma=False,
    )
```

```python
import functools

import jax
import jax.numpy as jnp
from jax import lax
from jax.experimental import pallas as pl
from jax.experimental.pallas import tpu as pltpu
from jax.sharding import PartitionSpec as P

HEAD_DIM = 64
norm_eps = 1e-05
masked_score = -1000000000.0
low = jnp.bfloat16
wide = jnp.float32
tile_rows = 256


def cost(micros):
    return pl.CostEstimate(flops=int(micros * 1.1e9), transcendentals=0, bytes_accessed=1 << 20)


def dot_nn(left, right):
    return lax.dot_general(left, right, (((1,), (0,)), ((), ())), preferred_element_type=wide)


def dot_nt(left, right):
    return lax.dot_general(left, right, (((1,), (1,)), ((), ())), preferred_element_type=wide)


def dot_tn(left, right):
    return lax.dot_general(left, right, (((0,), (0,)), ((), ())), preferred_element_type=wide)


def column_of(ids_row):
    parts = []
    for start in range(0, ids_row.shape[1], 128):
        piece = ids_row[:, start : start + 128].astype(wide)
        parts.append(jnp.transpose(jnp.broadcast_to(piece, (128, 128))))
    return jnp.concatenate(parts, axis=0)


def lanes(values):
    return [values[:, first : first + 128] for first in range(0, values.shape[1], 128)]


def variants(count):
    return [(2 * n, min(2 * n + 3, count)) for n in range(count // 2)]


def key_tile(ref, tile, half, side):
    rows = slice((tile % half) * tile_rows, (tile % half + 1) * tile_rows)
    return ref[(tile // half) ^ side, rows, :]


def allowed_part(ids_ref, ids_column, first):
    return ids_ref[:, first : first + 128].astype(wide) <= ids_column


def row_tile(half, shift):
    return lambda i, c: jnp.clip(i - half * (c[0] ^ shift), 0, half - 1)


def attend_forward_body(
    count, half, col_ref, q_ref, k_ref, v_ref, ids_ref, own_ref, other_ref, lse_ref, s_ref
):
    step = pl.program_id(1)
    side = col_ref[0]
    lane = lax.broadcasted_iota(jnp.int32, (tile_rows, 128), 1)
    own_ids = ids_ref[:, pl.ds(pl.multiple_of(step * tile_rows, tile_rows), tile_rows)]

    def groups(values):
        return values.reshape(tile_rows // 8, 8, tile_rows)

    def variant(open_tiles, keys):
        query = q_ref[...]
        query_ids = own_ids.astype(wide)
        masks = {}
        for tile in range(open_tiles, keys):
            column = column_of(ids_ref[:, tile * tile_rows : (tile + 1) * tile_rows])
            masks[tile] = jnp.concatenate([column, column], axis=1) <= query_ids
        mixed = []
        for head in range(2):
            mine = lane // HEAD_DIM == head
            part = jnp.where(mine, query, jnp.zeros_like(query)) * jnp.asarray(0.125, low)
            top = None
            for tile in range(keys):
                scores = dot_nt(key_tile(k_ref, tile, half, side), part)
                if tile >= open_tiles:
                    scores = jnp.where(masks[tile], scores, masked_score)
                s_ref[head, tile * tile_rows : (tile + 1) * tile_rows, :] = scores
                peak = jnp.max(groups(scores), axis=0)
                top = peak if top is None else jnp.maximum(top, peak)
            top = jnp.max(top, axis=0, keepdims=True)
            total = None
            acc = None
            for tile in range(keys):
                expo = jnp.exp(s_ref[head, tile * tile_rows : (tile + 1) * tile_rows, :] - top)
                piece = jnp.sum(groups(expo), axis=0)
                total = piece if total is None else total + piece
                columns = slice((tile % half) * tile_rows, (tile % half + 1) * tile_rows)
                values = v_ref[
                    (tile // half) ^ side, head * HEAD_DIM : (head + 1) * HEAD_DIM, columns
                ]
                piece = dot_nn(values, expo.astype(low))
                acc = piece if acc is None else acc + piece
            total = jnp.sum(total, axis=0, keepdims=True)
            mixed.append(acc / total)
            lse_ref[head : head + 1, :] = top + jnp.log(total)
        out = jnp.transpose(jnp.concatenate(mixed, axis=0)).astype(low)
        owned = (step // half) ^ side == 0

        @pl.when(owned)
        def _():
            own_ref[...] = out

        @pl.when(jnp.logical_not(owned))
        def _():
            other_ref[...] = out

    for n, bounds in enumerate(variants(count)):
        pl.when(step // 2 == n)(functools.partial(variant, *bounds))


def attend_forward(meta, qkv, values_turned, ids, first, pairs):
    sides, rows, _ = qkv.shape
    length = sides * rows
    count = length // tile_rows
    half = rows // tile_rows
    head_cols = 128 * pairs
    own, other = row_tile(half, 0), row_tile(half, 1)
    return pl.pallas_call(
        functools.partial(attend_forward_body, count, half),
        grid_spec=pltpu.PrefetchScalarGridSpec(
            num_scalar_prefetch=1,
            grid=(pairs, count),
            in_specs=[
                pl.BlockSpec(
                    (None, tile_rows, 128),
                    lambda h, i, c: ((i // half) ^ c[0], i % half, 3 * (h + first)),
                ),
                pl.BlockSpec((sides, rows, 128), lambda h, i, c: (0, 0, 3 * (h + first) + 1)),
                pl.BlockSpec((sides, 128, rows), lambda h, i, c: (0, h + first, 0)),
                pl.BlockSpec((1, length), lambda h, i, c: (0, 0)),
            ],
            out_specs=[
                pl.BlockSpec((tile_rows, 128), lambda h, i, c: (own(i, c), h)),
                pl.BlockSpec((tile_rows, 128), lambda h, i, c: (other(i, c), h)),
                pl.BlockSpec((None, 2, tile_rows), lambda h, i, c: (h, 0, i)),
            ],
            scratch_shapes=[pltpu.VMEM((2, length, tile_rows), wide)],
        ),
        out_shape=[
            jax.ShapeDtypeStruct((rows, head_cols), low),
            jax.ShapeDtypeStruct((rows, head_cols), low),
            jax.ShapeDtypeStruct((pairs, 2, length), wide),
        ],
        cost_estimate=cost(14 * pairs),
        name="attend_forward",
    )(meta, qkv, qkv, values_turned, ids)


def attend_backward_body(
    count, half, col_ref, q_ref, k_ref, v_ref, kt_ref, g_ref, g_other_ref, ids_ref, lse_ref,
    own_ref, other_ref, sum_ref, p_ref, gp_ref, gq_ref, gk_acc, gv_acc,
):
    step, head = pl.program_id(1), pl.program_id(2)
    side = col_ref[0]
    lane = lax.broadcasted_iota(jnp.int32, (tile_rows, 128), 1)
    mine = lane // HEAD_DIM == head
    own_ids = ids_ref[:, pl.ds(pl.multiple_of(step * tile_rows, tile_rows), tile_rows)]
    spot = pl.ds(pl.multiple_of(head * HEAD_DIM, HEAD_DIM), HEAD_DIM)

    def store(tile, place, values):
        start = pl.multiple_of((tile % half) * tile_rows, tile_rows)
        here = (pl.ds(start, tile_rows), slice(place * 128, (place + 1) * 128))
        owned = (tile // half) ^ side == 0

        @pl.when(owned)
        def _():
            own_ref[here] = values

        @pl.when(jnp.logical_not(owned))
        def _():
            other_ref[here] = values

    @pl.when((step == 0) & (head == 0))
    def _():
        gk_acc[...] = jnp.zeros_like(gk_acc)
        gv_acc[...] = jnp.zeros_like(gv_acc)
        sum_ref[...] = jnp.zeros_like(sum_ref)

    def groups(values):
        return jnp.sum(values.reshape(tile_rows // 8, 8, tile_rows), axis=0)

    def variant(open_tiles, keys):
        query = q_ref[...]
        grad = jnp.where((step // half) ^ side == 0, g_ref[...], g_other_ref[...])
        part = jnp.where(mine, query, jnp.zeros_like(query)) * jnp.asarray(0.125, low)
        grad_part = jnp.where(mine, grad, jnp.zeros_like(grad))
        query_ids = own_ids.astype(wide)
        log_sum = jnp.where(head == 0, lse_ref[:1, :], lse_ref[1:, :])
        inner = None
        for tile in range(keys):
            here = slice(tile * tile_rows, (tile + 1) * tile_rows)
            scores = dot_nt(key_tile(k_ref, tile, half, side), part)
            grad_probs = dot_nt(key_tile(v_ref, tile, half, side), grad_part)
            gp_ref[here, :] = grad_probs
            probs = jnp.exp(scores - log_sum)
            if tile >= open_tiles:
                column = column_of(ids_ref[:, here])
                allowed = jnp.concatenate([column, column], axis=1) <= query_ids
                probs = jnp.where(allowed, probs, 0.0)
            p_ref[here, :] = probs
            piece = groups(probs * grad_probs)
            inner = piece if inner is None else inner + piece
            gv_acc[here, :] += dot_nn(probs.astype(low), grad_part)
        inner = jnp.sum(inner, axis=0, keepdims=True)
        grad_query = None
        for tile in range(keys):
            here = slice(tile * tile_rows, (tile + 1) * tile_rows)
            columns = slice((tile % half) * tile_rows, (tile % half + 1) * tile_rows)
            slopes = (p_ref[here, :] * (gp_ref[here, :] - inner)).astype(low)
            gk_acc[here, :] += dot_nn(slopes, part)
            piece = dot_nn(kt_ref[(tile // half) ^ side, spot, columns], slopes)
            grad_query = piece if grad_query is None else grad_query + piece
        gq_ref[spot, :] = grad_query

    for n, bounds in enumerate(variants(count)):
        pl.when(step // 2 == n)(functools.partial(variant, *bounds))

    @pl.when(head == 1)
    def _():
        out = jnp.transpose(gq_ref[...] * 0.125).astype(low)
        store(step, 0, out)
        sum_ref[0:1, :] += jnp.sum(out.astype(wide), axis=0, keepdims=True)

    @pl.when((step == count - 1) & (head == 1))
    def _():
        def finish(tile, _):
            here = pl.ds(pl.multiple_of(tile * tile_rows, tile_rows), tile_rows)
            grad_value = gv_acc[here, :].astype(low)
            store(tile, 1, gk_acc[here, :].astype(low))
            store(tile, 2, grad_value)
            sum_ref[1:2, :] += jnp.sum(grad_value.astype(wide), axis=0, keepdims=True)

        lax.fori_loop(0, count, finish, None)


def attend_backward(
    meta, qkv, keys_turned, grad, grad_other, ids, log_sums, first, pairs, lse_first
):
    sides, rows, _ = qkv.shape
    length = sides * rows
    count = length // tile_rows
    half = rows // tile_rows
    own, other = row_tile(half, 0), row_tile(half, 1)
    whole = pl.BlockSpec((rows, 384), lambda h, i, e, c: (0, h))
    return pl.pallas_call(
        functools.partial(attend_backward_body, count, half),
        grid_spec=pltpu.PrefetchScalarGridSpec(
            num_scalar_prefetch=1,
            grid=(pairs, count, 2),
            in_specs=[
                pl.BlockSpec(
                    (None, tile_rows, 128),
                    lambda h, i, e, c: ((i // half) ^ c[0], i % half, 3 * (h + first)),
                ),
                pl.BlockSpec((sides, rows, 128), lambda h, i, e, c: (0, 0, 3 * (h + first) + 1)),
                pl.BlockSpec((sides, rows, 128), lambda h, i, e, c: (0, 0, 3 * (h + first) + 2)),
                pl.BlockSpec((sides, 128, rows), lambda h, i, e, c: (0, h + first, 0)),
                pl.BlockSpec((tile_rows, 128), lambda h, i, e, c: (own(i, c), h + first)),
                pl.BlockSpec((tile_rows, 128), lambda h, i, e, c: (other(i, c), h + first)),
                pl.BlockSpec((1, length), lambda h, i, e, c: (0, 0)),
                pl.BlockSpec((None, 2, tile_rows), lambda h, i, e, c: (h + lse_first, 0, i)),
            ],
            out_specs=[whole, whole, pl.BlockSpec((8, 128), lambda h, i, e, c: (0, h))],
            scratch_shapes=[
                pltpu.VMEM((length, tile_rows), wide),
                pltpu.VMEM((length, tile_rows), wide),
                pltpu.VMEM((128, tile_rows), wide),
                pltpu.VMEM((length, 128), wide),
                pltpu.VMEM((length, 128), wide),
            ],
        ),
        out_shape=[jax.ShapeDtypeStruct((rows, 384 * pairs), low)] * 2
        + [jax.ShapeDtypeStruct((8, 128 * pairs), wide)],
        cost_estimate=cost(25 * pairs),
        name="attend_backward",
    )(meta, qkv, qkv, qkv, keys_turned, grad, grad_other, ids, log_sums)


def norm_parts(values):
    mean = jnp.mean(values, axis=-1, keepdims=True)
    centred = values - mean
    inverse = lax.rsqrt(jnp.mean(centred * centred, axis=-1, keepdims=True) + norm_eps)
    return centred * inverse, inverse


def norm_back(grad_normed, unit, inverse, gain):
    grad_unit = grad_normed * gain
    first_mean = jnp.mean(grad_unit, axis=-1, keepdims=True)
    second_mean = jnp.mean(grad_unit * unit, axis=-1, keepdims=True)
    return inverse * (grad_unit - first_mean - unit * second_mean)


erfc_terms = (
    -0.12664913241116757, 0.4719797697046255, -0.4849989149703286, 0.5173882238837517,
    -0.0742751946996765, 0.20647784419749105, 0.15044607588806108, 0.17042678586105697,
    0.16920458065681523,
)


def gelu_with_slope(values):
    turned = 1.0 / (1.0 + (0.3 * 0.5**0.5) * jnp.abs(values))
    bell = jnp.exp(-0.5 * (values * values))
    series = jnp.full_like(values, 0.5 * erfc_terms[0])
    for term in erfc_terms[1:]:
        series = series * turned + 0.5 * term
    tail = series * turned * bell
    below = jnp.where(values < 0.0, tail, 1.0 - tail)
    return values * below, below + values * (bell * (0.5 / jnp.pi) ** 0.5)


def swap(values, axis, distance):
    size = lax.axis_size(axis)
    return lax.ppermute(values, axis, [(i, i ^ distance) for i in range(size)])


def gather_near(shard):
    return swap(shard, "row", 1), swap(shard, "row", 2)


def gather_far(shard, from_x, from_y):
    cut = shard.shape[0] // 2
    first_xy = swap(from_x[:cut], "row", 2)
    second_xy = swap(from_y[cut:], "row", 1)
    return [(0, 0, shard), (1, 0, from_x), (2, 0, from_y), (3, 0, first_xy), (3, cut, second_xy)]


def piece_copies(layout, refs, target, row_index, shard_rows, sems):
    copies = []
    for n, ((distance, first, rows), ref) in enumerate(zip(layout, refs)):
        base = pl.multiple_of((row_index ^ distance) * shard_rows + first, 16)
        copies.append(pltpu.make_async_copy(ref, target.at[pl.ds(base, rows), :], sems.at[n]))
    return copies


def layout_of(pieces):
    return [(distance, first, piece.shape[0]) for distance, first, piece in pieces]


hbm = pl.BlockSpec(memory_space=pl.ANY)


def project_in_body(layout, tiles, meta_ref, mine_ref, other_ref, bias_ref, *rest):
    pieces = rest[: len(layout)]
    out_ref, turned_ref, keys_ref, values_ref, weight_out, weight, sems, out_sem = rest[len(layout) :]
    step = pl.program_id(0)
    keep = pltpu.make_async_copy(weight, weight_out, out_sem)

    def project(rows):
        out = (dot_nn(rows, weight[...]) + bias_ref[...]).astype(low)
        out_ref[...] = out
        turned_ref[...] = jnp.transpose(rows)
        for pair in range(out.shape[1] // 384):
            here = slice(128 * pair, 128 * (pair + 1))
            keys_ref[here, :] = jnp.transpose(out[:, 384 * pair + 128 : 384 * pair + 256])
            values_ref[here, :] = jnp.transpose(out[:, 384 * pair + 256 : 384 * (pair + 1)])

    @pl.when(step == 0)
    def _():
        copies = piece_copies(layout, pieces, weight, meta_ref[1], weight.shape[0] // 4, sems)
        for copy in copies:
            copy.start()
        for copy in copies:
            copy.wait()
        keep.start()

    @pl.when(step < tiles)
    def _():
        project(mine_ref[...])

    @pl.when(step >= tiles)
    def _():
        project(other_ref[...])

    @pl.when(step == 2 * tiles - 1)
    def _():
        keep.wait()


def project_in(meta, mine, other, bias, pieces):
    rows, model = mine.shape
    size = 2 * tile_rows
    tiles = rows // size
    width = pieces[0][2].shape[1]
    return pl.pallas_call(
        functools.partial(project_in_body, layout_of(pieces), tiles),
        grid_spec=pltpu.PrefetchScalarGridSpec(
            num_scalar_prefetch=1,
            grid=(2 * tiles,),
            in_specs=[
                pl.BlockSpec((size, model), lambda i, m: (jnp.minimum(i, tiles - 1), 0)),
                pl.BlockSpec((size, model), lambda i, m: (jnp.maximum(i - tiles, 0), 0)),
                pl.BlockSpec((1, width), lambda i, m: (0, 0)),
            ]
            + [hbm] * len(pieces),
            out_specs=[
                pl.BlockSpec((None, size, width), lambda i, m: (i // tiles, i % tiles, 0)),
                pl.BlockSpec((model, size), lambda i, m: (0, i)),
                pl.BlockSpec((None, width // 3, size), lambda i, m: (i // tiles, 0, i % tiles)),
                pl.BlockSpec((None, width // 3, size), lambda i, m: (i // tiles, 0, i % tiles)),
                hbm,
            ],
            scratch_shapes=[
                pltpu.VMEM((model, width), low),
                pltpu.SemaphoreType.DMA((len(pieces),)),
                pltpu.SemaphoreType.DMA(()),
            ],
        ),
        out_shape=[
            jax.ShapeDtypeStruct((2, rows, width), low),
            jax.ShapeDtypeStruct((model, 2 * rows), low),
            jax.ShapeDtypeStruct((2, width // 3, rows), low),
            jax.ShapeDtypeStruct((2, width // 3, rows), low),
            jax.ShapeDtypeStruct((model, width), low),
        ],
        cost_estimate=cost(7),
        name="project_in",
    )(meta, mine, other, bias, *[piece for _, _, piece in pieces])


def load_weights(layout, pieces, weight, meta_ref, sems):
    copies = []
    for side in range(2):
        copies += piece_copies(
            layout, pieces[side], weight.at[side], meta_ref[1], weight.shape[1] // 4, sems.at[side]
        )
    for copy in copies:
        copy.start()
    for copy in copies:
        copy.wait()


hidden_chunk = 768


def feed_body(
    layout, head_cols, hidden_cols, meta_ref, tok_ref, row_ref, mixed_ref, mixed_last_ref,
    got_ref, got_last_ref, cot_ref, vec_ref, up_bias_ref, *rest,
):
    count = len(layout)
    pieces = (rest[:count], rest[count : 2 * count])
    (
        out_ref, hidden_ref, grad_ref, two_ref, cot_turned_ref, branch_ref, middle_ref, own_ref,
        other_ref, sum_ref, bias_ref, weight, sems, mixer_ref, grad_two_ref,
    ) = rest[2 * count :]

    @pl.when(pl.program_id(0) == 0)
    def _():
        load_weights(layout, pieces, weight, meta_ref, sems)
        sum_ref[...] = jnp.zeros_like(sum_ref)
        bias_ref[...] = jnp.zeros_like(bias_ref)

    bias_out, gain, bias, bias_down = (vec_ref[n : n + 1, :] for n in range(4))
    cot = cot_ref[...]
    cot_turned_ref[...] = jnp.transpose(cot)
    start = tok_ref[...].astype(wide) + row_ref[...]
    cut = mixed_ref.shape[1]
    branch = dot_nt(mixed_ref[...], weight[0, :, :cut])
    branch = branch + dot_nt(mixed_last_ref[...], weight[0, :, cut:head_cols])
    branch = branch + dot_nt(got_ref[...], weight[1, :, :cut])
    branch = branch + dot_nt(got_last_ref[...], weight[1, :, cut:head_cols])
    middle = start + (branch + bias_out)
    unit, inverse = norm_parts(middle)
    two = (unit * gain + bias).astype(low)
    two_ref[...] = jnp.transpose(two)
    mixer_ref[...] = jnp.zeros_like(mixer_ref)
    grad_two_ref[...] = jnp.zeros_like(grad_two_ref)

    def visit(side, _):
        mixer = None
        grad_two = None
        for first in range(0, hidden_cols, hidden_chunk):
            here = slice(first, first + hidden_chunk)
            up = weight[side, :, head_cols + first : head_cols + first + hidden_chunk]
            at = head_cols + hidden_cols + first
            down = weight[side, :, at : at + hidden_chunk]
            hidden, slope = gelu_with_slope(dot_nn(two, up) + up_bias_ref[side, :, here])
            hidden = hidden.astype(low)
            hidden_ref[side, :, here] = hidden
            part = dot_nt(hidden, down)
            mixer = part if mixer is None else mixer + part
            grad_pre = (dot_nn(cot, down) * slope).astype(low)
            grad_ref[side, :, here] = grad_pre
            bias_ref[side, :, here] += jnp.sum(grad_pre.astype(wide), axis=0, keepdims=True)
            part = dot_nt(grad_pre, up)
            grad_two = part if grad_two is None else grad_two + part
        mixer_ref[...] += mixer
        grad_two_ref[...] += grad_two

    lax.fori_loop(0, 2, visit, None)
    mixer, grad_two = mixer_ref[...], grad_two_ref[...]
    out_ref[...] = (middle + (mixer + bias_down)).astype(low)
    cot = cot.astype(wide)
    grad_middle = cot + norm_back(grad_two, unit, inverse, gain)
    grad_branch = grad_middle.astype(low)
    middle_ref[...] = grad_middle
    branch_ref[...] = jnp.transpose(grad_branch)
    own_ref[...] = dot_nn(grad_branch, weight[0, :, :head_cols]).astype(low)
    other_ref[...] = dot_nn(grad_branch, weight[1, :, :head_cols]).astype(low)
    for n, values in enumerate((grad_branch.astype(wide), grad_two * unit, grad_two, cot)):
        sum_ref[n : n + 1, :] += jnp.sum(values, axis=0, keepdims=True)


def feed(meta, tokens, table_row, mixed, got, cot, vectors, up_bias, mine, other):
    rows, model = tokens.shape
    size = tile_rows
    head_cols = sum(part.shape[1] for part in mixed)
    hidden_cols = up_bias.shape[2]
    width = mine[0][2].shape[1]

    def tile(columns):
        return pl.BlockSpec((size, columns), lambda i, m: (i, 0))

    def fixed(*shape):
        return pl.BlockSpec(shape, lambda i, m: (0,) * len(shape))

    def turned(depth):
        return pl.BlockSpec((depth, size), lambda i, m: (0, i))

    def array(columns, dtype):
        return jax.ShapeDtypeStruct((rows, columns), dtype)

    flipped = jax.ShapeDtypeStruct((model, rows), low)
    return pl.pallas_call(
        functools.partial(feed_body, layout_of(mine), head_cols, hidden_cols),
        grid_spec=pltpu.PrefetchScalarGridSpec(
            num_scalar_prefetch=1,
            grid=(rows // size,),
            in_specs=[tile(model), fixed(1, model)]
            + [tile(part.shape[1]) for part in (*mixed, *got)]
            + [tile(model), fixed(8, model), fixed(2, 1, hidden_cols)]
            + [hbm] * (2 * len(mine)),
            out_specs=[tile(model)]
            + [pl.BlockSpec((2, size, hidden_cols), lambda i, m: (0, i, 0))] * 2
            + [turned(model)] * 3
            + [tile(model), tile(head_cols), tile(head_cols), fixed(8, model)]
            + [fixed(2, 1, hidden_cols)],
            scratch_shapes=[
                pltpu.VMEM((2, model, width), low),
                pltpu.SemaphoreType.DMA((2, len(mine))),
                pltpu.VMEM((size, model), wide),
                pltpu.VMEM((size, model), wide),
            ],
        ),
        out_shape=[array(model, low)]
        + [jax.ShapeDtypeStruct((2, rows, hidden_cols), low)] * 2
        + [flipped] * 3
        + [array(model, wide), array(head_cols, low), array(head_cols, low)]
        + [jax.ShapeDtypeStruct((8, model), wide)]
        + [jax.ShapeDtypeStruct((2, 1, hidden_cols), wide)],
        cost_estimate=cost(45),
        name="feed",
    )(
        meta, tokens, table_row, *mixed, *got, cot, vectors, up_bias,
        *[piece for _, _, piece in mine], *[piece for _, _, piece in other],
    )


def weight_parts_body(products, near, meta_ref, *refs):
    send_ref, keep_ref = refs[-2:]
    shard = send_ref.shape[0] // 2
    order = [pl.multiple_of((meta_ref[1] ^ d) * shard, 64) for d in (3, near, 3 - near, 0)]

    def in_order(ref):
        return jnp.concatenate([ref[pl.ds(start, shard), :] for start in order], axis=0)

    at = 0
    for lefts, arrived, first, tiles in products:
        inputs = refs[at : at + 2 * lefts + arrived]
        at += 2 * lefts + arrived

        @pl.when((pl.program_id(0) >= first) & (pl.program_id(0) < first + tiles))
        def _(inputs=inputs, lefts=lefts, arrived=arrived):
            total = None
            for n in range(lefts):
                part = dot_nn(in_order(inputs[2 * n]), inputs[2 * n + 1][...])
                total = part if total is None else total + part
            if arrived:
                total = total + in_order(inputs[-1]).astype(wide)
            total = total.astype(low)
            send_ref[...] = total[: 2 * shard]
            keep_ref[...] = total[2 * shard :]


def weight_parts(meta, products, near, micros):
    model = products[0][0][0][0].shape[0]
    operands, specs, shapes = [], [], []
    step = 384 if any(pairs[0][2].shape[-1] % 512 for pairs, _ in products) else 512
    first = 0
    for pairs, arrived in products:
        tiles = pairs[0][2].shape[-1] // step

        def tile(i, m, first=first, tiles=tiles):
            return (0, jnp.clip(i - first, 0, tiles - 1))

        for left, place, right in pairs:
            depth = right.shape[-2]
            specs.append(pl.BlockSpec((model, depth), lambda i, m, p=place: (0, p)))
            if right.ndim == 3:
                specs.append(pl.BlockSpec((None, depth, step), lambda i, m, t=tile: (0, *t(i, m))))
            else:
                specs.append(pl.BlockSpec((depth, step), tile))
            operands += [left, right]
        if arrived is not None:
            specs.append(pl.BlockSpec((model, step), tile))
            operands.append(arrived)
        shapes.append((len(pairs), int(arrived is not None), first, tiles))
        first += tiles
    half = jax.ShapeDtypeStruct((model // 2, first * step), low)
    return pl.pallas_call(
        functools.partial(weight_parts_body, shapes, near),
        grid_spec=pltpu.PrefetchScalarGridSpec(
            num_scalar_prefetch=1,
            grid=(first,),
            in_specs=specs,
            out_specs=[pl.BlockSpec((model // 2, step), lambda i, m: (0, i))] * 2,
        ),
        out_shape=[half, half],
        cost_estimate=cost(micros),
        name="weight_parts",
    )(meta, *operands)


def product_body(left_ref, right_ref, out_ref):
    out_ref[...] = dot_nn(left_ref[...], right_ref[...]).astype(low)


def product(left, right, micros):
    rows, depth = left.shape
    columns = right.shape[-1]
    step = 512 if columns % 512 == 0 else 384
    right_spec = pl.BlockSpec((depth, step), lambda i: (0, i))
    if right.ndim == 3:
        right_spec = pl.BlockSpec((None, depth, step), lambda i: (1, 0, i))
    return pl.pallas_call(
        product_body,
        grid=(columns // step,),
        in_specs=[pl.BlockSpec((rows, depth), lambda i: (0, 0)), right_spec],
        out_specs=pl.BlockSpec((rows, step), lambda i: (0, i)),
        out_shape=jax.ShapeDtypeStruct((rows, columns), low),
        cost_estimate=cost(micros),
        name="product",
    )(left, right)


def table_body(step_ref, sum_ref, out_ref):
    out_ref[...] = jnp.zeros_like(out_ref)

    def add(n, _):
        out_ref[pl.ds(step_ref[n], 1), :] += sum_ref[pl.ds(n, 1), :]

    lax.fori_loop(0, sum_ref.shape[0], add, None)


def table_rows(steps, sums, rows):
    return pl.pallas_call(
        table_body,
        grid_spec=pltpu.PrefetchScalarGridSpec(
            num_scalar_prefetch=1,
            grid=(1,),
            in_specs=[pl.BlockSpec(sums.shape, lambda i, t: (0, 0))],
            out_specs=pl.BlockSpec((rows, sums.shape[1]), lambda i, t: (0, 0)),
        ),
        out_shape=jax.ShapeDtypeStruct((rows, sums.shape[1]), wide),
        cost_estimate=cost(2),
        name="table_rows",
    )(steps, sums)


def pack_body(*refs):
    out_ref = refs[-1]
    for n in range(out_ref.shape[1] // 128):
        kind, pair = n % 3, n // 3
        out_ref[:, 128 * n : 128 * (n + 1)] = refs[kind][:, 128 * pair : 128 * (pair + 1)].astype(low)


def pack(*weights):
    rows, columns = weights[0].shape
    return pl.pallas_call(
        pack_body,
        out_shape=jax.ShapeDtypeStruct((rows, 3 * columns), low),
        cost_estimate=cost(1),
        name="pack",
    )(*weights)


def grad_in_body(cuts, tok_ref, row_ref, gain_ref, own_ref, other_ref, middle_ref, *rest):
    grads = rest[: 2 * len(cuts)]
    out_ref, sum_ref = rest[2 * len(cuts) :]

    @pl.when(pl.program_id(0) == 0)
    def _():
        sum_ref[...] = jnp.zeros_like(sum_ref)

    grad = None
    for n, (first, last) in enumerate(cuts):
        for values, weight in ((grads[2 * n], own_ref), (grads[2 * n + 1], other_ref)):
            part = dot_nt(values[...], weight[:, first:last])
            grad = part if grad is None else grad + part
    unit, inverse = norm_parts(tok_ref[...].astype(wide) + row_ref[...])
    tokens = middle_ref[...] + norm_back(grad, unit, inverse, gain_ref[...])
    out_ref[...] = tokens
    for n, values in enumerate((grad * unit, grad, tokens)):
        sum_ref[n : n + 1, :] += jnp.sum(values, axis=0, keepdims=True)


def grad_in(tokens, table_row, gain, own, other, grad_middle, grads):
    rows, model = tokens.shape
    size = tile_rows
    width = own.shape[1]
    cuts = []
    for mine, _ in grads:
        first = cuts[-1][1] if cuts else 0
        cuts.append((first, first + mine.shape[1]))

    def tile(columns):
        return pl.BlockSpec((size, columns), lambda i: (i, 0))

    def fixed(*shape):
        return pl.BlockSpec(shape, lambda i: (0, 0))

    flat = [values for pair in grads for values in pair]
    return pl.pallas_call(
        functools.partial(grad_in_body, cuts),
        grid=(rows // size,),
        in_specs=[
            tile(model), fixed(1, model), fixed(1, model), fixed(model, width),
            fixed(model, width), tile(model),
        ]
        + [tile(values.shape[1]) for values in flat],
        out_specs=[tile(model), fixed(8, model)],
        out_shape=[
            jax.ShapeDtypeStruct((rows, model), wide),
            jax.ShapeDtypeStruct((8, model), wide),
        ],
        cost_estimate=cost(9),
        name="grad_in",
    )(tokens, table_row, gain, own, other, grad_middle, *flat)


def after(values, *needed):
    needed = jax.tree.leaves(needed)
    return lax.optimization_barrier((values, *needed))[0] if needed else values


def line_steps(values):
    if lax.axis_size("dp") != 4:
        return lax.psum(values, "dp")
    for distance in (1, 2):
        arrived = swap(values, "dp", distance)
        token = yield values
        arrived = after(arrived, token)
        values = (values.astype(wide) + arrived.astype(wide)).astype(values.dtype)
    return values


def split_line_steps(values):
    if lax.axis_size("dp") != 4:
        return lax.psum(values, "dp")
    me = lax.axis_index("dp")
    first, second = me % 2, me // 2
    half = values.shape[0] // 2

    def take(array, place, count):
        return lax.dynamic_slice_in_dim(array, place * count, count, 0)

    def join(place, mine, other):
        swapped = jnp.concatenate([other, mine], axis=0)
        return jnp.where(place == 0, jnp.concatenate([mine, other], axis=0), swapped)

    for place, distance in ((first, 1), (second, 2)):
        sent = take(values, 1 - place, half)
        arrived = swap(sent, "dp", distance)
        token = yield sent
        arrived = after(arrived, token)
        values = (take(values, place, half).astype(wide) + arrived.astype(wide)).astype(low)
        half //= 2
    for place, distance in ((second, 2), (first, 1)):
        arrived = swap(values, "dp", distance)
        token = yield values
        values = join(place, values, after(arrived, token))
    return values


def weight_steps(parts, near, line=line_steps):
    send, keep = parts
    shard = send.shape[0] // 2
    arrived = swap(send, "row", near)
    token = yield send
    arrived = after(arrived, token)
    passed = (keep[:shard].astype(wide) + arrived[:shard].astype(wide)).astype(low)
    last = swap(passed, "row", 3 - near)
    token = yield passed
    last = after(last, token)
    share = keep[shard:].astype(wide) + arrived[shard:].astype(wide) + last.astype(wide)
    total = yield from line(share.astype(low))
    return total.astype(wide)


def vector_steps(values):
    for axis, distance in (("row", 1), ("row", 2)):
        arrived = swap(values, axis, distance)
        token = yield values
        values = values + after(arrived, token)
    total = yield from line_steps(values)
    return total


class Chains:
    def __init__(self):
        self.steps, self.done = [], {}

    def add(self, steps):
        self.steps.append(steps)
        return [next(steps)]

    def advance(self, token=None, chosen=None):
        sent = []
        for n, steps in enumerate(self.steps):
            if n not in self.done and (chosen is None or n in chosen):
                try:
                    sent.append(steps.send(token))
                except StopIteration as stop:
                    self.done[n] = stop.value
        return sent


def shards(
    tokens, timesteps, block_ids, table, gain_one, bias_one, w_query, w_key, w_value, b_query,
    b_value, w_out, b_out, gain_two, bias_two, w_up, b_up, w_down, b_down, cotangent,
):
    seq_count, local_len, model_width = tokens.shape
    row_size, dp_size = lax.axis_size("row"), lax.axis_size("dp")
    assert seq_count == 1 and lax.axis_size("col") == 2 and row_size == 4
    head_cols = w_query.shape[1]
    hidden_cols = w_up.shape[1]
    col_index = lax.axis_index("col")
    row_index = lax.axis_index("row")
    seq_index = lax.axis_index("dp") * row_size + row_index
    seq_total = dp_size * row_size
    meta = jnp.stack([col_index, row_index]).astype(jnp.int32)

    cuts = [slice(first, first + 128) for first in range(0, head_cols, 128)]
    group_one = pack(w_query, w_key, w_value)
    in_bias = jnp.concatenate(
        [part for cut in cuts for part in (b_query[cut], jnp.zeros_like(b_query[cut]), b_value[cut])]
    )[None]
    in_pieces = gather_far(group_one, *gather_near(group_one))
    group_two = jnp.concatenate([w_out.T, w_up, w_down.T], axis=1).astype(low)
    group_two = after(group_two, in_pieces[3][2], in_pieces[4][2])
    near_x, near_y = gather_near(group_two)

    table_row = lax.dynamic_slice_in_dim(table, timesteps[0], 1, 0)
    unit_one, _ = norm_parts(tokens[0].astype(wide) + table_row)
    rows_mine = (unit_one * gain_one + bias_one).astype(low)
    rows_other = swap(rows_mine, "col", 1)
    up_bias = jnp.stack([b_up, swap(b_up, "col", 1)])[:, None]
    qkv, rows_turned, keys_turned, values_turned, in_own = project_in(
        meta, rows_mine, after(rows_other, up_bias), in_bias, in_pieces
    )
    in_other = swap(in_own, "col", 1)
    shard_other = swap(group_two, "col", 1)
    pairs = head_cols // 128
    mixed, mixed_other, log_sums = attend_forward(
        meta, qkv, values_turned, block_ids, 0, pairs - 1
    )
    got = swap(mixed_other, "col", 1)
    near_x, near_y = after(near_x, mixed), after(near_y, mixed)
    near_x_other, near_y_other = swap(near_x, "col", 1), swap(near_y, "col", 1)
    mine = gather_far(group_two, near_x, near_y)
    mixed_last, mixed_last_other, log_sums_last = attend_forward(
        meta, after(qkv, in_other, shard_other, got, near_x_other, near_y_other), values_turned,
        block_ids, pairs - 1, 1,
    )
    got_last = swap(mixed_last_other, "col", 1)
    far = [after(piece, mixed_last) for _, _, piece in mine[3:]]
    others = [shard_other, near_x_other, near_y_other] + [swap(piece, "col", 1) for piece in far]
    other = [(distance, first, piece) for (distance, first, _), piece in zip(mine, others)]

    spare = jnp.zeros_like(b_out)
    vectors = jnp.stack([b_out, gain_two, bias_two, b_down, spare, spare, spare, spare])
    cot = cotangent[0]
    (
        layer_out, hidden, grad_hidden, two_turned, cot_turned, branch_turned,
        grad_middle, grad_own, grad_other, sums, grad_up_bias,
    ) = feed(
        meta, tokens[0], table_row, (mixed, mixed_last), (got, got_last), cot, vectors, up_bias,
        mine, other,
    )
    up_arrived = swap(product(two_turned, grad_hidden, 4), "col", 1)
    down_arrived = swap(product(cot_turned, hidden, 4), "col", 1)
    grad_got = swap(grad_other, "col", 1)
    up_parts = weight_parts(meta, [([(two_turned, 0, grad_hidden)], up_arrived)], 1, 6)
    chains = Chains()
    chains.add(weight_steps(up_parts, 1, split_line_steps))
    down_parts = weight_parts(
        meta, [([(cot_turned, 0, hidden)], after(down_arrived, *up_parts))], 2, 6
    )
    chains.add(weight_steps(down_parts, 2, split_line_steps))
    grad_b_up = grad_up_bias[0, 0] + swap(grad_up_bias[1, 0], "col", 1)
    before = [*up_parts, *down_parts, grad_b_up]

    own_grads, aways, gots, bias_sums = [], [], [], []
    for pair in range(pairs):
        last = pair == pairs - 1
        own, away, bias_sum = attend_backward(
            meta, after(qkv, *before), keys_turned, grad_own, grad_got, block_ids,
            log_sums_last if last else log_sums, pair, 1, 0 if last else pair,
        )
        own_grads.append(own)
        gots.append(swap(away, "col", 1))
        bias_sums.append(bias_sum)
        before = [*chains.advance(own), gots[-1]]
        aways.append(away)
        if pair == 0:
            out_sent = product(
                branch_turned, after(jnp.concatenate([got, got_last], axis=1), *before), 2
            )
            out_arrived = swap(out_sent, "col", 1)
            before.append(out_sent)
            continue
        if pair == pairs - 2:
            out_keep = jnp.concatenate([mixed, mixed_last], axis=1)
            products = [([(branch_turned, 0, out_keep)], out_arrived)]
            ours, theirs = own_grads, aways
        else:
            products, ours, theirs = [], [own], [away]
        near = 1 if last else 2
        products += [([(rows_turned, 0, a), (rows_turned, 1, b)], None) for a, b in zip(ours, theirs)]
        parts = weight_parts(meta, products, near, 3 * len(products))
        before += parts
        chains.add(weight_steps(parts, near, line_steps if last else split_line_steps))
    grad_tokens, late_sums = grad_in(
        after(tokens[0], *before), table_row, gain_one[None], in_own, in_other, grad_middle,
        list(zip(own_grads, gots)),
    )
    chains.advance(grad_tokens)

    shared = jnp.concatenate([late_sums[:3], sums[:4]])
    shared = shared + swap(shared, "col", 1)
    slot = lax.broadcasted_iota(jnp.int32, (seq_total, 1), 0) == seq_index
    packed = jnp.concatenate(
        [
            jnp.concatenate([shared[:2], shared[3:]]).reshape(-1),
            jnp.concatenate([part[:1] for part in bias_sums], axis=1).reshape(-1),
            jnp.concatenate([part[1:2] for part in bias_sums], axis=1).reshape(-1),
            grad_b_up,
            jnp.where(slot, shared[2:3], 0.0).reshape(-1),
            jnp.where(slot, timesteps[0].astype(wide), 0.0).reshape(-1),
        ]
    )
    pad = -packed.shape[0] % 1024
    chains.add(vector_steps(jnp.pad(packed, (0, pad)).reshape(-1, 128)))
    sent = None
    for chain in (4, 2, 3, 4, 0, 1, 4, 3, 2, 4, 3, 2, 0, 1, 2):
        sent = chains.advance(sent, (chain,)) or sent
        if 4 in chains.done:
            sent = chains.done[4]
    while len(chains.done) < len(chains.steps):
        chains.advance(sent)
    done = chains.done
    own_up, own_down = done[0], done[1]
    own_out, done[2] = done[2][:, :head_cols], done[2][:, head_cols:]
    own_in = jnp.concatenate([done[2], done[3]], axis=1)
    own_in = [
        jnp.concatenate([own_in[:, 128 * n : 128 * (n + 1)] for n in range(kind, 3 * pairs, 3)], axis=1)
        for kind in range(3)
    ]
    packed = done[4].reshape(-1)
    place = 0
    taken = []
    for size in (6 * model_width, 2 * head_cols, hidden_cols, seq_total * model_width, seq_total):
        taken.append(packed[place : place + size])
        place += size
    six = taken[0].reshape(6, model_width)
    grad_table = table_rows(
        taken[4].astype(jnp.int32), taken[3].reshape(seq_total, model_width), table.shape[0]
    )
    return (
        layer_out[None],
        grad_tokens[None],
        grad_table,
        six[0],
        six[1],
        own_in[0],
        own_in[1],
        own_in[2],
        taken[1][:head_cols],
        taken[1][head_cols:],
        own_out.T,
        six[2],
        six[3],
        six[4],
        own_up,
        taken[2],
        own_down.T,
        six[5],
    )


def solution(mesh):
    return jax.shard_map(
        shards,
        mesh=mesh,
        in_specs=(
            P(("dp", "row"), "col", None),
            P(("dp", "row")),
            P(("dp", "row"), None),
            P(),
            P(),
            P(),
            P("row", "col"),
            P("row", "col"),
            P("row", "col"),
            P("col"),
            P("col"),
            P("col", "row"),
            P(),
            P(),
            P(),
            P("row", "col"),
            P("col"),
            P("col", "row"),
            P(),
            P(("dp", "row"), "col", None),
        ),
        out_specs=(
            P(("dp", "row"), "col", None),
            P(("dp", "row"), "col", None),
            P(),
            P(),
            P(),
            P("row", "col"),
            P("row", "col"),
            P("row", "col"),
            P("col"),
            P("col"),
            P("col", "row"),
            P(),
            P(),
            P(),
            P("row", "col"),
            P("col"),
            P("col", "row"),
            P(),
        ),
        check_vma=False,
    )
```

```python
import functools

import jax
import jax.numpy as jnp
from jax import lax
from jax.experimental import pallas as pl
from jax.experimental.pallas import tpu as pltpu
from jax.sharding import PartitionSpec as P

HEAD_DIM = 64
norm_eps = 1e-05
masked_score = -1000000000.0
low = jnp.bfloat16
wide = jnp.float32
tile_rows = 256


def cost(micros):
    return pl.CostEstimate(flops=int(micros * 1.1e9), transcendentals=0, bytes_accessed=1 << 20)


def dot_nn(left, right):
    return lax.dot_general(left, right, (((1,), (0,)), ((), ())), preferred_element_type=wide)


def dot_nt(left, right):
    return lax.dot_general(left, right, (((1,), (1,)), ((), ())), preferred_element_type=wide)


def dot_tn(left, right):
    return lax.dot_general(left, right, (((0,), (0,)), ((), ())), preferred_element_type=wide)


def column_of(ids_row):
    parts = []
    for start in range(0, ids_row.shape[1], 128):
        piece = ids_row[:, start : start + 128].astype(wide)
        parts.append(jnp.transpose(jnp.broadcast_to(piece, (128, 128))))
    return jnp.concatenate(parts, axis=0)


def lanes(values):
    return [values[:, first : first + 128] for first in range(0, values.shape[1], 128)]


def variants(count):
    return [(2 * n, min(2 * n + 3, count)) for n in range(count // 2)]


def key_tile(ref, tile, half, side):
    rows = slice((tile % half) * tile_rows, (tile % half + 1) * tile_rows)
    return ref[(tile // half) ^ side, rows, :]


def allowed_part(ids_ref, ids_column, first):
    return ids_ref[:, first : first + 128].astype(wide) <= ids_column


def row_tile(half, shift):
    return lambda i, c: jnp.clip(i - half * (c[0] ^ shift), 0, half - 1)


def attend_forward_body(
    count, half, col_ref, q_ref, k_ref, v_ref, ids_ref, own_ref, other_ref, lse_ref, s_ref
):
    step = pl.program_id(1)
    side = col_ref[0]
    lane = lax.broadcasted_iota(jnp.int32, (tile_rows, 128), 1)
    own_ids = ids_ref[:, pl.ds(pl.multiple_of(step * tile_rows, tile_rows), tile_rows)]

    def groups(values):
        return values.reshape(tile_rows // 8, 8, tile_rows)

    def variant(open_tiles, keys):
        query = q_ref[...]
        query_ids = own_ids.astype(wide)
        masks = {}
        for tile in range(open_tiles, keys):
            column = column_of(ids_ref[:, tile * tile_rows : (tile + 1) * tile_rows])
            masks[tile] = jnp.concatenate([column, column], axis=1) <= query_ids
        mixed = []
        for head in range(2):
            mine = lane // HEAD_DIM == head
            part = jnp.where(mine, query, jnp.zeros_like(query)) * jnp.asarray(0.125, low)
            top = None
            for tile in range(keys):
                scores = dot_nt(key_tile(k_ref, tile, half, side), part)
                if tile >= open_tiles:
                    scores = jnp.where(masks[tile], scores, masked_score)
                s_ref[head, tile * tile_rows : (tile + 1) * tile_rows, :] = scores
                peak = jnp.max(groups(scores), axis=0)
                top = peak if top is None else jnp.maximum(top, peak)
            top = jnp.max(top, axis=0, keepdims=True)
            total = None
            acc = None
            for tile in range(keys):
                expo = jnp.exp(s_ref[head, tile * tile_rows : (tile + 1) * tile_rows, :] - top)
                piece = jnp.sum(groups(expo), axis=0)
                total = piece if total is None else total + piece
                columns = slice((tile % half) * tile_rows, (tile % half + 1) * tile_rows)
                values = v_ref[
                    (tile // half) ^ side, head * HEAD_DIM : (head + 1) * HEAD_DIM, columns
                ]
                piece = dot_nn(values, expo.astype(low))
                acc = piece if acc is None else acc + piece
            total = jnp.sum(total, axis=0, keepdims=True)
            mixed.append(acc / total)
            lse_ref[head : head + 1, :] = top + jnp.log(total)
        out = jnp.transpose(jnp.concatenate(mixed, axis=0)).astype(low)
        owned = (step // half) ^ side == 0

        @pl.when(owned)
        def _():
            own_ref[...] = out

        @pl.when(jnp.logical_not(owned))
        def _():
            other_ref[...] = out

    for n, bounds in enumerate(variants(count)):
        pl.when(step // 2 == n)(functools.partial(variant, *bounds))


def attend_forward(meta, qkv, values_turned, ids, first, pairs):
    sides, rows, _ = qkv.shape
    length = sides * rows
    count = length // tile_rows
    half = rows // tile_rows
    head_cols = 128 * pairs
    own, other = row_tile(half, 0), row_tile(half, 1)
    return pl.pallas_call(
        functools.partial(attend_forward_body, count, half),
        grid_spec=pltpu.PrefetchScalarGridSpec(
            num_scalar_prefetch=1,
            grid=(pairs, count),
            in_specs=[
                pl.BlockSpec(
                    (None, tile_rows, 128),
                    lambda h, i, c: ((i // half) ^ c[0], i % half, 3 * (h + first)),
                ),
                pl.BlockSpec((sides, rows, 128), lambda h, i, c: (0, 0, 3 * (h + first) + 1)),
                pl.BlockSpec((sides, 128, rows), lambda h, i, c: (0, h + first, 0)),
                pl.BlockSpec((1, length), lambda h, i, c: (0, 0)),
            ],
            out_specs=[
                pl.BlockSpec((tile_rows, 128), lambda h, i, c: (own(i, c), h)),
                pl.BlockSpec((tile_rows, 128), lambda h, i, c: (other(i, c), h)),
                pl.BlockSpec((None, 2, tile_rows), lambda h, i, c: (h, 0, i)),
            ],
            scratch_shapes=[pltpu.VMEM((2, length, tile_rows), wide)],
        ),
        out_shape=[
            jax.ShapeDtypeStruct((rows, head_cols), low),
            jax.ShapeDtypeStruct((rows, head_cols), low),
            jax.ShapeDtypeStruct((pairs, 2, length), wide),
        ],
        cost_estimate=cost(14 * pairs),
        name="attend_forward",
    )(meta, qkv, qkv, values_turned, ids)


def attend_backward_body(
    count, half, col_ref, q_ref, k_ref, v_ref, kt_ref, g_ref, g_other_ref, ids_ref, lse_ref,
    own_ref, other_ref, sum_ref, p_ref, gp_ref, gq_ref, gk_acc, gv_acc,
):
    step, head = pl.program_id(1), pl.program_id(2)
    side = col_ref[0]
    lane = lax.broadcasted_iota(jnp.int32, (tile_rows, 128), 1)
    mine = lane // HEAD_DIM == head
    own_ids = ids_ref[:, pl.ds(pl.multiple_of(step * tile_rows, tile_rows), tile_rows)]
    spot = pl.ds(pl.multiple_of(head * HEAD_DIM, HEAD_DIM), HEAD_DIM)

    def store(tile, place, values):
        start = pl.multiple_of((tile % half) * tile_rows, tile_rows)
        here = (pl.ds(start, tile_rows), slice(place * 128, (place + 1) * 128))
        owned = (tile // half) ^ side == 0

        @pl.when(owned)
        def _():
            own_ref[here] = values

        @pl.when(jnp.logical_not(owned))
        def _():
            other_ref[here] = values

    @pl.when((step == 0) & (head == 0))
    def _():
        gk_acc[...] = jnp.zeros_like(gk_acc)
        gv_acc[...] = jnp.zeros_like(gv_acc)
        sum_ref[...] = jnp.zeros_like(sum_ref)

    def groups(values):
        return jnp.sum(values.reshape(tile_rows // 8, 8, tile_rows), axis=0)

    def variant(open_tiles, keys):
        query = q_ref[...]
        grad = jnp.where((step // half) ^ side == 0, g_ref[...], g_other_ref[...])
        part = jnp.where(mine, query, jnp.zeros_like(query)) * jnp.asarray(0.125, low)
        grad_part = jnp.where(mine, grad, jnp.zeros_like(grad))
        query_ids = own_ids.astype(wide)
        log_sum = jnp.where(head == 0, lse_ref[:1, :], lse_ref[1:, :])
        inner = None
        for tile in range(keys):
            here = slice(tile * tile_rows, (tile + 1) * tile_rows)
            scores = dot_nt(key_tile(k_ref, tile, half, side), part)
            grad_probs = dot_nt(key_tile(v_ref, tile, half, side), grad_part)
            gp_ref[here, :] = grad_probs
            probs = jnp.exp(scores - log_sum)
            if tile >= open_tiles:
                column = column_of(ids_ref[:, here])
                allowed = jnp.concatenate([column, column], axis=1) <= query_ids
                probs = jnp.where(allowed, probs, 0.0)
            p_ref[here, :] = probs
            piece = groups(probs * grad_probs)
            inner = piece if inner is None else inner + piece
            gv_acc[here, :] += dot_nn(probs.astype(low), grad_part)
        inner = jnp.sum(inner, axis=0, keepdims=True)
        grad_query = None
        for tile in range(keys):
            here = slice(tile * tile_rows, (tile + 1) * tile_rows)
            columns = slice((tile % half) * tile_rows, (tile % half + 1) * tile_rows)
            slopes = (p_ref[here, :] * (gp_ref[here, :] - inner)).astype(low)
            gk_acc[here, :] += dot_nn(slopes, part)
            piece = dot_nn(kt_ref[(tile // half) ^ side, spot, columns], slopes)
            grad_query = piece if grad_query is None else grad_query + piece
        gq_ref[spot, :] = grad_query

    for n, bounds in enumerate(variants(count)):
        pl.when(step // 2 == n)(functools.partial(variant, *bounds))

    @pl.when(head == 1)
    def _():
        out = jnp.transpose(gq_ref[...] * 0.125).astype(low)
        store(step, 0, out)
        sum_ref[0:1, :] += jnp.sum(out.astype(wide), axis=0, keepdims=True)

    @pl.when((step == count - 1) & (head == 1))
    def _():
        def finish(tile, _):
            here = pl.ds(pl.multiple_of(tile * tile_rows, tile_rows), tile_rows)
            grad_value = gv_acc[here, :].astype(low)
            store(tile, 1, gk_acc[here, :].astype(low))
            store(tile, 2, grad_value)
            sum_ref[1:2, :] += jnp.sum(grad_value.astype(wide), axis=0, keepdims=True)

        lax.fori_loop(0, count, finish, None)


def attend_backward(
    meta, qkv, keys_turned, grad, grad_other, ids, log_sums, first, pairs, lse_first
):
    sides, rows, _ = qkv.shape
    length = sides * rows
    count = length // tile_rows
    half = rows // tile_rows
    own, other = row_tile(half, 0), row_tile(half, 1)
    whole = pl.BlockSpec((rows, 384), lambda h, i, e, c: (0, h))
    return pl.pallas_call(
        functools.partial(attend_backward_body, count, half),
        grid_spec=pltpu.PrefetchScalarGridSpec(
            num_scalar_prefetch=1,
            grid=(pairs, count, 2),
            in_specs=[
                pl.BlockSpec(
                    (None, tile_rows, 128),
                    lambda h, i, e, c: ((i // half) ^ c[0], i % half, 3 * (h + first)),
                ),
                pl.BlockSpec((sides, rows, 128), lambda h, i, e, c: (0, 0, 3 * (h + first) + 1)),
                pl.BlockSpec((sides, rows, 128), lambda h, i, e, c: (0, 0, 3 * (h + first) + 2)),
                pl.BlockSpec((sides, 128, rows), lambda h, i, e, c: (0, h + first, 0)),
                pl.BlockSpec((tile_rows, 128), lambda h, i, e, c: (own(i, c), h + first)),
                pl.BlockSpec((tile_rows, 128), lambda h, i, e, c: (other(i, c), h + first)),
                pl.BlockSpec((1, length), lambda h, i, e, c: (0, 0)),
                pl.BlockSpec((None, 2, tile_rows), lambda h, i, e, c: (h + lse_first, 0, i)),
            ],
            out_specs=[whole, whole, pl.BlockSpec((8, 128), lambda h, i, e, c: (0, h))],
            scratch_shapes=[
                pltpu.VMEM((length, tile_rows), wide),
                pltpu.VMEM((length, tile_rows), wide),
                pltpu.VMEM((128, tile_rows), wide),
                pltpu.VMEM((length, 128), wide),
                pltpu.VMEM((length, 128), wide),
            ],
        ),
        out_shape=[jax.ShapeDtypeStruct((rows, 384 * pairs), low)] * 2
        + [jax.ShapeDtypeStruct((8, 128 * pairs), wide)],
        cost_estimate=cost(25 * pairs),
        name="attend_backward",
    )(meta, qkv, qkv, qkv, keys_turned, grad, grad_other, ids, log_sums)


def norm_parts(values):
    mean = jnp.mean(values, axis=-1, keepdims=True)
    centred = values - mean
    inverse = lax.rsqrt(jnp.mean(centred * centred, axis=-1, keepdims=True) + norm_eps)
    return centred * inverse, inverse


def norm_back(grad_normed, unit, inverse, gain):
    grad_unit = grad_normed * gain
    first_mean = jnp.mean(grad_unit, axis=-1, keepdims=True)
    second_mean = jnp.mean(grad_unit * unit, axis=-1, keepdims=True)
    return inverse * (grad_unit - first_mean - unit * second_mean)


erfc_terms = (
    -0.12664913241116757, 0.4719797697046255, -0.4849989149703286, 0.5173882238837517,
    -0.0742751946996765, 0.20647784419749105, 0.15044607588806108, 0.17042678586105697,
    0.16920458065681523,
)


def gelu_with_slope(values):
    turned = 1.0 / (1.0 + (0.3 * 0.5**0.5) * jnp.abs(values))
    bell = jnp.exp(-0.5 * (values * values))
    series = jnp.full_like(values, 0.5 * erfc_terms[0])
    for term in erfc_terms[1:]:
        series = series * turned + 0.5 * term
    tail = series * turned * bell
    below = jnp.where(values < 0.0, tail, 1.0 - tail)
    return values * below, below + values * (bell * (0.5 / jnp.pi) ** 0.5)


def swap(values, axis, distance):
    size = lax.axis_size(axis)
    return lax.ppermute(values, axis, [(i, i ^ distance) for i in range(size)])


def gather_near(shard):
    return swap(shard, "row", 1), swap(shard, "row", 2)


def gather_far(shard, from_x, from_y):
    cut = shard.shape[0] // 2
    first_xy = swap(from_x[:cut], "row", 2)
    second_xy = swap(from_y[cut:], "row", 1)
    return [(0, 0, shard), (1, 0, from_x), (2, 0, from_y), (3, 0, first_xy), (3, cut, second_xy)]


def piece_copies(layout, refs, target, row_index, shard_rows, sems):
    copies = []
    for n, ((distance, first, rows), ref) in enumerate(zip(layout, refs)):
        base = pl.multiple_of((row_index ^ distance) * shard_rows + first, 16)
        copies.append(pltpu.make_async_copy(ref, target.at[pl.ds(base, rows), :], sems.at[n]))
    return copies


def layout_of(pieces):
    return [(distance, first, piece.shape[0]) for distance, first, piece in pieces]


hbm = pl.BlockSpec(memory_space=pl.ANY)


def project_in_body(layout, tiles, meta_ref, mine_ref, other_ref, bias_ref, *rest):
    pieces = rest[: len(layout)]
    out_ref, turned_ref, keys_ref, values_ref, weight_out, weight, sems, out_sem = rest[len(layout) :]
    step = pl.program_id(0)
    keep = pltpu.make_async_copy(weight, weight_out, out_sem)

    def project(rows):
        out = (dot_nn(rows, weight[...]) + bias_ref[...]).astype(low)
        out_ref[...] = out
        turned_ref[...] = jnp.transpose(rows)
        for pair in range(out.shape[1] // 384):
            here = slice(128 * pair, 128 * (pair + 1))
            keys_ref[here, :] = jnp.transpose(out[:, 384 * pair + 128 : 384 * pair + 256])
            values_ref[here, :] = jnp.transpose(out[:, 384 * pair + 256 : 384 * (pair + 1)])

    @pl.when(step == 0)
    def _():
        copies = piece_copies(layout, pieces, weight, meta_ref[1], weight.shape[0] // 4, sems)
        for copy in copies:
            copy.start()
        for copy in copies:
            copy.wait()
        keep.start()

    @pl.when(step < tiles)
    def _():
        project(mine_ref[...])

    @pl.when(step >= tiles)
    def _():
        project(other_ref[...])

    @pl.when(step == 2 * tiles - 1)
    def _():
        keep.wait()


def project_in(meta, mine, other, bias, pieces):
    rows, model = mine.shape
    size = 2 * tile_rows
    tiles = rows // size
    width = pieces[0][2].shape[1]
    return pl.pallas_call(
        functools.partial(project_in_body, layout_of(pieces), tiles),
        grid_spec=pltpu.PrefetchScalarGridSpec(
            num_scalar_prefetch=1,
            grid=(2 * tiles,),
            in_specs=[
                pl.BlockSpec((size, model), lambda i, m: (jnp.minimum(i, tiles - 1), 0)),
                pl.BlockSpec((size, model), lambda i, m: (jnp.maximum(i - tiles, 0), 0)),
                pl.BlockSpec((1, width), lambda i, m: (0, 0)),
            ]
            + [hbm] * len(pieces),
            out_specs=[
                pl.BlockSpec((None, size, width), lambda i, m: (i // tiles, i % tiles, 0)),
                pl.BlockSpec((model, size), lambda i, m: (0, i)),
                pl.BlockSpec((None, width // 3, size), lambda i, m: (i // tiles, 0, i % tiles)),
                pl.BlockSpec((None, width // 3, size), lambda i, m: (i // tiles, 0, i % tiles)),
                hbm,
            ],
            scratch_shapes=[
                pltpu.VMEM((model, width), low),
                pltpu.SemaphoreType.DMA((len(pieces),)),
                pltpu.SemaphoreType.DMA(()),
            ],
        ),
        out_shape=[
            jax.ShapeDtypeStruct((2, rows, width), low),
            jax.ShapeDtypeStruct((model, 2 * rows), low),
            jax.ShapeDtypeStruct((2, width // 3, rows), low),
            jax.ShapeDtypeStruct((2, width // 3, rows), low),
            jax.ShapeDtypeStruct((model, width), low),
        ],
        cost_estimate=cost(7),
        name="project_in",
    )(meta, mine, other, bias, *[piece for _, _, piece in pieces])


def load_weights(layout, pieces, weight, meta_ref, sems):
    copies = []
    for side in range(2):
        copies += piece_copies(
            layout, pieces[side], weight.at[side], meta_ref[1], weight.shape[1] // 4, sems.at[side]
        )
    for copy in copies:
        copy.start()
    for copy in copies:
        copy.wait()


hidden_chunk = 768


def feed_body(
    layout, head_cols, hidden_cols, meta_ref, tok_ref, row_ref, mixed_ref, mixed_last_ref,
    got_ref, got_last_ref, cot_ref, vec_ref, up_bias_ref, *rest,
):
    count = len(layout)
    pieces = (rest[:count], rest[count : 2 * count])
    (
        out_ref, hidden_ref, grad_ref, two_ref, cot_turned_ref, branch_ref, middle_ref, own_ref,
        other_ref, sum_ref, bias_ref, weight, sems, mixer_ref, grad_two_ref,
    ) = rest[2 * count :]

    @pl.when(pl.program_id(0) == 0)
    def _():
        load_weights(layout, pieces, weight, meta_ref, sems)
        sum_ref[...] = jnp.zeros_like(sum_ref)
        bias_ref[...] = jnp.zeros_like(bias_ref)

    bias_out, gain, bias, bias_down = (vec_ref[n : n + 1, :] for n in range(4))
    cot = cot_ref[...]
    cot_turned_ref[...] = jnp.transpose(cot)
    start = tok_ref[...].astype(wide) + row_ref[...]
    cut = mixed_ref.shape[1]
    branch = dot_nt(mixed_ref[...], weight[0, :, :cut])
    branch = branch + dot_nt(mixed_last_ref[...], weight[0, :, cut:head_cols])
    branch = branch + dot_nt(got_ref[...], weight[1, :, :cut])
    branch = branch + dot_nt(got_last_ref[...], weight[1, :, cut:head_cols])
    middle = start + (branch + bias_out)
    unit, inverse = norm_parts(middle)
    two = (unit * gain + bias).astype(low)
    two_ref[...] = jnp.transpose(two)
    mixer_ref[...] = jnp.zeros_like(mixer_ref)
    grad_two_ref[...] = jnp.zeros_like(grad_two_ref)

    def visit(side, _):
        mixer = None
        grad_two = None
        for first in range(0, hidden_cols, hidden_chunk):
            here = slice(first, first + hidden_chunk)
            up = weight[side, :, head_cols + first : head_cols + first + hidden_chunk]
            at = head_cols + hidden_cols + first
            down = weight[side, :, at : at + hidden_chunk]
            hidden, slope = gelu_with_slope(dot_nn(two, up) + up_bias_ref[side, :, here])
            hidden = hidden.astype(low)
            hidden_ref[side, :, here] = hidden
            part = dot_nt(hidden, down)
            mixer = part if mixer is None else mixer + part
            grad_pre = (dot_nn(cot, down) * slope).astype(low)
            grad_ref[side, :, here] = grad_pre
            bias_ref[side, :, here] += jnp.sum(grad_pre.astype(wide), axis=0, keepdims=True)
            part = dot_nt(grad_pre, up)
            grad_two = part if grad_two is None else grad_two + part
        mixer_ref[...] += mixer
        grad_two_ref[...] += grad_two

    lax.fori_loop(0, 2, visit, None)
    mixer, grad_two = mixer_ref[...], grad_two_ref[...]
    out_ref[...] = (middle + (mixer + bias_down)).astype(low)
    cot = cot.astype(wide)
    grad_middle = cot + norm_back(grad_two, unit, inverse, gain)
    grad_branch = grad_middle.astype(low)
    middle_ref[...] = grad_middle
    branch_ref[...] = jnp.transpose(grad_branch)
    own_ref[...] = dot_nn(grad_branch, weight[0, :, :head_cols]).astype(low)
    other_ref[...] = dot_nn(grad_branch, weight[1, :, :head_cols]).astype(low)
    for n, values in enumerate((grad_branch.astype(wide), grad_two * unit, grad_two, cot)):
        sum_ref[n : n + 1, :] += jnp.sum(values, axis=0, keepdims=True)


def feed(meta, tokens, table_row, mixed, got, cot, vectors, up_bias, mine, other):
    rows, model = tokens.shape
    size = tile_rows
    head_cols = sum(part.shape[1] for part in mixed)
    hidden_cols = up_bias.shape[2]
    width = mine[0][2].shape[1]

    def tile(columns):
        return pl.BlockSpec((size, columns), lambda i, m: (i, 0))

    def fixed(*shape):
        return pl.BlockSpec(shape, lambda i, m: (0,) * len(shape))

    def turned(depth):
        return pl.BlockSpec((depth, size), lambda i, m: (0, i))

    def array(columns, dtype):
        return jax.ShapeDtypeStruct((rows, columns), dtype)

    flipped = jax.ShapeDtypeStruct((model, rows), low)
    return pl.pallas_call(
        functools.partial(feed_body, layout_of(mine), head_cols, hidden_cols),
        grid_spec=pltpu.PrefetchScalarGridSpec(
            num_scalar_prefetch=1,
            grid=(rows // size,),
            in_specs=[tile(model), fixed(1, model)]
            + [tile(part.shape[1]) for part in (*mixed, *got)]
            + [tile(model), fixed(8, model), fixed(2, 1, hidden_cols)]
            + [hbm] * (2 * len(mine)),
            out_specs=[tile(model)]
            + [pl.BlockSpec((2, size, hidden_cols), lambda i, m: (0, i, 0))] * 2
            + [turned(model)] * 3
            + [tile(model), tile(head_cols), tile(head_cols), fixed(8, model)]
            + [fixed(2, 1, hidden_cols)],
            scratch_shapes=[
                pltpu.VMEM((2, model, width), low),
                pltpu.SemaphoreType.DMA((2, len(mine))),
                pltpu.VMEM((size, model), wide),
                pltpu.VMEM((size, model), wide),
            ],
        ),
        out_shape=[array(model, low)]
        + [jax.ShapeDtypeStruct((2, rows, hidden_cols), low)] * 2
        + [flipped] * 3
        + [array(model, wide), array(head_cols, low), array(head_cols, low)]
        + [jax.ShapeDtypeStruct((8, model), wide)]
        + [jax.ShapeDtypeStruct((2, 1, hidden_cols), wide)],
        cost_estimate=cost(45),
        name="feed",
    )(
        meta, tokens, table_row, *mixed, *got, cot, vectors, up_bias,
        *[piece for _, _, piece in mine], *[piece for _, _, piece in other],
    )


def weight_parts_body(products, near, meta_ref, *refs):
    send_ref, keep_ref = refs[-2:]
    shard = send_ref.shape[0] // 2
    order = [pl.multiple_of((meta_ref[1] ^ d) * shard, 64) for d in (3, near, 3 - near, 0)]

    def in_order(ref):
        return jnp.concatenate([ref[pl.ds(start, shard), :] for start in order], axis=0)

    at = 0
    for lefts, arrived, first, tiles in products:
        inputs = refs[at : at + 2 * lefts + arrived]
        at += 2 * lefts + arrived

        @pl.when((pl.program_id(0) >= first) & (pl.program_id(0) < first + tiles))
        def _(inputs=inputs, lefts=lefts, arrived=arrived):
            total = None
            for n in range(lefts):
                part = dot_nn(in_order(inputs[2 * n]), inputs[2 * n + 1][...])
                total = part if total is None else total + part
            if arrived:
                total = total + in_order(inputs[-1]).astype(wide)
            total = total.astype(low)
            send_ref[...] = total[: 2 * shard]
            keep_ref[...] = total[2 * shard :]


def weight_parts(meta, products, near, micros):
    model = products[0][0][0][0].shape[0]
    operands, specs, shapes = [], [], []
    step = 384 if any(pairs[0][2].shape[-1] % 512 for pairs, _ in products) else 512
    first = 0
    for pairs, arrived in products:
        tiles = pairs[0][2].shape[-1] // step

        def tile(i, m, first=first, tiles=tiles):
            return (0, jnp.clip(i - first, 0, tiles - 1))

        for left, place, right in pairs:
            depth = right.shape[-2]
            specs.append(pl.BlockSpec((model, depth), lambda i, m, p=place: (0, p)))
            if right.ndim == 3:
                specs.append(pl.BlockSpec((None, depth, step), lambda i, m, t=tile: (0, *t(i, m))))
            else:
                specs.append(pl.BlockSpec((depth, step), tile))
            operands += [left, right]
        if arrived is not None:
            specs.append(pl.BlockSpec((model, step), tile))
            operands.append(arrived)
        shapes.append((len(pairs), int(arrived is not None), first, tiles))
        first += tiles
    half = jax.ShapeDtypeStruct((model // 2, first * step), low)
    return pl.pallas_call(
        functools.partial(weight_parts_body, shapes, near),
        grid_spec=pltpu.PrefetchScalarGridSpec(
            num_scalar_prefetch=1,
            grid=(first,),
            in_specs=specs,
            out_specs=[pl.BlockSpec((model // 2, step), lambda i, m: (0, i))] * 2,
        ),
        out_shape=[half, half],
        cost_estimate=cost(micros),
        name="weight_parts",
    )(meta, *operands)


def product_body(left_ref, right_ref, out_ref):
    out_ref[...] = dot_nn(left_ref[...], right_ref[...]).astype(low)


def product(left, right, micros):
    rows, depth = left.shape
    columns = right.shape[-1]
    step = 512 if columns % 512 == 0 else 384
    right_spec = pl.BlockSpec((depth, step), lambda i: (0, i))
    if right.ndim == 3:
        right_spec = pl.BlockSpec((None, depth, step), lambda i: (1, 0, i))
    return pl.pallas_call(
        product_body,
        grid=(columns // step,),
        in_specs=[pl.BlockSpec((rows, depth), lambda i: (0, 0)), right_spec],
        out_specs=pl.BlockSpec((rows, step), lambda i: (0, i)),
        out_shape=jax.ShapeDtypeStruct((rows, columns), low),
        cost_estimate=cost(micros),
        name="product",
    )(left, right)


def table_body(step_ref, sum_ref, out_ref):
    out_ref[...] = jnp.zeros_like(out_ref)

    def add(n, _):
        out_ref[pl.ds(step_ref[n], 1), :] += sum_ref[pl.ds(n, 1), :]

    lax.fori_loop(0, sum_ref.shape[0], add, None)


def table_rows(steps, sums, rows):
    return pl.pallas_call(
        table_body,
        grid_spec=pltpu.PrefetchScalarGridSpec(
            num_scalar_prefetch=1,
            grid=(1,),
            in_specs=[pl.BlockSpec(sums.shape, lambda i, t: (0, 0))],
            out_specs=pl.BlockSpec((rows, sums.shape[1]), lambda i, t: (0, 0)),
        ),
        out_shape=jax.ShapeDtypeStruct((rows, sums.shape[1]), wide),
        cost_estimate=cost(2),
        name="table_rows",
    )(steps, sums)


def pack_body(*refs):
    out_ref = refs[-1]
    for n in range(out_ref.shape[1] // 128):
        kind, pair = n % 3, n // 3
        out_ref[:, 128 * n : 128 * (n + 1)] = refs[kind][:, 128 * pair : 128 * (pair + 1)].astype(low)


def pack(*weights):
    rows, columns = weights[0].shape
    return pl.pallas_call(
        pack_body,
        out_shape=jax.ShapeDtypeStruct((rows, 3 * columns), low),
        cost_estimate=cost(1),
        name="pack",
    )(*weights)


def grad_in_body(cuts, tok_ref, row_ref, gain_ref, own_ref, other_ref, middle_ref, *rest):
    grads = rest[: 2 * len(cuts)]
    out_ref, sum_ref = rest[2 * len(cuts) :]

    @pl.when(pl.program_id(0) == 0)
    def _():
        sum_ref[...] = jnp.zeros_like(sum_ref)

    grad = None
    for n, (first, last) in enumerate(cuts):
        for values, weight in ((grads[2 * n], own_ref), (grads[2 * n + 1], other_ref)):
            part = dot_nt(values[...], weight[:, first:last])
            grad = part if grad is None else grad + part
    unit, inverse = norm_parts(tok_ref[...].astype(wide) + row_ref[...])
    tokens = middle_ref[...] + norm_back(grad, unit, inverse, gain_ref[...])
    out_ref[...] = tokens
    for n, values in enumerate((grad * unit, grad, tokens)):
        sum_ref[n : n + 1, :] += jnp.sum(values, axis=0, keepdims=True)


def grad_in(tokens, table_row, gain, own, other, grad_middle, grads):
    rows, model = tokens.shape
    size = tile_rows
    width = own.shape[1]
    cuts = []
    for mine, _ in grads:
        first = cuts[-1][1] if cuts else 0
        cuts.append((first, first + mine.shape[1]))

    def tile(columns):
        return pl.BlockSpec((size, columns), lambda i: (i, 0))

    def fixed(*shape):
        return pl.BlockSpec(shape, lambda i: (0, 0))

    flat = [values for pair in grads for values in pair]
    return pl.pallas_call(
        functools.partial(grad_in_body, cuts),
        grid=(rows // size,),
        in_specs=[
            tile(model), fixed(1, model), fixed(1, model), fixed(model, width),
            fixed(model, width), tile(model),
        ]
        + [tile(values.shape[1]) for values in flat],
        out_specs=[tile(model), fixed(8, model)],
        out_shape=[
            jax.ShapeDtypeStruct((rows, model), wide),
            jax.ShapeDtypeStruct((8, model), wide),
        ],
        cost_estimate=cost(9),
        name="grad_in",
    )(tokens, table_row, gain, own, other, grad_middle, *flat)


def after(values, *needed):
    needed = jax.tree.leaves(needed)
    return lax.optimization_barrier((values, *needed))[0] if needed else values


def line_steps(values):
    if lax.axis_size("dp") != 4:
        return lax.psum(values, "dp")
    for distance in (1, 2):
        arrived = swap(values, "dp", distance)
        token = yield values
        arrived = after(arrived, token)
        values = (values.astype(wide) + arrived.astype(wide)).astype(values.dtype)
    return values


def split_line_steps(values):
    if lax.axis_size("dp") != 4:
        return lax.psum(values, "dp")
    me = lax.axis_index("dp")
    first, second = me % 2, me // 2
    half = values.shape[0] // 2

    def take(array, place, count):
        return lax.dynamic_slice_in_dim(array, place * count, count, 0)

    def join(place, mine, other):
        swapped = jnp.concatenate([other, mine], axis=0)
        return jnp.where(place == 0, jnp.concatenate([mine, other], axis=0), swapped)

    for place, distance in ((first, 1), (second, 2)):
        sent = take(values, 1 - place, half)
        arrived = swap(sent, "dp", distance)
        token = yield sent
        arrived = after(arrived, token)
        values = (take(values, place, half).astype(wide) + arrived.astype(wide)).astype(low)
        half //= 2
    for place, distance in ((second, 2), (first, 1)):
        arrived = swap(values, "dp", distance)
        token = yield values
        values = join(place, values, after(arrived, token))
    return values


def weight_steps(parts, near, line=line_steps):
    send, keep = parts
    shard = send.shape[0] // 2
    arrived = swap(send, "row", near)
    token = yield send
    arrived = after(arrived, token)
    passed = (keep[:shard].astype(wide) + arrived[:shard].astype(wide)).astype(low)
    last = swap(passed, "row", 3 - near)
    token = yield passed
    last = after(last, token)
    share = keep[shard:].astype(wide) + arrived[shard:].astype(wide) + last.astype(wide)
    total = yield from line(share.astype(low))
    return total.astype(wide)


def vector_steps(values):
    for axis, distance in (("row", 1), ("row", 2)):
        arrived = swap(values, axis, distance)
        token = yield values
        values = values + after(arrived, token)
    total = yield from line_steps(values)
    return total


class Chains:
    def __init__(self):
        self.steps, self.done = [], {}

    def add(self, steps):
        self.steps.append(steps)
        return [next(steps)]

    def advance(self, token=None, chosen=None):
        sent = []
        for n, steps in enumerate(self.steps):
            if n not in self.done and (chosen is None or n in chosen):
                try:
                    sent.append(steps.send(token))
                except StopIteration as stop:
                    self.done[n] = stop.value
        return sent


def shards(
    tokens, timesteps, block_ids, table, gain_one, bias_one, w_query, w_key, w_value, b_query,
    b_value, w_out, b_out, gain_two, bias_two, w_up, b_up, w_down, b_down, cotangent,
):
    seq_count, local_len, model_width = tokens.shape
    row_size, dp_size = lax.axis_size("row"), lax.axis_size("dp")
    assert seq_count == 1 and lax.axis_size("col") == 2 and row_size == 4
    head_cols = w_query.shape[1]
    hidden_cols = w_up.shape[1]
    col_index = lax.axis_index("col")
    row_index = lax.axis_index("row")
    seq_index = lax.axis_index("dp") * row_size + row_index
    seq_total = dp_size * row_size
    meta = jnp.stack([col_index, row_index]).astype(jnp.int32)

    cuts = [slice(first, first + 128) for first in range(0, head_cols, 128)]
    group_one = pack(w_query, w_key, w_value)
    in_bias = jnp.concatenate(
        [part for cut in cuts for part in (b_query[cut], jnp.zeros_like(b_query[cut]), b_value[cut])]
    )[None]
    in_pieces = gather_far(group_one, *gather_near(group_one))
    group_two = jnp.concatenate([w_out.T, w_up, w_down.T], axis=1).astype(low)
    group_two = after(group_two, in_pieces[3][2], in_pieces[4][2])
    near_x, near_y = gather_near(group_two)

    table_row = lax.dynamic_slice_in_dim(table, timesteps[0], 1, 0)
    unit_one, _ = norm_parts(tokens[0].astype(wide) + table_row)
    rows_mine = (unit_one * gain_one + bias_one).astype(low)
    rows_other = swap(rows_mine, "col", 1)
    up_bias = jnp.stack([b_up, swap(b_up, "col", 1)])[:, None]
    qkv, rows_turned, keys_turned, values_turned, in_own = project_in(
        meta, rows_mine, after(rows_other, up_bias), in_bias, in_pieces
    )
    in_other = swap(in_own, "col", 1)
    shard_other = swap(group_two, "col", 1)
    pairs = head_cols // 128
    mixed, mixed_other, log_sums = attend_forward(
        meta, qkv, values_turned, block_ids, 0, pairs - 1
    )
    got = swap(mixed_other, "col", 1)
    near_x, near_y = after(near_x, mixed), after(near_y, mixed)
    near_x_other, near_y_other = swap(near_x, "col", 1), swap(near_y, "col", 1)
    mine = gather_far(group_two, near_x, near_y)
    mixed_last, mixed_last_other, log_sums_last = attend_forward(
        meta, after(qkv, in_other, shard_other, got, near_x_other, near_y_other), values_turned,
        block_ids, pairs - 1, 1,
    )
    got_last = swap(mixed_last_other, "col", 1)
    far = [after(piece, mixed_last) for _, _, piece in mine[3:]]
    others = [shard_other, near_x_other, near_y_other] + [swap(piece, "col", 1) for piece in far]
    other = [(distance, first, piece) for (distance, first, _), piece in zip(mine, others)]

    spare = jnp.zeros_like(b_out)
    vectors = jnp.stack([b_out, gain_two, bias_two, b_down, spare, spare, spare, spare])
    cot = cotangent[0]
    (
        layer_out, hidden, grad_hidden, two_turned, cot_turned, branch_turned,
        grad_middle, grad_own, grad_other, sums, grad_up_bias,
    ) = feed(
        meta, tokens[0], table_row, (mixed, mixed_last), (got, got_last), cot, vectors, up_bias,
        mine, other,
    )
    up_arrived = swap(product(two_turned, grad_hidden, 4), "col", 1)
    down_arrived = swap(product(cot_turned, hidden, 4), "col", 1)
    grad_got = swap(grad_other, "col", 1)
    up_parts = weight_parts(meta, [([(two_turned, 0, grad_hidden)], up_arrived)], 1, 6)
    chains = Chains()
    chains.add(weight_steps(up_parts, 1, split_line_steps))
    down_parts = weight_parts(
        meta, [([(cot_turned, 0, hidden)], after(down_arrived, *up_parts))], 2, 6
    )
    chains.add(weight_steps(down_parts, 2, split_line_steps))
    grad_b_up = grad_up_bias[0, 0] + swap(grad_up_bias[1, 0], "col", 1)
    before = [*up_parts, *down_parts, grad_b_up]

    own_grads, aways, gots, bias_sums = [], [], [], []
    for pair in range(pairs):
        last = pair == pairs - 1
        own, away, bias_sum = attend_backward(
            meta, after(qkv, *before), keys_turned, grad_own, grad_got, block_ids,
            log_sums_last if last else log_sums, pair, 1, 0 if last else pair,
        )
        own_grads.append(own)
        gots.append(swap(away, "col", 1))
        bias_sums.append(bias_sum)
        before = [*chains.advance(own), gots[-1]]
        aways.append(away)
        if pair == 0:
            out_sent = product(
                branch_turned, after(jnp.concatenate([got, got_last], axis=1), *before), 2
            )
            out_arrived = swap(out_sent, "col", 1)
            before.append(out_sent)
            continue
        if pair == pairs - 2:
            out_keep = jnp.concatenate([mixed, mixed_last], axis=1)
            products = [([(branch_turned, 0, out_keep)], out_arrived)]
            ours, theirs = own_grads, aways
        else:
            products, ours, theirs = [], [own], [away]
        near = 1 if last else 2
        products += [([(rows_turned, 0, a), (rows_turned, 1, b)], None) for a, b in zip(ours, theirs)]
        parts = weight_parts(meta, products, near, 3 * len(products))
        before += parts
        chains.add(weight_steps(parts, near, line_steps if last else split_line_steps))
    grad_tokens, late_sums = grad_in(
        after(tokens[0], *before), table_row, gain_one[None], in_own, in_other, grad_middle,
        list(zip(own_grads, gots)),
    )
    first_sent = chains.advance(grad_tokens)
    bias_sums = after(bias_sums[0], grad_tokens), after(bias_sums[1], grad_tokens), *bias_sums[2:]

    shared = jnp.concatenate([late_sums[:3], sums[:4]])
    shared = shared + after(swap(shared, "col", 1), first_sent)
    slot = lax.broadcasted_iota(jnp.int32, (seq_total, 1), 0) == seq_index
    packed = jnp.concatenate(
        [
            jnp.concatenate([shared[:2], shared[3:]]).reshape(-1),
            jnp.concatenate([part[:1] for part in bias_sums], axis=1).reshape(-1),
            jnp.concatenate([part[1:2] for part in bias_sums], axis=1).reshape(-1),
            grad_b_up,
            jnp.where(slot, shared[2:3], 0.0).reshape(-1),
            jnp.where(slot, timesteps[0].astype(wide), 0.0).reshape(-1),
        ]
    )
    pad = -packed.shape[0] % 1024
    chains.add(vector_steps(jnp.pad(packed, (0, pad)).reshape(-1, 128)))
    sent = None
    for chain in (4, 4, 2, 3, 0, 1, 4, 3, 2, 4, 3, 2, 0, 1, 2):
        sent = chains.advance(sent, (chain,)) or sent
        if 4 in chains.done:
            sent = chains.done[4]
    while len(chains.done) < len(chains.steps):
        chains.advance(sent)
    done = chains.done
    own_up, own_down = done[0], done[1]
    own_out, done[2] = done[2][:, :head_cols], done[2][:, head_cols:]
    own_in = jnp.concatenate([done[2], done[3]], axis=1)
    own_in = [
        jnp.concatenate([own_in[:, 128 * n : 128 * (n + 1)] for n in range(kind, 3 * pairs, 3)], axis=1)
        for kind in range(3)
    ]
    packed = done[4].reshape(-1)
    place = 0
    taken = []
    for size in (6 * model_width, 2 * head_cols, hidden_cols, seq_total * model_width, seq_total):
        taken.append(packed[place : place + size])
        place += size
    six = taken[0].reshape(6, model_width)
    grad_table = table_rows(
        taken[4].astype(jnp.int32), taken[3].reshape(seq_total, model_width), table.shape[0]
    )
    return (
        layer_out[None],
        grad_tokens[None],
        grad_table,
        six[0],
        six[1],
        own_in[0],
        own_in[1],
        own_in[2],
        taken[1][:head_cols],
        taken[1][head_cols:],
        own_out.T,
        six[2],
        six[3],
        six[4],
        own_up,
        taken[2],
        own_down.T,
        six[5],
    )


def solution(mesh):
    return jax.shard_map(
        shards,
        mesh=mesh,
        in_specs=(
            P(("dp", "row"), "col", None),
            P(("dp", "row")),
            P(("dp", "row"), None),
            P(),
            P(),
            P(),
            P("row", "col"),
            P("row", "col"),
            P("row", "col"),
            P("col"),
            P("col"),
            P("col", "row"),
            P(),
            P(),
            P(),
            P("row", "col"),
            P("col"),
            P("col", "row"),
            P(),
            P(("dp", "row"), "col", None),
        ),
        out_specs=(
            P(("dp", "row"), "col", None),
            P(("dp", "row"), "col", None),
            P(),
            P(),
            P(),
            P("row", "col"),
            P("row", "col"),
            P("row", "col"),
            P("col"),
            P("col"),
            P("col", "row"),
            P(),
            P(),
            P(),
            P("row", "col"),
            P("col"),
            P("col", "row"),
            P(),
        ),
        check_vma=False,
    )
```

```python
import functools

import jax
import jax.numpy as jnp
from jax import lax
from jax.experimental import pallas as pl
from jax.experimental.pallas import tpu as pltpu
from jax.sharding import PartitionSpec as P

HEAD_DIM = 64
norm_eps = 1e-05
masked_score = -1000000000.0
low = jnp.bfloat16
wide = jnp.float32
tile_rows = 256


def cost(micros):
    return pl.CostEstimate(flops=int(micros * 1.1e9), transcendentals=0, bytes_accessed=1 << 20)


def dot_nn(left, right):
    return lax.dot_general(left, right, (((1,), (0,)), ((), ())), preferred_element_type=wide)


def dot_nt(left, right):
    return lax.dot_general(left, right, (((1,), (1,)), ((), ())), preferred_element_type=wide)


def dot_tn(left, right):
    return lax.dot_general(left, right, (((0,), (0,)), ((), ())), preferred_element_type=wide)


def column_of(ids_row):
    parts = []
    for start in range(0, ids_row.shape[1], 128):
        piece = ids_row[:, start : start + 128].astype(wide)
        parts.append(jnp.transpose(jnp.broadcast_to(piece, (128, 128))))
    return jnp.concatenate(parts, axis=0)


def lanes(values):
    return [values[:, first : first + 128] for first in range(0, values.shape[1], 128)]


def variants(count):
    return [(2 * n, min(2 * n + 3, count)) for n in range(count // 2)]


def key_tile(ref, tile, half, side):
    rows = slice((tile % half) * tile_rows, (tile % half + 1) * tile_rows)
    return ref[(tile // half) ^ side, rows, :]


def allowed_part(ids_ref, ids_column, first):
    return ids_ref[:, first : first + 128].astype(wide) <= ids_column


def row_tile(half, shift):
    return lambda i, c: jnp.clip(i - half * (c[0] ^ shift), 0, half - 1)


def attend_forward_body(
    count, half, col_ref, q_ref, k_ref, v_ref, ids_ref, own_ref, other_ref, lse_ref, s_ref
):
    step = pl.program_id(1)
    side = col_ref[0]
    lane = lax.broadcasted_iota(jnp.int32, (tile_rows, 128), 1)
    own_ids = ids_ref[:, pl.ds(pl.multiple_of(step * tile_rows, tile_rows), tile_rows)]

    def groups(values):
        return values.reshape(tile_rows // 8, 8, tile_rows)

    def variant(open_tiles, keys):
        query = q_ref[...]
        query_ids = own_ids.astype(wide)
        masks = {}
        for tile in range(open_tiles, keys):
            column = column_of(ids_ref[:, tile * tile_rows : (tile + 1) * tile_rows])
            masks[tile] = jnp.concatenate([column, column], axis=1) <= query_ids
        mixed = []
        for head in range(2):
            mine = lane // HEAD_DIM == head
            part = jnp.where(mine, query, jnp.zeros_like(query)) * jnp.asarray(0.125, low)
            top = None
            for tile in range(keys):
                scores = dot_nt(key_tile(k_ref, tile, half, side), part)
                if tile >= open_tiles:
                    scores = jnp.where(masks[tile], scores, masked_score)
                s_ref[head, tile * tile_rows : (tile + 1) * tile_rows, :] = scores
                peak = jnp.max(groups(scores), axis=0)
                top = peak if top is None else jnp.maximum(top, peak)
            top = jnp.max(top, axis=0, keepdims=True)
            total = None
            acc = None
            for tile in range(keys):
                expo = jnp.exp(s_ref[head, tile * tile_rows : (tile + 1) * tile_rows, :] - top)
                piece = jnp.sum(groups(expo), axis=0)
                total = piece if total is None else total + piece
                columns = slice((tile % half) * tile_rows, (tile % half + 1) * tile_rows)
                values = v_ref[
                    (tile // half) ^ side, head * HEAD_DIM : (head + 1) * HEAD_DIM, columns
                ]
                piece = dot_nn(values, expo.astype(low))
                acc = piece if acc is None else acc + piece
            total = jnp.sum(total, axis=0, keepdims=True)
            mixed.append(acc / total)
            lse_ref[head : head + 1, :] = top + jnp.log(total)
        out = jnp.transpose(jnp.concatenate(mixed, axis=0)).astype(low)
        owned = (step // half) ^ side == 0

        @pl.when(owned)
        def _():
            own_ref[...] = out

        @pl.when(jnp.logical_not(owned))
        def _():
            other_ref[...] = out

    for n, bounds in enumerate(variants(count)):
        pl.when(step // 2 == n)(functools.partial(variant, *bounds))


def attend_forward(meta, qkv, values_turned, ids, first, pairs):
    sides, rows, _ = qkv.shape
    length = sides * rows
    count = length // tile_rows
    half = rows // tile_rows
    head_cols = 128 * pairs
    own, other = row_tile(half, 0), row_tile(half, 1)
    return pl.pallas_call(
        functools.partial(attend_forward_body, count, half),
        grid_spec=pltpu.PrefetchScalarGridSpec(
            num_scalar_prefetch=1,
            grid=(pairs, count),
            in_specs=[
                pl.BlockSpec(
                    (None, tile_rows, 128),
                    lambda h, i, c: ((i // half) ^ c[0], i % half, 3 * (h + first)),
                ),
                pl.BlockSpec((sides, rows, 128), lambda h, i, c: (0, 0, 3 * (h + first) + 1)),
                pl.BlockSpec((sides, 128, rows), lambda h, i, c: (0, h + first, 0)),
                pl.BlockSpec((1, length), lambda h, i, c: (0, 0)),
            ],
            out_specs=[
                pl.BlockSpec((tile_rows, 128), lambda h, i, c: (own(i, c), h)),
                pl.BlockSpec((tile_rows, 128), lambda h, i, c: (other(i, c), h)),
                pl.BlockSpec((None, 2, tile_rows), lambda h, i, c: (h, 0, i)),
            ],
            scratch_shapes=[pltpu.VMEM((2, length, tile_rows), wide)],
        ),
        out_shape=[
            jax.ShapeDtypeStruct((rows, head_cols), low),
            jax.ShapeDtypeStruct((rows, head_cols), low),
            jax.ShapeDtypeStruct((pairs, 2, length), wide),
        ],
        cost_estimate=cost(14 * pairs),
        name="attend_forward",
    )(meta, qkv, qkv, values_turned, ids)


def attend_backward_body(
    count, half, col_ref, q_ref, k_ref, v_ref, kt_ref, g_ref, g_other_ref, ids_ref, lse_ref,
    own_ref, other_ref, sum_ref, p_ref, gp_ref, gq_ref, gk_acc, gv_acc,
):
    step, head = pl.program_id(1), pl.program_id(2)
    side = col_ref[0]
    lane = lax.broadcasted_iota(jnp.int32, (tile_rows, 128), 1)
    mine = lane // HEAD_DIM == head
    own_ids = ids_ref[:, pl.ds(pl.multiple_of(step * tile_rows, tile_rows), tile_rows)]
    spot = pl.ds(pl.multiple_of(head * HEAD_DIM, HEAD_DIM), HEAD_DIM)

    def store(tile, place, values):
        start = pl.multiple_of((tile % half) * tile_rows, tile_rows)
        here = (pl.ds(start, tile_rows), slice(place * 128, (place + 1) * 128))
        owned = (tile // half) ^ side == 0

        @pl.when(owned)
        def _():
            own_ref[here] = values

        @pl.when(jnp.logical_not(owned))
        def _():
            other_ref[here] = values

    @pl.when((step == 0) & (head == 0))
    def _():
        gk_acc[...] = jnp.zeros_like(gk_acc)
        gv_acc[...] = jnp.zeros_like(gv_acc)
        sum_ref[...] = jnp.zeros_like(sum_ref)

    def groups(values):
        return jnp.sum(values.reshape(tile_rows // 8, 8, tile_rows), axis=0)

    def variant(open_tiles, keys):
        query = q_ref[...]
        grad = jnp.where((step // half) ^ side == 0, g_ref[...], g_other_ref[...])
        part = jnp.where(mine, query, jnp.zeros_like(query)) * jnp.asarray(0.125, low)
        grad_part = jnp.where(mine, grad, jnp.zeros_like(grad))
        query_ids = own_ids.astype(wide)
        log_sum = jnp.where(head == 0, lse_ref[:1, :], lse_ref[1:, :])
        inner = None
        for tile in range(keys):
            here = slice(tile * tile_rows, (tile + 1) * tile_rows)
            scores = dot_nt(key_tile(k_ref, tile, half, side), part)
            grad_probs = dot_nt(key_tile(v_ref, tile, half, side), grad_part)
            gp_ref[here, :] = grad_probs
            probs = jnp.exp(scores - log_sum)
            if tile >= open_tiles:
                column = column_of(ids_ref[:, here])
                allowed = jnp.concatenate([column, column], axis=1) <= query_ids
                probs = jnp.where(allowed, probs, 0.0)
            p_ref[here, :] = probs
            piece = groups(probs * grad_probs)
            inner = piece if inner is None else inner + piece
            gv_acc[here, :] += dot_nn(probs.astype(low), grad_part)
        inner = jnp.sum(inner, axis=0, keepdims=True)
        grad_query = None
        for tile in range(keys):
            here = slice(tile * tile_rows, (tile + 1) * tile_rows)
            columns = slice((tile % half) * tile_rows, (tile % half + 1) * tile_rows)
            slopes = (p_ref[here, :] * (gp_ref[here, :] - inner)).astype(low)
            gk_acc[here, :] += dot_nn(slopes, part)
            piece = dot_nn(kt_ref[(tile // half) ^ side, spot, columns], slopes)
            grad_query = piece if grad_query is None else grad_query + piece
        gq_ref[spot, :] = grad_query

    for n, bounds in enumerate(variants(count)):
        pl.when(step // 2 == n)(functools.partial(variant, *bounds))

    @pl.when(head == 1)
    def _():
        out = jnp.transpose(gq_ref[...] * 0.125).astype(low)
        store(step, 0, out)
        sum_ref[0:1, :] += jnp.sum(out.astype(wide), axis=0, keepdims=True)

    @pl.when((step == count - 1) & (head == 1))
    def _():
        def finish(tile, _):
            here = pl.ds(pl.multiple_of(tile * tile_rows, tile_rows), tile_rows)
            grad_value = gv_acc[here, :].astype(low)
            store(tile, 1, gk_acc[here, :].astype(low))
            store(tile, 2, grad_value)
            sum_ref[1:2, :] += jnp.sum(grad_value.astype(wide), axis=0, keepdims=True)

        lax.fori_loop(0, count, finish, None)


def attend_backward(
    meta, qkv, keys_turned, grad, grad_other, ids, log_sums, first, pairs, lse_first
):
    sides, rows, _ = qkv.shape
    length = sides * rows
    count = length // tile_rows
    half = rows // tile_rows
    own, other = row_tile(half, 0), row_tile(half, 1)
    whole = pl.BlockSpec((rows, 384), lambda h, i, e, c: (0, h))
    return pl.pallas_call(
        functools.partial(attend_backward_body, count, half),
        grid_spec=pltpu.PrefetchScalarGridSpec(
            num_scalar_prefetch=1,
            grid=(pairs, count, 2),
            in_specs=[
                pl.BlockSpec(
                    (None, tile_rows, 128),
                    lambda h, i, e, c: ((i // half) ^ c[0], i % half, 3 * (h + first)),
                ),
                pl.BlockSpec((sides, rows, 128), lambda h, i, e, c: (0, 0, 3 * (h + first) + 1)),
                pl.BlockSpec((sides, rows, 128), lambda h, i, e, c: (0, 0, 3 * (h + first) + 2)),
                pl.BlockSpec((sides, 128, rows), lambda h, i, e, c: (0, h + first, 0)),
                pl.BlockSpec((tile_rows, 128), lambda h, i, e, c: (own(i, c), h + first)),
                pl.BlockSpec((tile_rows, 128), lambda h, i, e, c: (other(i, c), h + first)),
                pl.BlockSpec((1, length), lambda h, i, e, c: (0, 0)),
                pl.BlockSpec((None, 2, tile_rows), lambda h, i, e, c: (h + lse_first, 0, i)),
            ],
            out_specs=[whole, whole, pl.BlockSpec((8, 128), lambda h, i, e, c: (0, h))],
            scratch_shapes=[
                pltpu.VMEM((length, tile_rows), wide),
                pltpu.VMEM((length, tile_rows), wide),
                pltpu.VMEM((128, tile_rows), wide),
                pltpu.VMEM((length, 128), wide),
                pltpu.VMEM((length, 128), wide),
            ],
        ),
        out_shape=[jax.ShapeDtypeStruct((rows, 384 * pairs), low)] * 2
        + [jax.ShapeDtypeStruct((8, 128 * pairs), wide)],
        cost_estimate=cost(25 * pairs),
        name="attend_backward",
    )(meta, qkv, qkv, qkv, keys_turned, grad, grad_other, ids, log_sums)


def norm_parts(values):
    mean = jnp.mean(values, axis=-1, keepdims=True)
    centred = values - mean
    inverse = lax.rsqrt(jnp.mean(centred * centred, axis=-1, keepdims=True) + norm_eps)
    return centred * inverse, inverse


def norm_back(grad_normed, unit, inverse, gain):
    grad_unit = grad_normed * gain
    first_mean = jnp.mean(grad_unit, axis=-1, keepdims=True)
    second_mean = jnp.mean(grad_unit * unit, axis=-1, keepdims=True)
    return inverse * (grad_unit - first_mean - unit * second_mean)


erfc_terms = (
    -0.12664913241116757, 0.4719797697046255, -0.4849989149703286, 0.5173882238837517,
    -0.0742751946996765, 0.20647784419749105, 0.15044607588806108, 0.17042678586105697,
    0.16920458065681523,
)


def gelu_with_slope(values):
    turned = 1.0 / (1.0 + (0.3 * 0.5**0.5) * jnp.abs(values))
    bell = jnp.exp(-0.5 * (values * values))
    series = jnp.full_like(values, 0.5 * erfc_terms[0])
    for term in erfc_terms[1:]:
        series = series * turned + 0.5 * term
    tail = series * turned * bell
    below = jnp.where(values < 0.0, tail, 1.0 - tail)
    return values * below, below + values * (bell * (0.5 / jnp.pi) ** 0.5)


def swap(values, axis, distance):
    size = lax.axis_size(axis)
    return lax.ppermute(values, axis, [(i, i ^ distance) for i in range(size)])


def gather_near(shard):
    return swap(shard, "row", 1), swap(shard, "row", 2)


def gather_far(shard, from_x, from_y):
    cut = shard.shape[0] // 2
    first_xy = swap(from_x[:cut], "row", 2)
    second_xy = swap(from_y[cut:], "row", 1)
    return [(0, 0, shard), (1, 0, from_x), (2, 0, from_y), (3, 0, first_xy), (3, cut, second_xy)]


def piece_copies(layout, refs, target, row_index, shard_rows, sems):
    copies = []
    for n, ((distance, first, rows), ref) in enumerate(zip(layout, refs)):
        base = pl.multiple_of((row_index ^ distance) * shard_rows + first, 16)
        copies.append(pltpu.make_async_copy(ref, target.at[pl.ds(base, rows), :], sems.at[n]))
    return copies


def layout_of(pieces):
    return [(distance, first, piece.shape[0]) for distance, first, piece in pieces]


hbm = pl.BlockSpec(memory_space=pl.ANY)


def project_in_body(layout, tiles, meta_ref, mine_ref, other_ref, bias_ref, *rest):
    pieces = rest[: len(layout)]
    out_ref, turned_ref, keys_ref, values_ref, weight_out, weight, sems, out_sem = rest[len(layout) :]
    step = pl.program_id(0)
    keep = pltpu.make_async_copy(weight, weight_out, out_sem)

    def project(rows):
        out = (dot_nn(rows, weight[...]) + bias_ref[...]).astype(low)
        out_ref[...] = out
        turned_ref[...] = jnp.transpose(rows)
        for pair in range(out.shape[1] // 384):
            here = slice(128 * pair, 128 * (pair + 1))
            keys_ref[here, :] = jnp.transpose(out[:, 384 * pair + 128 : 384 * pair + 256])
            values_ref[here, :] = jnp.transpose(out[:, 384 * pair + 256 : 384 * (pair + 1)])

    @pl.when(step == 0)
    def _():
        copies = piece_copies(layout, pieces, weight, meta_ref[1], weight.shape[0] // 4, sems)
        for copy in copies:
            copy.start()
        for copy in copies:
            copy.wait()
        keep.start()

    @pl.when(step < tiles)
    def _():
        project(mine_ref[...])

    @pl.when(step >= tiles)
    def _():
        project(other_ref[...])

    @pl.when(step == 2 * tiles - 1)
    def _():
        keep.wait()


def project_in(meta, mine, other, bias, pieces):
    rows, model = mine.shape
    size = 2 * tile_rows
    tiles = rows // size
    width = pieces[0][2].shape[1]
    return pl.pallas_call(
        functools.partial(project_in_body, layout_of(pieces), tiles),
        grid_spec=pltpu.PrefetchScalarGridSpec(
            num_scalar_prefetch=1,
            grid=(2 * tiles,),
            in_specs=[
                pl.BlockSpec((size, model), lambda i, m: (jnp.minimum(i, tiles - 1), 0)),
                pl.BlockSpec((size, model), lambda i, m: (jnp.maximum(i - tiles, 0), 0)),
                pl.BlockSpec((1, width), lambda i, m: (0, 0)),
            ]
            + [hbm] * len(pieces),
            out_specs=[
                pl.BlockSpec((None, size, width), lambda i, m: (i // tiles, i % tiles, 0)),
                pl.BlockSpec((model, size), lambda i, m: (0, i)),
                pl.BlockSpec((None, width // 3, size), lambda i, m: (i // tiles, 0, i % tiles)),
                pl.BlockSpec((None, width // 3, size), lambda i, m: (i // tiles, 0, i % tiles)),
                hbm,
            ],
            scratch_shapes=[
                pltpu.VMEM((model, width), low),
                pltpu.SemaphoreType.DMA((len(pieces),)),
                pltpu.SemaphoreType.DMA(()),
            ],
        ),
        out_shape=[
            jax.ShapeDtypeStruct((2, rows, width), low),
            jax.ShapeDtypeStruct((model, 2 * rows), low),
            jax.ShapeDtypeStruct((2, width // 3, rows), low),
            jax.ShapeDtypeStruct((2, width // 3, rows), low),
            jax.ShapeDtypeStruct((model, width), low),
        ],
        cost_estimate=cost(7),
        name="project_in",
    )(meta, mine, other, bias, *[piece for _, _, piece in pieces])


def load_weights(layout, pieces, weight, meta_ref, sems):
    copies = []
    for side in range(2):
        copies += piece_copies(
            layout, pieces[side], weight.at[side], meta_ref[1], weight.shape[1] // 4, sems.at[side]
        )
    for copy in copies:
        copy.start()
    for copy in copies:
        copy.wait()


hidden_chunk = 768


def feed_body(
    layout, head_cols, hidden_cols, meta_ref, tok_ref, row_ref, mixed_ref, mixed_last_ref,
    got_ref, got_last_ref, cot_ref, vec_ref, up_bias_ref, *rest,
):
    count = len(layout)
    pieces = (rest[:count], rest[count : 2 * count])
    (
        out_ref, hidden_ref, grad_ref, two_ref, cot_turned_ref, branch_ref, middle_ref, own_ref,
        other_ref, sum_ref, bias_ref, weight, sems, mixer_ref, grad_two_ref,
    ) = rest[2 * count :]

    @pl.when(pl.program_id(0) == 0)
    def _():
        load_weights(layout, pieces, weight, meta_ref, sems)
        sum_ref[...] = jnp.zeros_like(sum_ref)
        bias_ref[...] = jnp.zeros_like(bias_ref)

    bias_out, gain, bias, bias_down = (vec_ref[n : n + 1, :] for n in range(4))
    cot = cot_ref[...]
    cot_turned_ref[...] = jnp.transpose(cot)
    start = tok_ref[...].astype(wide) + row_ref[...]
    cut = mixed_ref.shape[1]
    branch = dot_nt(mixed_ref[...], weight[0, :, :cut])
    branch = branch + dot_nt(mixed_last_ref[...], weight[0, :, cut:head_cols])
    branch = branch + dot_nt(got_ref[...], weight[1, :, :cut])
    branch = branch + dot_nt(got_last_ref[...], weight[1, :, cut:head_cols])
    middle = start + (branch + bias_out)
    unit, inverse = norm_parts(middle)
    two = (unit * gain + bias).astype(low)
    two_ref[...] = jnp.transpose(two)
    mixer_ref[...] = jnp.zeros_like(mixer_ref)
    grad_two_ref[...] = jnp.zeros_like(grad_two_ref)

    def visit(side, _):
        mixer = None
        grad_two = None
        for first in range(0, hidden_cols, hidden_chunk):
            here = slice(first, first + hidden_chunk)
            up = weight[side, :, head_cols + first : head_cols + first + hidden_chunk]
            at = head_cols + hidden_cols + first
            down = weight[side, :, at : at + hidden_chunk]
            hidden, slope = gelu_with_slope(dot_nn(two, up) + up_bias_ref[side, :, here])
            hidden = hidden.astype(low)
            hidden_ref[side, :, here] = hidden
            part = dot_nt(hidden, down)
            mixer = part if mixer is None else mixer + part
            grad_pre = (dot_nn(cot, down) * slope).astype(low)
            grad_ref[side, :, here] = grad_pre
            bias_ref[side, :, here] += jnp.sum(grad_pre.astype(wide), axis=0, keepdims=True)
            part = dot_nt(grad_pre, up)
            grad_two = part if grad_two is None else grad_two + part
        mixer_ref[...] += mixer
        grad_two_ref[...] += grad_two

    lax.fori_loop(0, 2, visit, None)
    mixer, grad_two = mixer_ref[...], grad_two_ref[...]
    out_ref[...] = (middle + (mixer + bias_down)).astype(low)
    cot = cot.astype(wide)
    grad_middle = cot + norm_back(grad_two, unit, inverse, gain)
    grad_branch = grad_middle.astype(low)
    middle_ref[...] = grad_middle
    branch_ref[...] = jnp.transpose(grad_branch)
    own_ref[...] = dot_nn(grad_branch, weight[0, :, :head_cols]).astype(low)
    other_ref[...] = dot_nn(grad_branch, weight[1, :, :head_cols]).astype(low)
    for n, values in enumerate((grad_branch.astype(wide), grad_two * unit, grad_two, cot)):
        sum_ref[n : n + 1, :] += jnp.sum(values, axis=0, keepdims=True)


def feed(meta, tokens, table_row, mixed, got, cot, vectors, up_bias, mine, other):
    rows, model = tokens.shape
    size = tile_rows
    head_cols = sum(part.shape[1] for part in mixed)
    hidden_cols = up_bias.shape[2]
    width = mine[0][2].shape[1]

    def tile(columns):
        return pl.BlockSpec((size, columns), lambda i, m: (i, 0))

    def fixed(*shape):
        return pl.BlockSpec(shape, lambda i, m: (0,) * len(shape))

    def turned(depth):
        return pl.BlockSpec((depth, size), lambda i, m: (0, i))

    def array(columns, dtype):
        return jax.ShapeDtypeStruct((rows, columns), dtype)

    flipped = jax.ShapeDtypeStruct((model, rows), low)
    return pl.pallas_call(
        functools.partial(feed_body, layout_of(mine), head_cols, hidden_cols),
        grid_spec=pltpu.PrefetchScalarGridSpec(
            num_scalar_prefetch=1,
            grid=(rows // size,),
            in_specs=[tile(model), fixed(1, model)]
            + [tile(part.shape[1]) for part in (*mixed, *got)]
            + [tile(model), fixed(8, model), fixed(2, 1, hidden_cols)]
            + [hbm] * (2 * len(mine)),
            out_specs=[tile(model)]
            + [pl.BlockSpec((2, size, hidden_cols), lambda i, m: (0, i, 0))] * 2
            + [turned(model)] * 3
            + [tile(model), tile(head_cols), tile(head_cols), fixed(8, model)]
            + [fixed(2, 1, hidden_cols)],
            scratch_shapes=[
                pltpu.VMEM((2, model, width), low),
                pltpu.SemaphoreType.DMA((2, len(mine))),
                pltpu.VMEM((size, model), wide),
                pltpu.VMEM((size, model), wide),
            ],
        ),
        out_shape=[array(model, low)]
        + [jax.ShapeDtypeStruct((2, rows, hidden_cols), low)] * 2
        + [flipped] * 3
        + [array(model, wide), array(head_cols, low), array(head_cols, low)]
        + [jax.ShapeDtypeStruct((8, model), wide)]
        + [jax.ShapeDtypeStruct((2, 1, hidden_cols), wide)],
        cost_estimate=cost(45),
        name="feed",
    )(
        meta, tokens, table_row, *mixed, *got, cot, vectors, up_bias,
        *[piece for _, _, piece in mine], *[piece for _, _, piece in other],
    )


def weight_parts_body(products, near, meta_ref, *refs):
    send_ref, keep_ref = refs[-2:]
    shard = send_ref.shape[0] // 2
    order = [pl.multiple_of((meta_ref[1] ^ d) * shard, 64) for d in (3, near, 3 - near, 0)]

    def in_order(ref):
        return jnp.concatenate([ref[pl.ds(start, shard), :] for start in order], axis=0)

    at = 0
    for lefts, arrived, first, tiles in products:
        inputs = refs[at : at + 2 * lefts + arrived]
        at += 2 * lefts + arrived

        @pl.when((pl.program_id(0) >= first) & (pl.program_id(0) < first + tiles))
        def _(inputs=inputs, lefts=lefts, arrived=arrived):
            total = None
            for n in range(lefts):
                part = dot_nn(in_order(inputs[2 * n]), inputs[2 * n + 1][...])
                total = part if total is None else total + part
            if arrived:
                total = total + in_order(inputs[-1]).astype(wide)
            total = total.astype(low)
            send_ref[...] = total[: 2 * shard]
            keep_ref[...] = total[2 * shard :]


def weight_parts(meta, products, near, micros):
    model = products[0][0][0][0].shape[0]
    operands, specs, shapes = [], [], []
    step = 384 if any(pairs[0][2].shape[-1] % 512 for pairs, _ in products) else 512
    first = 0
    for pairs, arrived in products:
        tiles = pairs[0][2].shape[-1] // step

        def tile(i, m, first=first, tiles=tiles):
            return (0, jnp.clip(i - first, 0, tiles - 1))

        for left, place, right in pairs:
            depth = right.shape[-2]
            specs.append(pl.BlockSpec((model, depth), lambda i, m, p=place: (0, p)))
            if right.ndim == 3:
                specs.append(pl.BlockSpec((None, depth, step), lambda i, m, t=tile: (0, *t(i, m))))
            else:
                specs.append(pl.BlockSpec((depth, step), tile))
            operands += [left, right]
        if arrived is not None:
            specs.append(pl.BlockSpec((model, step), tile))
            operands.append(arrived)
        shapes.append((len(pairs), int(arrived is not None), first, tiles))
        first += tiles
    half = jax.ShapeDtypeStruct((model // 2, first * step), low)
    return pl.pallas_call(
        functools.partial(weight_parts_body, shapes, near),
        grid_spec=pltpu.PrefetchScalarGridSpec(
            num_scalar_prefetch=1,
            grid=(first,),
            in_specs=specs,
            out_specs=[pl.BlockSpec((model // 2, step), lambda i, m: (0, i))] * 2,
        ),
        out_shape=[half, half],
        cost_estimate=cost(micros),
        name="weight_parts",
    )(meta, *operands)


def product_body(left_ref, right_ref, out_ref):
    out_ref[...] = dot_nn(left_ref[...], right_ref[...]).astype(low)


def product(left, right, micros):
    rows, depth = left.shape
    columns = right.shape[-1]
    step = 512 if columns % 512 == 0 else 384
    right_spec = pl.BlockSpec((depth, step), lambda i: (0, i))
    if right.ndim == 3:
        right_spec = pl.BlockSpec((None, depth, step), lambda i: (1, 0, i))
    return pl.pallas_call(
        product_body,
        grid=(columns // step,),
        in_specs=[pl.BlockSpec((rows, depth), lambda i: (0, 0)), right_spec],
        out_specs=pl.BlockSpec((rows, step), lambda i: (0, i)),
        out_shape=jax.ShapeDtypeStruct((rows, columns), low),
        cost_estimate=cost(micros),
        name="product",
    )(left, right)


def table_body(step_ref, sum_ref, out_ref):
    out_ref[...] = jnp.zeros_like(out_ref)

    def add(n, _):
        out_ref[pl.ds(step_ref[n], 1), :] += sum_ref[pl.ds(n, 1), :]

    lax.fori_loop(0, sum_ref.shape[0], add, None)


def table_rows(steps, sums, rows):
    return pl.pallas_call(
        table_body,
        grid_spec=pltpu.PrefetchScalarGridSpec(
            num_scalar_prefetch=1,
            grid=(1,),
            in_specs=[pl.BlockSpec(sums.shape, lambda i, t: (0, 0))],
            out_specs=pl.BlockSpec((rows, sums.shape[1]), lambda i, t: (0, 0)),
        ),
        out_shape=jax.ShapeDtypeStruct((rows, sums.shape[1]), wide),
        cost_estimate=cost(2),
        name="table_rows",
    )(steps, sums)


def pack_body(*refs):
    out_ref = refs[-1]
    for n in range(out_ref.shape[1] // 128):
        kind, pair = n % 3, n // 3
        out_ref[:, 128 * n : 128 * (n + 1)] = refs[kind][:, 128 * pair : 128 * (pair + 1)].astype(low)


def pack(*weights):
    rows, columns = weights[0].shape
    return pl.pallas_call(
        pack_body,
        out_shape=jax.ShapeDtypeStruct((rows, 3 * columns), low),
        cost_estimate=cost(1),
        name="pack",
    )(*weights)


def grad_in_body(cuts, tok_ref, row_ref, gain_ref, own_ref, other_ref, middle_ref, *rest):
    grads = rest[: 2 * len(cuts)]
    out_ref, sum_ref = rest[2 * len(cuts) :]

    @pl.when(pl.program_id(0) == 0)
    def _():
        sum_ref[...] = jnp.zeros_like(sum_ref)

    grad = None
    for n, (first, last) in enumerate(cuts):
        for values, weight in ((grads[2 * n], own_ref), (grads[2 * n + 1], other_ref)):
            part = dot_nt(values[...], weight[:, first:last])
            grad = part if grad is None else grad + part
    unit, inverse = norm_parts(tok_ref[...].astype(wide) + row_ref[...])
    tokens = middle_ref[...] + norm_back(grad, unit, inverse, gain_ref[...])
    out_ref[...] = tokens
    for n, values in enumerate((grad * unit, grad, tokens)):
        sum_ref[n : n + 1, :] += jnp.sum(values, axis=0, keepdims=True)


def grad_in(tokens, table_row, gain, own, other, grad_middle, grads):
    rows, model = tokens.shape
    size = tile_rows
    width = own.shape[1]
    cuts = []
    for mine, _ in grads:
        first = cuts[-1][1] if cuts else 0
        cuts.append((first, first + mine.shape[1]))

    def tile(columns):
        return pl.BlockSpec((size, columns), lambda i: (i, 0))

    def fixed(*shape):
        return pl.BlockSpec(shape, lambda i: (0, 0))

    flat = [values for pair in grads for values in pair]
    return pl.pallas_call(
        functools.partial(grad_in_body, cuts),
        grid=(rows // size,),
        in_specs=[
            tile(model), fixed(1, model), fixed(1, model), fixed(model, width),
            fixed(model, width), tile(model),
        ]
        + [tile(values.shape[1]) for values in flat],
        out_specs=[tile(model), fixed(8, model)],
        out_shape=[
            jax.ShapeDtypeStruct((rows, model), wide),
            jax.ShapeDtypeStruct((8, model), wide),
        ],
        cost_estimate=cost(9),
        name="grad_in",
    )(tokens, table_row, gain, own, other, grad_middle, *flat)


def after(values, *needed):
    needed = jax.tree.leaves(needed)
    return lax.optimization_barrier((values, *needed))[0] if needed else values


def line_steps(values):
    if lax.axis_size("dp") != 4:
        return lax.psum(values, "dp")
    for distance in (1, 2):
        arrived = swap(values, "dp", distance)
        token = yield values
        arrived = after(arrived, token)
        values = (values.astype(wide) + arrived.astype(wide)).astype(values.dtype)
    return values


def split_line_steps(values):
    if lax.axis_size("dp") != 4:
        return lax.psum(values, "dp")
    me = lax.axis_index("dp")
    first, second = me % 2, me // 2
    half = values.shape[0] // 2

    def take(array, place, count):
        return lax.dynamic_slice_in_dim(array, place * count, count, 0)

    def join(place, mine, other):
        swapped = jnp.concatenate([other, mine], axis=0)
        return jnp.where(place == 0, jnp.concatenate([mine, other], axis=0), swapped)

    for place, distance in ((first, 1), (second, 2)):
        sent = take(values, 1 - place, half)
        arrived = swap(sent, "dp", distance)
        token = yield sent
        arrived = after(arrived, token)
        values = (take(values, place, half).astype(wide) + arrived.astype(wide)).astype(low)
        half //= 2
    for place, distance in ((second, 2), (first, 1)):
        arrived = swap(values, "dp", distance)
        token = yield values
        values = join(place, values, after(arrived, token))
    return values


def weight_steps(parts, near, line=line_steps):
    send, keep = parts
    shard = send.shape[0] // 2
    arrived = swap(send, "row", near)
    token = yield send
    arrived = after(arrived, token)
    passed = (keep[:shard].astype(wide) + arrived[:shard].astype(wide)).astype(low)
    last = swap(passed, "row", 3 - near)
    token = yield passed
    last = after(last, token)
    share = keep[shard:].astype(wide) + arrived[shard:].astype(wide) + last.astype(wide)
    total = yield from line(share.astype(low))
    return total.astype(wide)


def vector_steps(values):
    for axis, distance in (("row", 1), ("row", 2)):
        arrived = swap(values, axis, distance)
        token = yield values
        values = values + after(arrived, token)
    total = yield from line_steps(values)
    return total


class Chains:
    def __init__(self):
        self.steps, self.done = [], {}

    def add(self, steps):
        self.steps.append(steps)
        return [next(steps)]

    def advance(self, token=None, chosen=None):
        sent = []
        for n, steps in enumerate(self.steps):
            if n not in self.done and (chosen is None or n in chosen):
                try:
                    sent.append(steps.send(token))
                except StopIteration as stop:
                    self.done[n] = stop.value
        return sent


def shards(
    tokens, timesteps, block_ids, table, gain_one, bias_one, w_query, w_key, w_value, b_query,
    b_value, w_out, b_out, gain_two, bias_two, w_up, b_up, w_down, b_down, cotangent,
):
    seq_count, local_len, model_width = tokens.shape
    row_size, dp_size = lax.axis_size("row"), lax.axis_size("dp")
    assert seq_count == 1 and lax.axis_size("col") == 2 and row_size == 4
    head_cols = w_query.shape[1]
    hidden_cols = w_up.shape[1]
    col_index = lax.axis_index("col")
    row_index = lax.axis_index("row")
    seq_index = lax.axis_index("dp") * row_size + row_index
    seq_total = dp_size * row_size
    meta = jnp.stack([col_index, row_index]).astype(jnp.int32)

    cuts = [slice(first, first + 128) for first in range(0, head_cols, 128)]
    group_one = pack(w_query, w_key, w_value)
    in_bias = jnp.concatenate(
        [part for cut in cuts for part in (b_query[cut], jnp.zeros_like(b_query[cut]), b_value[cut])]
    )[None]
    in_pieces = gather_far(group_one, *gather_near(group_one))
    group_two = jnp.concatenate([w_out.T, w_up, w_down.T], axis=1).astype(low)
    group_two = after(group_two, in_pieces[3][2], in_pieces[4][2])
    near_x, near_y = gather_near(group_two)

    table_row = lax.dynamic_slice_in_dim(table, timesteps[0], 1, 0)
    unit_one, _ = norm_parts(tokens[0].astype(wide) + table_row)
    rows_mine = (unit_one * gain_one + bias_one).astype(low)
    rows_other = swap(rows_mine, "col", 1)
    up_bias = jnp.stack([b_up, swap(b_up, "col", 1)])[:, None]
    qkv, rows_turned, keys_turned, values_turned, in_own = project_in(
        meta, rows_mine, after(rows_other, up_bias), in_bias, in_pieces
    )
    in_other = swap(in_own, "col", 1)
    shard_other = swap(group_two, "col", 1)
    pairs = head_cols // 128
    mixed, mixed_other, log_sums = attend_forward(
        meta, qkv, values_turned, block_ids, 0, pairs - 1
    )
    got = swap(mixed_other, "col", 1)
    near_x, near_y = after(near_x, mixed), after(near_y, mixed)
    near_x_other, near_y_other = swap(near_x, "col", 1), swap(near_y, "col", 1)
    mine = gather_far(group_two, near_x, near_y)
    mixed_last, mixed_last_other, log_sums_last = attend_forward(
        meta, after(qkv, in_other, shard_other, got, near_x_other, near_y_other), values_turned,
        block_ids, pairs - 1, 1,
    )
    got_last = swap(mixed_last_other, "col", 1)
    far = [after(piece, mixed_last) for _, _, piece in mine[3:]]
    others = [shard_other, near_x_other, near_y_other] + [swap(piece, "col", 1) for piece in far]
    other = [(distance, first, piece) for (distance, first, _), piece in zip(mine, others)]

    spare = jnp.zeros_like(b_out)
    vectors = jnp.stack([b_out, gain_two, bias_two, b_down, spare, spare, spare, spare])
    cot = cotangent[0]
    (
        layer_out, hidden, grad_hidden, two_turned, cot_turned, branch_turned,
        grad_middle, grad_own, grad_other, sums, grad_up_bias,
    ) = feed(
        meta, tokens[0], table_row, (mixed, mixed_last), (got, got_last), cot, vectors, up_bias,
        mine, other,
    )
    up_arrived = swap(product(two_turned, grad_hidden, 4), "col", 1)
    down_arrived = swap(product(cot_turned, hidden, 4), "col", 1)
    grad_got = swap(grad_other, "col", 1)
    up_parts = weight_parts(meta, [([(two_turned, 0, grad_hidden)], up_arrived)], 1, 6)
    chains = Chains()
    chains.add(weight_steps(up_parts, 1, split_line_steps))
    down_parts = weight_parts(
        meta, [([(cot_turned, 0, hidden)], after(down_arrived, *up_parts))], 2, 6
    )
    chains.add(weight_steps(down_parts, 2, split_line_steps))
    grad_b_up = grad_up_bias[0, 0] + swap(grad_up_bias[1, 0], "col", 1)
    before = [*up_parts, *down_parts, grad_b_up]

    own_grads, aways, gots, bias_sums = [], [], [], []
    for pair in range(pairs):
        last = pair == pairs - 1
        own, away, bias_sum = attend_backward(
            meta, after(qkv, *before), keys_turned, grad_own, grad_got, block_ids,
            log_sums_last if last else log_sums, pair, 1, 0 if last else pair,
        )
        own_grads.append(own)
        gots.append(swap(away, "col", 1))
        bias_sums.append(bias_sum)
        before = [*chains.advance(own), gots[-1]]
        aways.append(away)
        if pair == 0:
            out_sent = product(
                branch_turned, after(jnp.concatenate([got, got_last], axis=1), *before), 2
            )
            out_arrived = swap(out_sent, "col", 1)
            before.append(out_sent)
            continue
        if pair == pairs - 2:
            out_keep = jnp.concatenate([mixed, mixed_last], axis=1)
            products = [([(branch_turned, 0, out_keep)], out_arrived)]
            ours, theirs = own_grads, aways
        else:
            products, ours, theirs = [], [own], [away]
        near = 1 if last else 2
        products += [([(rows_turned, 0, a), (rows_turned, 1, b)], None) for a, b in zip(ours, theirs)]
        parts = weight_parts(meta, products, near, 3 * len(products))
        before += parts
        chains.add(weight_steps(parts, near, line_steps if last else split_line_steps))
    grad_tokens, late_sums = grad_in(
        after(tokens[0], *before), table_row, gain_one[None], in_own, in_other, grad_middle,
        list(zip(own_grads, gots)),
    )
    chains.advance(grad_tokens)
    bias_sums = [after(part, grad_tokens) for part in bias_sums]

    shared = jnp.concatenate([late_sums[:3], sums[:4]])
    shared = shared + swap(shared, "col", 1)
    slot = lax.broadcasted_iota(jnp.int32, (seq_total, 1), 0) == seq_index
    packed = jnp.concatenate(
        [
            jnp.concatenate([shared[:2], shared[3:]]).reshape(-1),
            jnp.concatenate([part[:1] for part in bias_sums], axis=1).reshape(-1),
            jnp.concatenate([part[1:2] for part in bias_sums], axis=1).reshape(-1),
            grad_b_up,
            jnp.where(slot, shared[2:3], 0.0).reshape(-1),
            jnp.where(slot, timesteps[0].astype(wide), 0.0).reshape(-1),
        ]
    )
    pad = -packed.shape[0] % 1024
    chains.add(vector_steps(jnp.pad(packed, (0, pad)).reshape(-1, 128)))
    sent = None
    for chain in (4, 2, 4, 3, 0, 1, 4, 3, 2, 4, 3, 2, 0, 1, 2):
        sent = chains.advance(sent, (chain,)) or sent
        if 4 in chains.done:
            sent = chains.done[4]
    while len(chains.done) < len(chains.steps):
        chains.advance(sent)
    done = chains.done
    own_up, own_down = done[0], done[1]
    own_out, done[2] = done[2][:, :head_cols], done[2][:, head_cols:]
    own_in = jnp.concatenate([done[2], done[3]], axis=1)
    own_in = [
        jnp.concatenate([own_in[:, 128 * n : 128 * (n + 1)] for n in range(kind, 3 * pairs, 3)], axis=1)
        for kind in range(3)
    ]
    packed = done[4].reshape(-1)
    place = 0
    taken = []
    for size in (6 * model_width, 2 * head_cols, hidden_cols, seq_total * model_width, seq_total):
        taken.append(packed[place : place + size])
        place += size
    six = taken[0].reshape(6, model_width)
    grad_table = table_rows(
        taken[4].astype(jnp.int32), taken[3].reshape(seq_total, model_width), table.shape[0]
    )
    return (
        layer_out[None],
        grad_tokens[None],
        grad_table,
        six[0],
        six[1],
        own_in[0],
        own_in[1],
        own_in[2],
        taken[1][:head_cols],
        taken[1][head_cols:],
        own_out.T,
        six[2],
        six[3],
        six[4],
        own_up,
        taken[2],
        own_down.T,
        six[5],
    )


def solution(mesh):
    return jax.shard_map(
        shards,
        mesh=mesh,
        in_specs=(
            P(("dp", "row"), "col", None),
            P(("dp", "row")),
            P(("dp", "row"), None),
            P(),
            P(),
            P(),
            P("row", "col"),
            P("row", "col"),
            P("row", "col"),
            P("col"),
            P("col"),
            P("col", "row"),
            P(),
            P(),
            P(),
            P("row", "col"),
            P("col"),
            P("col", "row"),
            P(),
            P(("dp", "row"), "col", None),
        ),
        out_specs=(
            P(("dp", "row"), "col", None),
            P(("dp", "row"), "col", None),
            P(),
            P(),
            P(),
            P("row", "col"),
            P("row", "col"),
            P("row", "col"),
            P("col"),
            P("col"),
            P("col", "row"),
            P(),
            P(),
            P(),
            P("row", "col"),
            P("col"),
            P("col", "row"),
            P(),
        ),
        check_vma=False,
    )
```

```python
import functools

import jax
import jax.numpy as jnp
from jax import lax
from jax.experimental import pallas as pl
from jax.experimental.pallas import tpu as pltpu
from jax.sharding import PartitionSpec as P

HEAD_DIM = 64
norm_eps = 1e-05
masked_score = -1000000000.0
low = jnp.bfloat16
wide = jnp.float32
tile_rows = 256


def cost(micros):
    return pl.CostEstimate(flops=int(micros * 1.1e9), transcendentals=0, bytes_accessed=1 << 20)


def dot_nn(left, right):
    return lax.dot_general(left, right, (((1,), (0,)), ((), ())), preferred_element_type=wide)


def dot_nt(left, right):
    return lax.dot_general(left, right, (((1,), (1,)), ((), ())), preferred_element_type=wide)


def dot_tn(left, right):
    return lax.dot_general(left, right, (((0,), (0,)), ((), ())), preferred_element_type=wide)


def column_of(ids_row):
    parts = []
    for start in range(0, ids_row.shape[1], 128):
        piece = ids_row[:, start : start + 128].astype(wide)
        parts.append(jnp.transpose(jnp.broadcast_to(piece, (128, 128))))
    return jnp.concatenate(parts, axis=0)


def lanes(values):
    return [values[:, first : first + 128] for first in range(0, values.shape[1], 128)]


def variants(count):
    return [(2 * n, min(2 * n + 3, count)) for n in range(count // 2)]


def key_tile(ref, tile, half, side):
    rows = slice((tile % half) * tile_rows, (tile % half + 1) * tile_rows)
    return ref[(tile // half) ^ side, rows, :]


def allowed_part(ids_ref, ids_column, first):
    return ids_ref[:, first : first + 128].astype(wide) <= ids_column


def row_tile(half, shift):
    return lambda i, c: jnp.clip(i - half * (c[0] ^ shift), 0, half - 1)


def attend_forward_body(
    count, half, col_ref, q_ref, k_ref, v_ref, ids_ref, own_ref, other_ref, lse_ref, s_ref
):
    step = pl.program_id(1)
    side = col_ref[0]
    lane = lax.broadcasted_iota(jnp.int32, (tile_rows, 128), 1)
    own_ids = ids_ref[:, pl.ds(pl.multiple_of(step * tile_rows, tile_rows), tile_rows)]

    def groups(values):
        return values.reshape(tile_rows // 8, 8, tile_rows)

    def variant(open_tiles, keys):
        query = q_ref[...]
        query_ids = own_ids.astype(wide)
        masks = {}
        for tile in range(open_tiles, keys):
            column = column_of(ids_ref[:, tile * tile_rows : (tile + 1) * tile_rows])
            masks[tile] = jnp.concatenate([column, column], axis=1) <= query_ids
        mixed = []
        for head in range(2):
            mine = lane // HEAD_DIM == head
            part = jnp.where(mine, query, jnp.zeros_like(query)) * jnp.asarray(0.125, low)
            top = None
            for tile in range(keys):
                scores = dot_nt(key_tile(k_ref, tile, half, side), part)
                if tile >= open_tiles:
                    scores = jnp.where(masks[tile], scores, masked_score)
                s_ref[head, tile * tile_rows : (tile + 1) * tile_rows, :] = scores
                peak = jnp.max(groups(scores), axis=0)
                top = peak if top is None else jnp.maximum(top, peak)
            top = jnp.max(top, axis=0, keepdims=True)
            total = None
            acc = None
            for tile in range(keys):
                expo = jnp.exp(s_ref[head, tile * tile_rows : (tile + 1) * tile_rows, :] - top)
                piece = jnp.sum(groups(expo), axis=0)
                total = piece if total is None else total + piece
                columns = slice((tile % half) * tile_rows, (tile % half + 1) * tile_rows)
                values = v_ref[
                    (tile // half) ^ side, head * HEAD_DIM : (head + 1) * HEAD_DIM, columns
                ]
                piece = dot_nn(values, expo.astype(low))
                acc = piece if acc is None else acc + piece
            total = jnp.sum(total, axis=0, keepdims=True)
            mixed.append(acc / total)
            lse_ref[head : head + 1, :] = top + jnp.log(total)
        out = jnp.transpose(jnp.concatenate(mixed, axis=0)).astype(low)
        owned = (step // half) ^ side == 0

        @pl.when(owned)
        def _():
            own_ref[...] = out

        @pl.when(jnp.logical_not(owned))
        def _():
            other_ref[...] = out

    for n, bounds in enumerate(variants(count)):
        pl.when(step // 2 == n)(functools.partial(variant, *bounds))


def attend_forward(meta, qkv, values_turned, ids, first, pairs):
    sides, rows, _ = qkv.shape
    length = sides * rows
    count = length // tile_rows
    half = rows // tile_rows
    head_cols = 128 * pairs
    own, other = row_tile(half, 0), row_tile(half, 1)
    return pl.pallas_call(
        functools.partial(attend_forward_body, count, half),
        grid_spec=pltpu.PrefetchScalarGridSpec(
            num_scalar_prefetch=1,
            grid=(pairs, count),
            in_specs=[
                pl.BlockSpec(
                    (None, tile_rows, 128),
                    lambda h, i, c: ((i // half) ^ c[0], i % half, 3 * (h + first)),
                ),
                pl.BlockSpec((sides, rows, 128), lambda h, i, c: (0, 0, 3 * (h + first) + 1)),
                pl.BlockSpec((sides, 128, rows), lambda h, i, c: (0, h + first, 0)),
                pl.BlockSpec((1, length), lambda h, i, c: (0, 0)),
            ],
            out_specs=[
                pl.BlockSpec((tile_rows, 128), lambda h, i, c: (own(i, c), h)),
                pl.BlockSpec((tile_rows, 128), lambda h, i, c: (other(i, c), h)),
                pl.BlockSpec((None, 2, tile_rows), lambda h, i, c: (h, 0, i)),
            ],
            scratch_shapes=[pltpu.VMEM((2, length, tile_rows), wide)],
        ),
        out_shape=[
            jax.ShapeDtypeStruct((rows, head_cols), low),
            jax.ShapeDtypeStruct((rows, head_cols), low),
            jax.ShapeDtypeStruct((pairs, 2, length), wide),
        ],
        cost_estimate=cost(14 * pairs),
        name="attend_forward",
    )(meta, qkv, qkv, values_turned, ids)


def attend_backward_body(
    count, half, col_ref, q_ref, k_ref, v_ref, kt_ref, g_ref, g_other_ref, ids_ref, lse_ref,
    own_ref, other_ref, sum_ref, p_ref, gp_ref, gq_ref, gk_acc, gv_acc,
):
    step, head = pl.program_id(1), pl.program_id(2)
    side = col_ref[0]
    lane = lax.broadcasted_iota(jnp.int32, (tile_rows, 128), 1)
    mine = lane // HEAD_DIM == head
    own_ids = ids_ref[:, pl.ds(pl.multiple_of(step * tile_rows, tile_rows), tile_rows)]
    spot = pl.ds(pl.multiple_of(head * HEAD_DIM, HEAD_DIM), HEAD_DIM)

    def store(tile, place, values):
        start = pl.multiple_of((tile % half) * tile_rows, tile_rows)
        here = (pl.ds(start, tile_rows), slice(place * 128, (place + 1) * 128))
        owned = (tile // half) ^ side == 0

        @pl.when(owned)
        def _():
            own_ref[here] = values

        @pl.when(jnp.logical_not(owned))
        def _():
            other_ref[here] = values

    @pl.when((step == 0) & (head == 0))
    def _():
        gk_acc[...] = jnp.zeros_like(gk_acc)
        gv_acc[...] = jnp.zeros_like(gv_acc)
        sum_ref[...] = jnp.zeros_like(sum_ref)

    def groups(values):
        return jnp.sum(values.reshape(tile_rows // 8, 8, tile_rows), axis=0)

    def variant(open_tiles, keys):
        query = q_ref[...]
        grad = jnp.where((step // half) ^ side == 0, g_ref[...], g_other_ref[...])
        part = jnp.where(mine, query, jnp.zeros_like(query)) * jnp.asarray(0.125, low)
        grad_part = jnp.where(mine, grad, jnp.zeros_like(grad))
        query_ids = own_ids.astype(wide)
        log_sum = jnp.where(head == 0, lse_ref[:1, :], lse_ref[1:, :])
        inner = None
        for tile in range(keys):
            here = slice(tile * tile_rows, (tile + 1) * tile_rows)
            scores = dot_nt(key_tile(k_ref, tile, half, side), part)
            grad_probs = dot_nt(key_tile(v_ref, tile, half, side), grad_part)
            gp_ref[here, :] = grad_probs
            probs = jnp.exp(scores - log_sum)
            if tile >= open_tiles:
                column = column_of(ids_ref[:, here])
                allowed = jnp.concatenate([column, column], axis=1) <= query_ids
                probs = jnp.where(allowed, probs, 0.0)
            p_ref[here, :] = probs
            piece = groups(probs * grad_probs)
            inner = piece if inner is None else inner + piece
            gv_acc[here, :] += dot_nn(probs.astype(low), grad_part)
        inner = jnp.sum(inner, axis=0, keepdims=True)
        grad_query = None
        for tile in range(keys):
            here = slice(tile * tile_rows, (tile + 1) * tile_rows)
            columns = slice((tile % half) * tile_rows, (tile % half + 1) * tile_rows)
            slopes = (p_ref[here, :] * (gp_ref[here, :] - inner)).astype(low)
            gk_acc[here, :] += dot_nn(slopes, part)
            piece = dot_nn(kt_ref[(tile // half) ^ side, spot, columns], slopes)
            grad_query = piece if grad_query is None else grad_query + piece
        gq_ref[spot, :] = grad_query

    for n, bounds in enumerate(variants(count)):
        pl.when(step // 2 == n)(functools.partial(variant, *bounds))

    @pl.when(head == 1)
    def _():
        out = jnp.transpose(gq_ref[...] * 0.125).astype(low)
        store(step, 0, out)
        sum_ref[0:1, :] += jnp.sum(out.astype(wide), axis=0, keepdims=True)

    @pl.when((step == count - 1) & (head == 1))
    def _():
        def finish(tile, _):
            here = pl.ds(pl.multiple_of(tile * tile_rows, tile_rows), tile_rows)
            grad_value = gv_acc[here, :].astype(low)
            store(tile, 1, gk_acc[here, :].astype(low))
            store(tile, 2, grad_value)
            sum_ref[1:2, :] += jnp.sum(grad_value.astype(wide), axis=0, keepdims=True)

        lax.fori_loop(0, count, finish, None)


def attend_backward(
    meta, qkv, keys_turned, grad, grad_other, ids, log_sums, first, pairs, lse_first
):
    sides, rows, _ = qkv.shape
    length = sides * rows
    count = length // tile_rows
    half = rows // tile_rows
    own, other = row_tile(half, 0), row_tile(half, 1)
    whole = pl.BlockSpec((rows, 384), lambda h, i, e, c: (0, h))
    return pl.pallas_call(
        functools.partial(attend_backward_body, count, half),
        grid_spec=pltpu.PrefetchScalarGridSpec(
            num_scalar_prefetch=1,
            grid=(pairs, count, 2),
            in_specs=[
                pl.BlockSpec(
                    (None, tile_rows, 128),
                    lambda h, i, e, c: ((i // half) ^ c[0], i % half, 3 * (h + first)),
                ),
                pl.BlockSpec((sides, rows, 128), lambda h, i, e, c: (0, 0, 3 * (h + first) + 1)),
                pl.BlockSpec((sides, rows, 128), lambda h, i, e, c: (0, 0, 3 * (h + first) + 2)),
                pl.BlockSpec((sides, 128, rows), lambda h, i, e, c: (0, h + first, 0)),
                pl.BlockSpec((tile_rows, 128), lambda h, i, e, c: (own(i, c), h + first)),
                pl.BlockSpec((tile_rows, 128), lambda h, i, e, c: (other(i, c), h + first)),
                pl.BlockSpec((1, length), lambda h, i, e, c: (0, 0)),
                pl.BlockSpec((None, 2, tile_rows), lambda h, i, e, c: (h + lse_first, 0, i)),
            ],
            out_specs=[whole, whole, pl.BlockSpec((8, 128), lambda h, i, e, c: (0, h))],
            scratch_shapes=[
                pltpu.VMEM((length, tile_rows), wide),
                pltpu.VMEM((length, tile_rows), wide),
                pltpu.VMEM((128, tile_rows), wide),
                pltpu.VMEM((length, 128), wide),
                pltpu.VMEM((length, 128), wide),
            ],
        ),
        out_shape=[jax.ShapeDtypeStruct((rows, 384 * pairs), low)] * 2
        + [jax.ShapeDtypeStruct((8, 128 * pairs), wide)],
        cost_estimate=cost(25 * pairs),
        name="attend_backward",
    )(meta, qkv, qkv, qkv, keys_turned, grad, grad_other, ids, log_sums)


def norm_parts(values):
    mean = jnp.mean(values, axis=-1, keepdims=True)
    centred = values - mean
    inverse = lax.rsqrt(jnp.mean(centred * centred, axis=-1, keepdims=True) + norm_eps)
    return centred * inverse, inverse


def norm_back(grad_normed, unit, inverse, gain):
    grad_unit = grad_normed * gain
    first_mean = jnp.mean(grad_unit, axis=-1, keepdims=True)
    second_mean = jnp.mean(grad_unit * unit, axis=-1, keepdims=True)
    return inverse * (grad_unit - first_mean - unit * second_mean)


erfc_terms = (
    -0.12664913241116757, 0.4719797697046255, -0.4849989149703286, 0.5173882238837517,
    -0.0742751946996765, 0.20647784419749105, 0.15044607588806108, 0.17042678586105697,
    0.16920458065681523,
)


def gelu_with_slope(values):
    turned = 1.0 / (1.0 + (0.3 * 0.5**0.5) * jnp.abs(values))
    bell = jnp.exp(-0.5 * (values * values))
    series = jnp.full_like(values, 0.5 * erfc_terms[0])
    for term in erfc_terms[1:]:
        series = series * turned + 0.5 * term
    tail = series * turned * bell
    below = jnp.where(values < 0.0, tail, 1.0 - tail)
    return values * below, below + values * (bell * (0.5 / jnp.pi) ** 0.5)


def swap(values, axis, distance):
    size = lax.axis_size(axis)
    return lax.ppermute(values, axis, [(i, i ^ distance) for i in range(size)])


def gather_near(shard):
    return swap(shard, "row", 1), swap(shard, "row", 2)


def gather_far(shard, from_x, from_y):
    cut = shard.shape[0] // 2
    first_xy = swap(from_x[:cut], "row", 2)
    second_xy = swap(from_y[cut:], "row", 1)
    return [(0, 0, shard), (1, 0, from_x), (2, 0, from_y), (3, 0, first_xy), (3, cut, second_xy)]


def piece_copies(layout, refs, target, row_index, shard_rows, sems):
    copies = []
    for n, ((distance, first, rows), ref) in enumerate(zip(layout, refs)):
        base = pl.multiple_of((row_index ^ distance) * shard_rows + first, 16)
        copies.append(pltpu.make_async_copy(ref, target.at[pl.ds(base, rows), :], sems.at[n]))
    return copies


def layout_of(pieces):
    return [(distance, first, piece.shape[0]) for distance, first, piece in pieces]


hbm = pl.BlockSpec(memory_space=pl.ANY)


def project_in_body(layout, tiles, meta_ref, mine_ref, other_ref, bias_ref, *rest):
    pieces = rest[: len(layout)]
    out_ref, keys_ref, values_ref, weight_out, weight, sems, out_sem = rest[len(layout) :]
    step = pl.program_id(0)
    keep = pltpu.make_async_copy(weight, weight_out, out_sem)

    def project(rows):
        out = (dot_nn(rows, weight[...]) + bias_ref[...]).astype(low)
        out_ref[...] = out
        for pair in range(out.shape[1] // 384):
            here = slice(128 * pair, 128 * (pair + 1))
            keys_ref[here, :] = jnp.transpose(out[:, 384 * pair + 128 : 384 * pair + 256])
            values_ref[here, :] = jnp.transpose(out[:, 384 * pair + 256 : 384 * (pair + 1)])

    @pl.when(step == 0)
    def _():
        copies = piece_copies(layout, pieces, weight, meta_ref[1], weight.shape[0] // 4, sems)
        for copy in copies:
            copy.start()
        for copy in copies:
            copy.wait()
        keep.start()

    @pl.when(step < tiles)
    def _():
        project(mine_ref[...])

    @pl.when(step >= tiles)
    def _():
        project(other_ref[...])

    @pl.when(step == 2 * tiles - 1)
    def _():
        keep.wait()


def project_in(meta, mine, other, bias, pieces):
    rows, model = mine.shape
    size = 2 * tile_rows
    tiles = rows // size
    width = pieces[0][2].shape[1]
    return pl.pallas_call(
        functools.partial(project_in_body, layout_of(pieces), tiles),
        grid_spec=pltpu.PrefetchScalarGridSpec(
            num_scalar_prefetch=1,
            grid=(2 * tiles,),
            in_specs=[
                pl.BlockSpec((size, model), lambda i, m: (jnp.minimum(i, tiles - 1), 0)),
                pl.BlockSpec((size, model), lambda i, m: (jnp.maximum(i - tiles, 0), 0)),
                pl.BlockSpec((1, width), lambda i, m: (0, 0)),
            ]
            + [hbm] * len(pieces),
            out_specs=[
                pl.BlockSpec((None, size, width), lambda i, m: (i // tiles, i % tiles, 0)),
                pl.BlockSpec((None, width // 3, size), lambda i, m: (i // tiles, 0, i % tiles)),
                pl.BlockSpec((None, width // 3, size), lambda i, m: (i // tiles, 0, i % tiles)),
                hbm,
            ],
            scratch_shapes=[
                pltpu.VMEM((model, width), low),
                pltpu.SemaphoreType.DMA((len(pieces),)),
                pltpu.SemaphoreType.DMA(()),
            ],
        ),
        out_shape=[
            jax.ShapeDtypeStruct((2, rows, width), low),
            jax.ShapeDtypeStruct((2, width // 3, rows), low),
            jax.ShapeDtypeStruct((2, width // 3, rows), low),
            jax.ShapeDtypeStruct((model, width), low),
        ],
        cost_estimate=cost(7),
        name="project_in",
    )(meta, mine, other, bias, *[piece for _, _, piece in pieces])


def load_weights(layout, pieces, weight, meta_ref, sems):
    copies = []
    for side in range(2):
        copies += piece_copies(
            layout, pieces[side], weight.at[side], meta_ref[1], weight.shape[1] // 4, sems.at[side]
        )
    for copy in copies:
        copy.start()
    for copy in copies:
        copy.wait()


hidden_chunk = 768


def feed_body(
    layout, head_cols, hidden_cols, meta_ref, tok_ref, row_ref, mixed_ref, mixed_last_ref,
    got_ref, got_last_ref, cot_ref, vec_ref, up_bias_ref, *rest,
):
    count = len(layout)
    pieces = (rest[:count], rest[count : 2 * count])
    (
        out_ref, hidden_ref, grad_ref, two_ref, cot_turned_ref, branch_ref, middle_ref, own_ref,
        other_ref, sum_ref, bias_ref, weight, sems, mixer_ref, grad_two_ref,
    ) = rest[2 * count :]

    @pl.when(pl.program_id(0) == 0)
    def _():
        load_weights(layout, pieces, weight, meta_ref, sems)
        sum_ref[...] = jnp.zeros_like(sum_ref)
        bias_ref[...] = jnp.zeros_like(bias_ref)

    bias_out, gain, bias, bias_down = (vec_ref[n : n + 1, :] for n in range(4))
    cot = cot_ref[...]
    cot_turned_ref[...] = jnp.transpose(cot)
    start = tok_ref[...].astype(wide) + row_ref[...]
    cut = mixed_ref.shape[1]
    branch = dot_nt(mixed_ref[...], weight[0, :, :cut])
    branch = branch + dot_nt(mixed_last_ref[...], weight[0, :, cut:head_cols])
    branch = branch + dot_nt(got_ref[...], weight[1, :, :cut])
    branch = branch + dot_nt(got_last_ref[...], weight[1, :, cut:head_cols])
    middle = start + (branch + bias_out)
    unit, inverse = norm_parts(middle)
    two = (unit * gain + bias).astype(low)
    two_ref[...] = jnp.transpose(two)
    mixer_ref[...] = jnp.zeros_like(mixer_ref)
    grad_two_ref[...] = jnp.zeros_like(grad_two_ref)

    def visit(side, _):
        mixer = None
        grad_two = None
        for first in range(0, hidden_cols, hidden_chunk):
            here = slice(first, first + hidden_chunk)
            up = weight[side, :, head_cols + first : head_cols + first + hidden_chunk]
            at = head_cols + hidden_cols + first
            down = weight[side, :, at : at + hidden_chunk]
            hidden, slope = gelu_with_slope(dot_nn(two, up) + up_bias_ref[side, :, here])
            hidden = hidden.astype(low)
            hidden_ref[side, :, here] = hidden
            part = dot_nt(hidden, down)
            mixer = part if mixer is None else mixer + part
            grad_pre = (dot_nn(cot, down) * slope).astype(low)
            grad_ref[side, :, here] = grad_pre
            bias_ref[side, :, here] += jnp.sum(grad_pre.astype(wide), axis=0, keepdims=True)
            part = dot_nt(grad_pre, up)
            grad_two = part if grad_two is None else grad_two + part
        mixer_ref[...] += mixer
        grad_two_ref[...] += grad_two

    lax.fori_loop(0, 2, visit, None)
    mixer, grad_two = mixer_ref[...], grad_two_ref[...]
    out_ref[...] = (middle + (mixer + bias_down)).astype(low)
    cot = cot.astype(wide)
    grad_middle = cot + norm_back(grad_two, unit, inverse, gain)
    grad_branch = grad_middle.astype(low)
    middle_ref[...] = grad_middle
    branch_ref[...] = jnp.transpose(grad_branch)
    own_ref[...] = dot_nn(grad_branch, weight[0, :, :head_cols]).astype(low)
    other_ref[...] = dot_nn(grad_branch, weight[1, :, :head_cols]).astype(low)
    for n, values in enumerate((grad_branch.astype(wide), grad_two * unit, grad_two, cot)):
        sum_ref[n : n + 1, :] += jnp.sum(values, axis=0, keepdims=True)


def feed(meta, tokens, table_row, mixed, got, cot, vectors, up_bias, mine, other):
    rows, model = tokens.shape
    size = tile_rows
    head_cols = sum(part.shape[1] for part in mixed)
    hidden_cols = up_bias.shape[2]
    width = mine[0][2].shape[1]

    def tile(columns):
        return pl.BlockSpec((size, columns), lambda i, m: (i, 0))

    def fixed(*shape):
        return pl.BlockSpec(shape, lambda i, m: (0,) * len(shape))

    def turned(depth):
        return pl.BlockSpec((depth, size), lambda i, m: (0, i))

    def array(columns, dtype):
        return jax.ShapeDtypeStruct((rows, columns), dtype)

    flipped = jax.ShapeDtypeStruct((model, rows), low)
    return pl.pallas_call(
        functools.partial(feed_body, layout_of(mine), head_cols, hidden_cols),
        grid_spec=pltpu.PrefetchScalarGridSpec(
            num_scalar_prefetch=1,
            grid=(rows // size,),
            in_specs=[tile(model), fixed(1, model)]
            + [tile(part.shape[1]) for part in (*mixed, *got)]
            + [tile(model), fixed(8, model), fixed(2, 1, hidden_cols)]
            + [hbm] * (2 * len(mine)),
            out_specs=[tile(model)]
            + [pl.BlockSpec((2, size, hidden_cols), lambda i, m: (0, i, 0))] * 2
            + [turned(model)] * 3
            + [tile(model), tile(head_cols), tile(head_cols), fixed(8, model)]
            + [fixed(2, 1, hidden_cols)],
            scratch_shapes=[
                pltpu.VMEM((2, model, width), low),
                pltpu.SemaphoreType.DMA((2, len(mine))),
                pltpu.VMEM((size, model), wide),
                pltpu.VMEM((size, model), wide),
            ],
        ),
        out_shape=[array(model, low)]
        + [jax.ShapeDtypeStruct((2, rows, hidden_cols), low)] * 2
        + [flipped] * 3
        + [array(model, wide), array(head_cols, low), array(head_cols, low)]
        + [jax.ShapeDtypeStruct((8, model), wide)]
        + [jax.ShapeDtypeStruct((2, 1, hidden_cols), wide)],
        cost_estimate=cost(45),
        name="feed",
    )(
        meta, tokens, table_row, *mixed, *got, cot, vectors, up_bias,
        *[piece for _, _, piece in mine], *[piece for _, _, piece in other],
    )


def weight_parts_body(products, near, meta_ref, *refs):
    send_ref, keep_ref = refs[-2:]
    shard = send_ref.shape[0] // 2
    order = [pl.multiple_of((meta_ref[1] ^ d) * shard, 64) for d in (3, near, 3 - near, 0)]

    def in_order(ref):
        return jnp.concatenate([ref[pl.ds(start, shard), :] for start in order], axis=0)

    for pairs, arrived, first, tiles in products:

        @pl.when((pl.program_id(0) >= first) & (pl.program_id(0) < first + tiles))
        def _(pairs=pairs, arrived=arrived):
            total = None
            for left, right in pairs:
                part = dot_nn(in_order(refs[left]), refs[right][...])
                total = part if total is None else total + part
            if arrived is not None:
                total = total + in_order(refs[arrived]).astype(wide)
            total = total.astype(low)
            send_ref[...] = total[: 2 * shard]
            keep_ref[...] = total[2 * shard :]


def weight_parts(meta, products, near, micros):
    model = products[0][0][0][0].shape[0]
    operands, specs, shapes = [], [], []
    step = 384 if any(pairs[0][1].shape[-1] % 512 for pairs, _ in products) else 512
    first = 0

    def place_of(operand, spec, shared=False):
        for n, known in enumerate(operands):
            if shared and known is operand:
                return n
        operands.append(operand)
        specs.append(spec)
        return len(operands) - 1

    for pairs, arrived in products:
        tiles = pairs[0][1].shape[-1] // step

        def tile(i, m, first=first, tiles=tiles):
            return (0, jnp.clip(i - first, 0, tiles - 1))

        places = []
        for left, right in pairs:
            depth = right.shape[-2]
            right_spec = pl.BlockSpec((depth, step), tile)
            if right.ndim == 3:
                right_spec = pl.BlockSpec(
                    (None, depth, step), lambda i, m, t=tile: (0, *t(i, m))
                )
            left_place = place_of(left, pl.BlockSpec(left.shape, lambda i, m: (0, 0)), True)
            places.append((left_place, place_of(right, right_spec)))
        at = None
        if arrived is not None:
            at = place_of(arrived, pl.BlockSpec((model, step), tile))
        shapes.append((places, at, first, tiles))
        first += tiles
    half = jax.ShapeDtypeStruct((model // 2, first * step), low)
    return pl.pallas_call(
        functools.partial(weight_parts_body, shapes, near),
        grid_spec=pltpu.PrefetchScalarGridSpec(
            num_scalar_prefetch=1,
            grid=(first,),
            in_specs=specs,
            out_specs=[pl.BlockSpec((model // 2, step), lambda i, m: (0, i))] * 2,
        ),
        out_shape=[half, half],
        cost_estimate=cost(micros),
        name="weight_parts",
    )(meta, *operands)


def product_body(left_ref, right_ref, out_ref):
    out_ref[...] = dot_nn(left_ref[...], right_ref[...]).astype(low)


def product(left, right, micros):
    rows, depth = left.shape
    columns = right.shape[-1]
    step = 512 if columns % 512 == 0 else 384
    right_spec = pl.BlockSpec((depth, step), lambda i: (0, i))
    if right.ndim == 3:
        right_spec = pl.BlockSpec((None, depth, step), lambda i: (1, 0, i))
    return pl.pallas_call(
        product_body,
        grid=(columns // step,),
        in_specs=[pl.BlockSpec((rows, depth), lambda i: (0, 0)), right_spec],
        out_specs=pl.BlockSpec((rows, step), lambda i: (0, i)),
        out_shape=jax.ShapeDtypeStruct((rows, columns), low),
        cost_estimate=cost(micros),
        name="product",
    )(left, right)


def table_body(step_ref, sum_ref, out_ref):
    out_ref[...] = jnp.zeros_like(out_ref)

    def add(n, _):
        out_ref[pl.ds(step_ref[n], 1), :] += sum_ref[pl.ds(n, 1), :]

    lax.fori_loop(0, sum_ref.shape[0], add, None)


def table_rows(steps, sums, rows):
    return pl.pallas_call(
        table_body,
        grid_spec=pltpu.PrefetchScalarGridSpec(
            num_scalar_prefetch=1,
            grid=(1,),
            in_specs=[pl.BlockSpec(sums.shape, lambda i, t: (0, 0))],
            out_specs=pl.BlockSpec((rows, sums.shape[1]), lambda i, t: (0, 0)),
        ),
        out_shape=jax.ShapeDtypeStruct((rows, sums.shape[1]), wide),
        cost_estimate=cost(2),
        name="table_rows",
    )(steps, sums)


def pack_body(*refs):
    out_ref = refs[-1]
    for n in range(out_ref.shape[1] // 128):
        kind, pair = n % 3, n // 3
        out_ref[:, 128 * n : 128 * (n + 1)] = refs[kind][:, 128 * pair : 128 * (pair + 1)].astype(low)


def pack(*weights):
    rows, columns = weights[0].shape
    return pl.pallas_call(
        pack_body,
        out_shape=jax.ShapeDtypeStruct((rows, 3 * columns), low),
        cost_estimate=cost(1),
        name="pack",
    )(*weights)


def grad_in_body(cuts, tok_ref, row_ref, gain_ref, own_ref, other_ref, middle_ref, *rest):
    grads = rest[: 2 * len(cuts)]
    out_ref, sum_ref = rest[2 * len(cuts) :]

    @pl.when(pl.program_id(0) == 0)
    def _():
        sum_ref[...] = jnp.zeros_like(sum_ref)

    grad = None
    for n, (first, last) in enumerate(cuts):
        for values, weight in ((grads[2 * n], own_ref), (grads[2 * n + 1], other_ref)):
            part = dot_nt(values[...], weight[:, first:last])
            grad = part if grad is None else grad + part
    unit, inverse = norm_parts(tok_ref[...].astype(wide) + row_ref[...])
    tokens = middle_ref[...] + norm_back(grad, unit, inverse, gain_ref[...])
    out_ref[...] = tokens
    for n, values in enumerate((grad * unit, grad, tokens)):
        sum_ref[n : n + 1, :] += jnp.sum(values, axis=0, keepdims=True)


def grad_in(tokens, table_row, gain, own, other, grad_middle, grads):
    rows, model = tokens.shape
    size = tile_rows
    width = own.shape[1]
    cuts = []
    for mine, _ in grads:
        first = cuts[-1][1] if cuts else 0
        cuts.append((first, first + mine.shape[1]))

    def tile(columns):
        return pl.BlockSpec((size, columns), lambda i: (i, 0))

    def fixed(*shape):
        return pl.BlockSpec(shape, lambda i: (0, 0))

    flat = [values for pair in grads for values in pair]
    return pl.pallas_call(
        functools.partial(grad_in_body, cuts),
        grid=(rows // size,),
        in_specs=[
            tile(model), fixed(1, model), fixed(1, model), fixed(model, width),
            fixed(model, width), tile(model),
        ]
        + [tile(values.shape[1]) for values in flat],
        out_specs=[tile(model), fixed(8, model)],
        out_shape=[
            jax.ShapeDtypeStruct((rows, model), wide),
            jax.ShapeDtypeStruct((8, model), wide),
        ],
        cost_estimate=cost(9),
        name="grad_in",
    )(tokens, table_row, gain, own, other, grad_middle, *flat)


def after(values, *needed):
    needed = jax.tree.leaves(needed)
    return lax.optimization_barrier((values, *needed))[0] if needed else values


def line_steps(values):
    if lax.axis_size("dp") != 4:
        return lax.psum(values, "dp")
    for distance in (1, 2):
        arrived = swap(values, "dp", distance)
        token = yield values
        arrived = after(arrived, token)
        values = (values.astype(wide) + arrived.astype(wide)).astype(values.dtype)
    return values


def split_line_steps(values):
    if lax.axis_size("dp") != 4:
        return lax.psum(values, "dp")
    me = lax.axis_index("dp")
    first, second = me % 2, me // 2
    half = values.shape[0] // 2

    def take(array, place, count):
        return lax.dynamic_slice_in_dim(array, place * count, count, 0)

    def join(place, mine, other):
        swapped = jnp.concatenate([other, mine], axis=0)
        return jnp.where(place == 0, jnp.concatenate([mine, other], axis=0), swapped)

    for place, distance in ((first, 1), (second, 2)):
        sent = take(values, 1 - place, half)
        arrived = swap(sent, "dp", distance)
        token = yield sent
        arrived = after(arrived, token)
        values = (take(values, place, half).astype(wide) + arrived.astype(wide)).astype(low)
        half //= 2
    for place, distance in ((second, 2), (first, 1)):
        arrived = swap(values, "dp", distance)
        token = yield values
        values = join(place, values, after(arrived, token))
    return values


def weight_steps(parts, near, line=line_steps):
    send, keep = parts
    shard = send.shape[0] // 2
    arrived = swap(send, "row", near)
    token = yield send
    arrived = after(arrived, token)
    passed = (keep[:shard].astype(wide) + arrived[:shard].astype(wide)).astype(low)
    last = swap(passed, "row", 3 - near)
    token = yield passed
    last = after(last, token)
    share = keep[shard:].astype(wide) + arrived[shard:].astype(wide) + last.astype(wide)
    total = yield from line(share.astype(low))
    return total.astype(wide)


def vector_steps(values):
    for axis, distance in (("row", 1), ("row", 2)):
        arrived = swap(values, axis, distance)
        token = yield values
        values = values + after(arrived, token)
    total = yield from line_steps(values)
    return total


class Chains:
    def __init__(self):
        self.steps, self.done = [], {}

    def add(self, steps):
        self.steps.append(steps)
        return [next(steps)]

    def advance(self, token=None, chosen=None):
        sent = []
        for n, steps in enumerate(self.steps):
            if n not in self.done and (chosen is None or n in chosen):
                try:
                    sent.append(steps.send(token))
                except StopIteration as stop:
                    self.done[n] = stop.value
        return sent


def shards(
    tokens, timesteps, block_ids, table, gain_one, bias_one, w_query, w_key, w_value, b_query,
    b_value, w_out, b_out, gain_two, bias_two, w_up, b_up, w_down, b_down, cotangent,
):
    seq_count, local_len, model_width = tokens.shape
    row_size, dp_size = lax.axis_size("row"), lax.axis_size("dp")
    assert seq_count == 1 and lax.axis_size("col") == 2 and row_size == 4
    head_cols = w_query.shape[1]
    hidden_cols = w_up.shape[1]
    col_index = lax.axis_index("col")
    row_index = lax.axis_index("row")
    seq_index = lax.axis_index("dp") * row_size + row_index
    seq_total = dp_size * row_size
    meta = jnp.stack([col_index, row_index]).astype(jnp.int32)

    cuts = [slice(first, first + 128) for first in range(0, head_cols, 128)]
    group_one = pack(w_query, w_key, w_value)
    in_bias = jnp.concatenate(
        [part for cut in cuts for part in (b_query[cut], jnp.zeros_like(b_query[cut]), b_value[cut])]
    )[None]
    in_pieces = gather_far(group_one, *gather_near(group_one))
    group_two = jnp.concatenate([w_out.T, w_up, w_down.T], axis=1).astype(low)
    group_two = after(group_two, in_pieces[3][2], in_pieces[4][2])
    near_x, near_y = gather_near(group_two)

    table_row = lax.dynamic_slice_in_dim(table, timesteps[0], 1, 0)
    unit_one, _ = norm_parts(tokens[0].astype(wide) + table_row)
    rows_mine = (unit_one * gain_one + bias_one).astype(low)
    rows_other = swap(rows_mine, "col", 1)
    up_bias = jnp.stack([b_up, swap(b_up, "col", 1)])[:, None]
    mine_turned, other_turned = rows_mine.T, rows_other.T
    qkv, keys_turned, values_turned, in_own = project_in(
        meta, rows_mine, after(rows_other, up_bias, mine_turned, other_turned), in_bias, in_pieces
    )
    in_other = swap(in_own, "col", 1)
    shard_other = swap(group_two, "col", 1)
    pairs = head_cols // 128
    mixed, mixed_other, log_sums = attend_forward(
        meta, qkv, values_turned, block_ids, 0, pairs - 1
    )
    got = swap(mixed_other, "col", 1)
    near_x, near_y = after(near_x, mixed), after(near_y, mixed)
    near_x_other, near_y_other = swap(near_x, "col", 1), swap(near_y, "col", 1)
    mine = gather_far(group_two, near_x, near_y)
    mixed_last, mixed_last_other, log_sums_last = attend_forward(
        meta, after(qkv, in_other, shard_other, got, near_x_other, near_y_other), values_turned,
        block_ids, pairs - 1, 1,
    )
    got_last = swap(mixed_last_other, "col", 1)
    far = [after(piece, mixed_last) for _, _, piece in mine[3:]]
    others = [shard_other, near_x_other, near_y_other] + [swap(piece, "col", 1) for piece in far]
    other = [(distance, first, piece) for (distance, first, _), piece in zip(mine, others)]

    spare = jnp.zeros_like(b_out)
    vectors = jnp.stack([b_out, gain_two, bias_two, b_down, spare, spare, spare, spare])
    cot = cotangent[0]
    (
        layer_out, hidden, grad_hidden, two_turned, cot_turned, branch_turned,
        grad_middle, grad_own, grad_other, sums, grad_up_bias,
    ) = feed(
        meta, tokens[0], table_row, (mixed, mixed_last), (got, got_last), cot, vectors, up_bias,
        mine, other,
    )
    up_arrived = swap(product(two_turned, grad_hidden, 4), "col", 1)
    down_arrived = swap(product(cot_turned, hidden, 4), "col", 1)
    grad_got = swap(grad_other, "col", 1)
    up_parts = weight_parts(meta, [([(two_turned, grad_hidden)], up_arrived)], 1, 6)
    chains = Chains()
    chains.add(weight_steps(up_parts, 1, split_line_steps))
    down_parts = weight_parts(
        meta, [([(cot_turned, hidden)], after(down_arrived, *up_parts))], 2, 6
    )
    chains.add(weight_steps(down_parts, 2, split_line_steps))
    grad_b_up = grad_up_bias[0, 0] + swap(grad_up_bias[1, 0], "col", 1)
    before = [*up_parts, *down_parts, grad_b_up]

    own_grads, aways, gots, bias_sums = [], [], [], []
    for pair in range(pairs):
        last = pair == pairs - 1
        own, away, bias_sum = attend_backward(
            meta, after(qkv, *before), keys_turned, grad_own, grad_got, block_ids,
            log_sums_last if last else log_sums, pair, 1, 0 if last else pair,
        )
        own_grads.append(own)
        gots.append(swap(away, "col", 1))
        bias_sums.append(bias_sum)
        before = [*chains.advance(own), gots[-1]]
        aways.append(away)
        if pair == 0:
            out_sent = product(
                branch_turned, after(jnp.concatenate([got, got_last], axis=1), *before), 2
            )
            out_arrived = swap(out_sent, "col", 1)
            before.append(out_sent)
            continue
        if pair == pairs - 2:
            out_keep = jnp.concatenate([mixed, mixed_last], axis=1)
            products = [([(branch_turned, out_keep)], out_arrived)]
            ours, theirs = own_grads, aways
        else:
            products, ours, theirs = [], [own], [away]
        near = 1 if last else 2
        products += [([(mine_turned, a), (other_turned, b)], None) for a, b in zip(ours, theirs)]
        parts = weight_parts(meta, products, near, 3 * len(products))
        before += parts
        chains.add(weight_steps(parts, near, line_steps if last else split_line_steps))
    grad_tokens, late_sums = grad_in(
        after(tokens[0], *before), table_row, gain_one[None], in_own, in_other, grad_middle,
        list(zip(own_grads, gots)),
    )
    chains.advance(grad_tokens)

    shared = jnp.concatenate([late_sums[:3], sums[:4]])
    shared = shared + swap(shared, "col", 1)
    slot = lax.broadcasted_iota(jnp.int32, (seq_total, 1), 0) == seq_index
    packed = jnp.concatenate(
        [
            jnp.concatenate([shared[:2], shared[3:]]).reshape(-1),
            jnp.concatenate([part[:1] for part in bias_sums], axis=1).reshape(-1),
            jnp.concatenate([part[1:2] for part in bias_sums], axis=1).reshape(-1),
            grad_b_up,
            jnp.where(slot, shared[2:3], 0.0).reshape(-1),
            jnp.where(slot, timesteps[0].astype(wide), 0.0).reshape(-1),
        ]
    )
    pad = -packed.shape[0] % 1024
    chains.add(vector_steps(jnp.pad(packed, (0, pad)).reshape(-1, 128)))
    sent = None
    for chain in (4, 2, 3, 4, 0, 1, 4, 3, 2, 4, 3, 2, 0, 1, 2):
        sent = chains.advance(sent, (chain,)) or sent
        if 4 in chains.done:
            sent = chains.done[4]
    while len(chains.done) < len(chains.steps):
        chains.advance(sent)
    done = chains.done
    own_up, own_down = done[0], done[1]
    own_out, done[2] = done[2][:, :head_cols], done[2][:, head_cols:]
    own_in = jnp.concatenate([done[2], done[3]], axis=1)
    own_in = [
        jnp.concatenate([own_in[:, 128 * n : 128 * (n + 1)] for n in range(kind, 3 * pairs, 3)], axis=1)
        for kind in range(3)
    ]
    packed = done[4].reshape(-1)
    place = 0
    taken = []
    for size in (6 * model_width, 2 * head_cols, hidden_cols, seq_total * model_width, seq_total):
        taken.append(packed[place : place + size])
        place += size
    six = taken[0].reshape(6, model_width)
    grad_table = table_rows(
        taken[4].astype(jnp.int32), taken[3].reshape(seq_total, model_width), table.shape[0]
    )
    return (
        layer_out[None],
        grad_tokens[None],
        grad_table,
        six[0],
        six[1],
        own_in[0],
        own_in[1],
        own_in[2],
        taken[1][:head_cols],
        taken[1][head_cols:],
        own_out.T,
        six[2],
        six[3],
        six[4],
        own_up,
        taken[2],
        own_down.T,
        six[5],
    )


def solution(mesh):
    return jax.shard_map(
        shards,
        mesh=mesh,
        in_specs=(
            P(("dp", "row"), "col", None),
            P(("dp", "row")),
            P(("dp", "row"), None),
            P(),
            P(),
            P(),
            P("row", "col"),
            P("row", "col"),
            P("row", "col"),
            P("col"),
            P("col"),
            P("col", "row"),
            P(),
            P(),
            P(),
            P("row", "col"),
            P("col"),
            P("col", "row"),
            P(),
            P(("dp", "row"), "col", None),
        ),
        out_specs=(
            P(("dp", "row"), "col", None),
            P(("dp", "row"), "col", None),
            P(),
            P(),
            P(),
            P("row", "col"),
            P("row", "col"),
            P("row", "col"),
            P("col"),
            P("col"),
            P("col", "row"),
            P(),
            P(),
            P(),
            P("row", "col"),
            P("col"),
            P("col", "row"),
            P(),
        ),
        check_vma=False,
    )
```
